256 devices in a mesh: seq: 32 (over y, x, core), head: 8 (over z).
Axes of the slice: x: 4, y: 4, z: 8, core: 2. Of those that a mesh axis runs over, the one named last changes fastest.
Arguments:
- frames: bfloat16 [8192, 4096], P('seq'), may hold values from -6 to 6
- norm_gain: float32 [4096], replicated, may hold values from 0.5 to 1.5
- qkv_weight: bfloat16 [4096, 3, 2048], P(None, None, 'head'), may hold values from -0.09375 to 0.09375
- gate_weight: bfloat16 [4096, 2, 8], P(None, None, 'head'), may hold values from -0.09375 to 0.09375
- beta_scale: float32 [8], P('head'), may hold values from 0.2 to 1
- decay_rate: float32 [8], P('head'), may hold values from 1e-06 to 0.05
- resets: int32 [8192], P('seq'), may hold values 0 or 1
- out_gain: float32 [2048], P('head'), may hold values from 0.5 to 1.5
- out_weight: bfloat16 [2048, 4096], P('head'), may hold values from -0.125 to 0.125
Outputs:
- mixed: bfloat16 [8192, 4096], P(('seq', 'head'))
The draws below stay inside these ranges and needn't reach their ends.
Inputs may be any that keep to these rules, and one draw needn't show every extreme that they name: `resets`: reset flags are 0 or 1.
All inputs are finite; a program needn't handle non-finite values. No bound on the sum of `resets` on one device may be relied on, other than what follows from the above.
Results may differ from the reference program's by a relative error of at most 0.017.
Values may be sent and summed in bfloat16 or wider, within the bound.
No kernel may reach another device: no remote copies, remote signals or barrier semaphores. Data moves between devices by JAX's collectives and lax.ppermute only.
A program may use at most 64 MiB of HBM per device.

```python
import math
import jax
import jax.numpy as jnp
from jax import lax

D = 4096
HEADS = 8
DH = 256
FRAMES = 8192
HD = 2048
N_HEAD = 8


def slow_heads(key):
    order = jax.random.permutation(jax.random.fold_in(key, 11), HEADS)
    count = HEADS - HEADS // 4
    return order < count


def log_between(key, lower, upper):
    spread = jax.random.uniform(key, (HEADS,), jnp.float32)
    return jnp.exp(math.log(lower) + spread * (math.log(upper) - math.log(lower)))


def draw_beta_scale(key, part):
    return log_between(jax.random.fold_in(key, 22), 0.2, 1.0).astype(jnp.float32)


def draw_decay_rate(key, part):
    selected_rows = slow_heads(key)
    weak = log_between(jax.random.fold_in(key, 31), 1e-06, 1e-05)
    strong = log_between(jax.random.fold_in(key, 32), 0.01, 0.05)
    return jnp.where(selected_rows, weak, strong).astype(jnp.float32)


def with_ends(array, own_key, least, high):
    dims = array.shape
    place = [jax.random.randint(jax.random.fold_in(own_key, axis), (), 0, dims[axis]) for axis in range(len(dims))]
    array = array.at[tuple(place)].set(least)
    longest = dims.index(max(dims))
    place[longest] = (place[longest] + 1) % dims[longest]
    return array.at[tuple(place)].set(high)


def shard_levels(rng, shape, shards, smallest, high):
    level, own = 1.0, jax.random.fold_in(rng, 6)
    for position, shards_of in shards:
        draws = jnp.exp(jax.random.uniform(jax.random.fold_in(own, position), (shards_of,), jnp.float32, smallest / len(shards), high / len(shards)))
        level = level * jnp.repeat(draws, shape[position] // shards_of).reshape([-1 if axis == position else 1 for axis in range(len(shape))])
    return level


def gaussian(key, extent, scale, limit, shards=(), dtype=jnp.bfloat16):
    values = jax.random.normal(key, extent, jnp.float32) * scale
    if len(shards) > 0:
        values = shard_levels(key, extent, shards, -0.22, 0.18) * values
    return jnp.clip(values, min=-limit, max=limit).astype(dtype)


def setup_inputs(seed: int = 0) -> dict:
    key_of = jax.random.split(jax.random.key(seed), 10)
    frames = gaussian(key_of[0], (FRAMES, D), 1.0, 6.0, ((0, 32),))
    norm_gain = jnp.clip(1.0 + 0.1 * jax.random.normal(key_of[1], (D,), jnp.float32), 0.5, 1.5)
    qkv_weight = gaussian(key_of[2], (D, 3, HD), D ** -0.5, 0.09375, ((2, 8),))
    gate_weight = gaussian(key_of[3], (D, 2, HEADS), D ** -0.5, 0.09375, ((2, 8),))
    beta_scale = draw_beta_scale(jax.random.fold_in(key_of[9], 71), 0)
    decay_rate = draw_decay_rate(jax.random.fold_in(key_of[9], 71), 0)
    resets = with_ends((jax.random.randint(key_of[6], (FRAMES,), 0, FRAMES) < 4).astype(jnp.int32), jax.random.fold_in(key_of[6], 1), 0, 1)
    out_gain = jnp.clip(1.0 + 0.1 * jax.random.normal(key_of[7], (HD,), jnp.float32), 0.5, 1.5)
    out_weight = gaussian(key_of[8], (HD, D), HD ** -0.5, 0.125, ((0, 8),))
    return dict(frames=frames, norm_gain=norm_gain, qkv_weight=qkv_weight, gate_weight=gate_weight, beta_scale=beta_scale, decay_rate=decay_rate, resets=resets, out_gain=out_gain, out_weight=out_weight)


HIGH_ACCURACY = lax.Precision.HIGHEST

def unit_rows(vectors):
    return vectors * lax.rsqrt(lax.optimization_barrier(jnp.sum(vectors * vectors, axis=-1, keepdims=True)) + 1e-06)

def reference(frames, norm_gain, qkv_weight, gate_weight, beta_scale, decay_rate, resets, out_gain, out_weight):
    expanded_input = frames.astype(jnp.float32)
    normed = (expanded_input * lax.rsqrt(lax.optimization_barrier(jnp.mean(expanded_input * expanded_input, axis=-1, keepdims=True)) + 1e-06) * norm_gain).astype(jnp.bfloat16)
    projected = jnp.dot(normed, qkv_weight.reshape(D, 3 * HEADS * DH), preferred_element_type=jnp.float32).reshape(FRAMES, 3, HEADS, DH)
    query_vec = unit_rows(projected[:, 0])
    key_vec = unit_rows(projected[:, 1])
    value_vec = projected[:, 2]
    gating = jnp.dot(normed, gate_weight.reshape(D, 2 * HEADS), preferred_element_type=jnp.float32).reshape(FRAMES, 2, HEADS)
    strength = beta_scale * jax.nn.sigmoid(gating[:, 0])
    forget = jnp.exp(-decay_rate * jax.nn.softplus(gating[:, 1])) * (1.0 - resets.astype(jnp.float32))[:, None]

    def advance(memory_state, inputs):
        query_at_step, key_at_step, value_t, strength_t, forget_t = inputs
        retrieved_value = jnp.einsum('mj,mjo->mo', key_at_step, memory_state, precision=HIGH_ACCURACY)
        erased = memory_state - strength_t[:, None, None] * key_at_step[:, :, None] * retrieved_value[:, None, :]
        memory_state = forget_t[:, None, None] * erased + strength_t[:, None, None] * key_at_step[:, :, None] * value_t[:, None, :]
        return (memory_state, jnp.einsum('zqu,zq->zu', memory_state, query_at_step, precision=HIGH_ACCURACY))
    initial = jnp.zeros((HEADS, DH, DH), jnp.float32)
    _, read_out = lax.scan(advance, initial, (query_vec, key_vec, value_vec, strength, forget))
    normalized = read_out * lax.rsqrt(lax.optimization_barrier(jnp.mean(read_out * read_out, axis=-1, keepdims=True)) + 1e-06) * out_gain.reshape(HEADS, DH)
    flat = normalized.reshape(FRAMES, HEADS * DH).astype(jnp.bfloat16)
    group_width = HEADS * DH // N_HEAD
    total = jnp.zeros((FRAMES, D), jnp.float32)
    for group in range(N_HEAD):
        lower_edge = group * group_width
        partial_sum = jnp.dot(flat[:, lower_edge:lower_edge + group_width], out_weight[lower_edge:lower_edge + group_width], preferred_element_type=jnp.float32).astype(jnp.bfloat16)
        total = total + partial_sum.astype(jnp.float32)
    return total.astype(jnp.bfloat16)
```

```python
import functools

import jax
import jax.numpy as jnp
from jax import lax
from jax.experimental import pallas as pl
from jax.experimental.pallas import tpu as pltpu
from jax.sharding import PartitionSpec as P

KB = 1024
F32 = jnp.float32
BF16 = jnp.bfloat16
NN = (((1,), (0,)), ((), ()))
NT = (((1,), (1,)), ((), ()))
TN = (((0,), (0,)), ((), ()))


def mm(a, b, dims=NN):
    return lax.dot_general(a, b, dims, preferred_element_type=F32)


def split(a):
    hi = a.astype(BF16)
    return hi, (a - hi.astype(F32)).astype(BF16)


def mm3(a, b, dims=NN):
    (ah, al), (bh, bl) = a, b
    return mm(ah, bh, dims) + (mm(ah, bl, dims) + mm(al, bh, dims))


def unit_rows(vectors):
    return vectors * lax.rsqrt(jnp.sum(vectors * vectors, axis=-1, keepdims=True) + 1e-06)


def chunk_kernel(
    scale_ref, x_ref, gain_ref, w_ref, gate_ref, resets_ref,
    carry_ref, local_ref, query_ref,
    xn_ref, acc_ref, gating_ref,
):
    step = pl.program_id(0)
    n = x_ref.shape[0]

    @pl.when(step == 0)
    def _():
        x = x_ref[...].astype(F32)
        rs = lax.rsqrt(jnp.mean(x * x, axis=-1, keepdims=True) + 1e-06)
        xn_ref[...] = (x * rs * gain_ref[...]).astype(BF16)

    xb = xn_ref[:, pl.ds(pl.multiple_of(step * KB, KB), KB)]
    parts = [mm(xb, w_ref[j]) for j in range(3)]
    gating = mm(gate_ref[...], xb, NT)

    @pl.when(step == 0)
    def _():
        for j in range(3):
            acc_ref[j] = parts[j]
        gating_ref[...] = gating

    @pl.when(step > 0)
    def _():
        for j in range(3):
            acc_ref[j] = acc_ref[j] + parts[j]
        gating_ref[...] = gating_ref[...] + gating

    @pl.when(step == pl.num_programs(0) - 1)
    def _():
        query = unit_rows(acc_ref[0])
        key = unit_rows(acc_ref[1])
        value = acc_ref[2]
        gating = gating_ref[...]
        beta_row = scale_ref[0] * jax.nn.sigmoid(gating[0:1])
        logf_row = -scale_ref[1] * jax.nn.softplus(gating[1:2])
        reset_row = resets_ref[...].astype(F32)
        t = lax.broadcasted_iota(jnp.int32, (n, n), 0)
        s = lax.broadcasted_iota(jnp.int32, (n, n), 1)
        causal = t >= s
        eye = t == s

        def to_col(row):
            return jnp.sum(jnp.where(eye, row, 0.0), axis=1, keepdims=True)

        def to_row(col):
            return jnp.sum(jnp.where(eye, col, 0.0), axis=0, keepdims=True)

        beta = to_col(beta_row)
        cum = jnp.sum(jnp.where(causal, logf_row, 0.0), axis=1, keepdims=True)
        seg = jnp.sum(jnp.where(causal, reset_row, 0.0), axis=1, keepdims=True)
        cum_row = to_row(cum)
        seg_row = to_row(seg)
        same = (seg == seg_row) & causal
        decay = jnp.where(same, jnp.exp(jnp.where(same, cum - cum_row, 0.0)), 0.0)
        gamma = jnp.where(seg == 0.0, jnp.exp(cum), 0.0)
        cum_last, seg_last = cum[n - 1 : n], seg[n - 1 : n]
        tail = jnp.where(seg == seg_last, jnp.exp(cum_last - cum), 0.0)
        gamma_last = gamma[n - 1 : n]

        ks = split(key)
        gram = mm3(ks, ks, NT)
        low = jnp.where(t > s, beta * decay * gram, 0.0)
        apart = t ^ s
        inv = jnp.where(eye, 1.0, jnp.where(apart == 1, -low, 0.0))
        for level in range(1, n.bit_length() - 1):
            part = jnp.where((apart >> level) == 1, low, 0.0)
            vs = split(inv)
            inv = inv - mm3(vs, split(mm3(split(part), vs)))
        rhs = jnp.concatenate([(beta * gamma) * key, beta * value], axis=1)
        solved = split(mm3(split(inv), split(rhs)))
        folded = mm3(split(key * tail), solved, TN)
        carry_ref[:, :n] = (jnp.where(eye, gamma_last, 0.0) - folded[:, :n]).astype(BF16)
        carry_ref[:, n:] = folded[:, n:].astype(BF16)
        scores = mm3(split(query), ks, NT) * decay
        seen = mm3(split(scores), solved)
        query_ref[...] = gamma * query - seen[:, :n]
        local_ref[...] = seen[:, n:]


def after(later, earlier, n):
    both = mm(later[:, :n], earlier)
    return both[:, :n], both[:, n:] + later[:, n:].astype(F32)


def pair_kernel(own_ref, other_ref, out_ref):
    n = own_ref.shape[0]
    first = lax.axis_index("seq") % 2 == 0
    own, other = own_ref[...], other_ref[...]
    earlier = jnp.where(first, own, other)
    later = jnp.where(first, other, own)
    a, b = after(later, earlier, n)
    out_ref[:, :n] = a.astype(BF16)
    out_ref[:, n:] = b.astype(BF16)


def row_kernel(own_ref, one_ref, two_ref, three_ref, total_ref, prefix_ref, held):
    n = own_ref.shape[0]
    place = (lax.axis_index("seq") // 2) % 4
    for shift, ref in enumerate((own_ref, one_ref, two_ref, three_ref)):
        held[(place + (4 - shift)) % 4] = ref[...]

    def joined(later, earlier):
        a, b = after(later, earlier, n)
        return jnp.concatenate([a, b], axis=1).astype(BF16)

    low = joined(held[1], held[0])
    high = joined(held[3], held[2])
    a, b = after(high, low, n)
    total_ref[:, :n] = a.astype(BF16)
    total_ref[:, n:] = b.astype(BF16)

    @pl.when(place == 0)
    def _():
        prefix_ref[...] = jnp.zeros_like(prefix_ref)

    @pl.when(place == 1)
    def _():
        prefix_ref[...] = held[0]

    @pl.when(place == 2)
    def _():
        prefix_ref[...] = low

    @pl.when(place == 3)
    def _():
        prefix_ref[...] = joined(held[2], low)


def read_kernel(
    one_ref, two_ref, three_ref, prefix_ref, other_ref, query_ref, local_ref, gain_ref,
    out_ref, held, state,
):
    n = query_ref.shape[0]
    index = lax.axis_index("seq")
    place = index // 8
    for shift, ref in enumerate((one_ref, two_ref, three_ref)):
        held[(place + (3 - shift)) % 4] = ref[...]

    def push(pair, value):
        hi, lo = split(value)
        return mm(pair[:, :n], hi) + mm(pair[:, :n], lo) + pair[:, n:].astype(F32)

    @pl.when(place == 0)
    def _():
        state[...] = jnp.zeros_like(state)

    @pl.when(place > 0)
    def _():
        state[...] = held[0, :, n:].astype(F32)

    for turn in (1, 2):
        @pl.when(place > turn)
        def _():
            state[...] = push(held[turn], state[...])

    @pl.when((index // 2) % 4 > 0)
    def _():
        state[...] = push(prefix_ref[...], state[...])

    @pl.when(index % 2 > 0)
    def _():
        state[...] = push(other_ref[...], state[...])

    read = local_ref[...] + mm3(split(query_ref[...]), split(state[...]))
    read = read * lax.rsqrt(jnp.mean(read * read, axis=-1, keepdims=True) + 1e-06)
    out_ref[...] = (read * gain_ref[...]).astype(BF16)


def vmem():
    return pl.BlockSpec(memory_space=pltpu.VMEM)


def per_device(
    frames, norm_gain, qkv_weight, gate_weight, beta_scale, decay_rate, resets, out_gain, out_weight
):
    rows, width = frames.shape
    n = qkv_weight.shape[2]
    weight = qkv_weight.transpose(1, 0, 2)
    gate = gate_weight.transpose(2, 1, 0).reshape(2, width)
    scales = jnp.concatenate([beta_scale, decay_rate])
    whole = lambda shape: pl.BlockSpec(shape, lambda i: (0,) * len(shape), pipeline_mode=pl.Buffered(1))
    carry, local, query = pl.pallas_call(
        chunk_kernel,
        name="chunk",
        grid=(width // KB,),
        in_specs=[
            pl.BlockSpec(memory_space=pltpu.SMEM),
            whole((rows, width)),
            whole((1, width)),
            pl.BlockSpec((3, KB, n), lambda i: (0, i, 0)),
            pl.BlockSpec((2, KB), lambda i: (0, i)),
            whole((1, rows)),
        ],
        out_specs=[whole((n, 2 * n)), whole((rows, n)), whole((rows, n))],
        out_shape=[
            jax.ShapeDtypeStruct((n, 2 * n), BF16),
            jax.ShapeDtypeStruct((rows, n), F32),
            jax.ShapeDtypeStruct((rows, n), F32),
        ],
        scratch_shapes=[
            pltpu.VMEM((rows, width), BF16),
            pltpu.VMEM((3, rows, n), F32),
            pltpu.VMEM((2, rows), F32),
        ],
    )(scales, frames, norm_gain.reshape(1, width), weight, gate, resets.reshape(1, rows))

    count = 32

    def moved(value, place_of):
        return lax.ppermute(value, "seq", [(i, place_of(i)) for i in range(count)])

    def along_x(shift):
        return lambda i: (i // 8) * 8 + (i + 2 * shift) % 8

    def along_y(shift):
        return lambda i: (i + 8 * shift) % 32

    pair_shape = jax.ShapeDtypeStruct((n, 2 * n), BF16)
    other = moved(carry, lambda i: i ^ 1)
    pair = pl.pallas_call(
        pair_kernel, name="pair", in_specs=[vmem()] * 2, out_specs=vmem(), out_shape=pair_shape
    )(carry, other)
    near = [moved(pair, along_x(s)) for s in (1, 2, 3)]
    total, prefix = pl.pallas_call(
        row_kernel,
        name="row",
        in_specs=[vmem()] * 4,
        out_specs=[vmem()] * 2,
        out_shape=[pair_shape] * 2,
        scratch_shapes=[pltpu.VMEM((4, n, 2 * n), BF16)],
    )(pair, *near)
    far = [moved(total, along_y(s)) for s in (1, 2, 3)]
    flat = pl.pallas_call(
        read_kernel,
        name="read",
        in_specs=[vmem()] * 8,
        out_specs=vmem(),
        out_shape=jax.ShapeDtypeStruct((rows, n), BF16),
        scratch_shapes=[pltpu.VMEM((4, n, 2 * n), BF16), pltpu.VMEM((n, n), F32)],
    )(*far, prefix, other, query, local, out_gain.reshape(1, n))
    return lax.psum_scatter(
        jnp.dot(flat, out_weight, preferred_element_type=F32).astype(BF16),
        "head",
        scatter_dimension=0,
        tiled=True,
    )


def solution(mesh):
    in_specs = (
        P("seq", None),
        P(),
        P(None, None, "head"),
        P(None, None, "head"),
        P("head"),
        P("head"),
        P("seq"),
        P("head"),
        P("head", None),
    )
    out_specs = P(("seq", "head"), None)
    return jax.shard_map(
        per_device, mesh=mesh, in_specs=in_specs, out_specs=out_specs, check_vma=False
    )
```

```python
import jax
import jax.numpy as jnp
from jax import lax
from jax.experimental import pallas as pl
from jax.experimental.pallas import tpu as pltpu
from jax.sharding import Mesh
from jax.sharding import PartitionSpec as P

KB = 1024
F32 = jnp.float32
BF16 = jnp.bfloat16
NN = (((1,), (0,)), ((), ()))
NT = (((1,), (1,)), ((), ()))
TN = (((0,), (0,)), ((), ()))
SEQ = ("y", "xh", "xl", "core")
SMALL = pltpu.CompilerParams(vmem_limit_bytes=8 << 20)
MIDDLE = pltpu.CompilerParams(vmem_limit_bytes=16 << 20)
LARGE = pltpu.CompilerParams(vmem_limit_bytes=58 << 20)


def mm(a, b, dims=NN):
    return lax.dot_general(a, b, dims, preferred_element_type=F32)


def split(a):
    hi = a.astype(BF16)
    return hi, (a - hi.astype(F32)).astype(BF16)


def mm3(a, b, dims=NN):
    (ah, al), (bh, bl) = a, b
    return mm(ah, bh, dims) + (mm(ah, bl, dims) + mm(al, bh, dims))


def unit_rows(vectors):
    return vectors * lax.rsqrt(jnp.sum(vectors * vectors, axis=-1, keepdims=True) + 1e-06)


def chunk_kernel(
    scale_ref, rate_ref, x_ref, gain_ref, w_ref, gate_ref, resets_ref,
    carry_ref, local_ref, query_ref,
    xn_ref, acc_ref, gating_ref,
):
    step = pl.program_id(0)
    n = x_ref.shape[0]

    @pl.when(step == 0)
    def _():
        x = x_ref[...].astype(F32)
        rs = lax.rsqrt(jnp.mean(x * x, axis=-1, keepdims=True) + 1e-06)
        xn_ref[...] = (x * rs * gain_ref[...]).astype(BF16)

    xb = xn_ref[:, pl.ds(pl.multiple_of(step * KB, KB), KB)]
    parts = [mm(xb, w_ref[j]) for j in range(3)]
    gating = mm(gate_ref[...], xb, NT)

    @pl.when(step == 0)
    def _():
        for j in range(3):
            acc_ref[j] = parts[j]
        gating_ref[...] = gating

    @pl.when(step > 0)
    def _():
        for j in range(3):
            acc_ref[j] = acc_ref[j] + parts[j]
        gating_ref[...] = gating_ref[...] + gating

    @pl.when(step == pl.num_programs(0) - 1)
    def _():
        query = unit_rows(acc_ref[0])
        key = unit_rows(acc_ref[1])
        value = acc_ref[2]
        gating = gating_ref[...]
        beta_row = scale_ref[...] * jax.nn.sigmoid(gating[0:1])
        logf_row = -rate_ref[...] * jax.nn.softplus(gating[1:2])
        reset_row = resets_ref[...].astype(F32)
        t = lax.broadcasted_iota(jnp.int32, (n, n), 0)
        s = lax.broadcasted_iota(jnp.int32, (n, n), 1)
        causal = t >= s
        eye = t == s

        def to_col(row):
            return jnp.sum(jnp.where(eye, row, 0.0), axis=1, keepdims=True)

        def to_row(col):
            return jnp.sum(jnp.where(eye, col, 0.0), axis=0, keepdims=True)

        beta = to_col(beta_row)
        cum = jnp.sum(jnp.where(causal, logf_row, 0.0), axis=1, keepdims=True)
        seg = jnp.sum(jnp.where(causal, reset_row, 0.0), axis=1, keepdims=True)
        cum_row = to_row(cum)
        seg_row = to_row(seg)
        same = (seg == seg_row) & causal
        decay = jnp.where(same, jnp.exp(jnp.where(same, cum - cum_row, 0.0)), 0.0)
        gamma = jnp.where(seg == 0.0, jnp.exp(cum), 0.0)
        cum_last, seg_last = cum[n - 1 : n], seg[n - 1 : n]
        tail = jnp.where(seg == seg_last, jnp.exp(cum_last - cum), 0.0)
        gamma_last = gamma[n - 1 : n]

        ks = split(key)
        gram = mm3(ks, ks, NT)
        low = jnp.where(t > s, beta * decay * gram, 0.0)
        apart = t ^ s
        inv = jnp.where(eye, 1.0, jnp.where(apart == 1, -low, 0.0))
        for level in range(1, n.bit_length() - 1):
            part = jnp.where((apart >> level) == 1, low, 0.0)
            vs = split(inv)
            inv = inv - mm3(vs, split(mm3(split(part), vs)))
        rhs = jnp.concatenate([(beta * gamma) * key, beta * value], axis=1)
        solved = split(mm3(split(inv), split(rhs)))
        folded = mm3(split(key * tail), solved, TN)
        carry_ref[:, :n] = (jnp.where(eye, gamma_last, 0.0) - folded[:, :n]).astype(BF16)
        carry_ref[:, n:] = folded[:, n:].astype(BF16)
        scores = mm3(split(query), ks, NT) * decay
        seen = mm3(split(scores), solved)
        query_ref[...] = gamma * query - seen[:, :n]
        local_ref[...] = seen[:, n:]


def after(later, earlier, n):
    both = mm(later[:, :n], earlier)
    return both[:, :n], both[:, n:] + later[:, n:].astype(F32)


def pair_kernel(own_ref, other_ref, out_ref):
    n = own_ref.shape[0]
    first = lax.axis_index("core") == 0
    own, other = own_ref[...], other_ref[...]
    earlier = jnp.where(first, own, other)
    later = jnp.where(first, other, own)
    a, b = after(later, earlier, n)
    out_ref[:, :n] = a.astype(BF16)
    out_ref[:, n:] = b.astype(BF16)


def row_kernel(own_ref, one_ref, two_ref, three_ref, total_ref, prefix_ref, held):
    n = own_ref.shape[0]
    place = lax.axis_index("xh") * 2 + lax.axis_index("xl")
    for shift, ref in enumerate((own_ref, one_ref, two_ref, three_ref)):
        held[(place + (4 - shift)) % 4] = ref[...]

    def joined(later, earlier):
        a, b = after(later, earlier, n)
        return jnp.concatenate([a, b], axis=1).astype(BF16)

    low = joined(held[1], held[0])
    high = joined(held[3], held[2])
    a, b = after(high, low, n)
    total_ref[:, :n] = a.astype(BF16)
    total_ref[:, n:] = b.astype(BF16)

    @pl.when(place == 0)
    def _():
        prefix_ref[...] = jnp.zeros_like(prefix_ref)

    @pl.when(place == 1)
    def _():
        prefix_ref[...] = held[0]

    @pl.when(place == 2)
    def _():
        prefix_ref[...] = low

    @pl.when(place == 3)
    def _():
        prefix_ref[...] = joined(held[2], low)


def read_kernel(
    one_ref, two_ref, three_ref, prefix_ref, other_ref, query_ref, local_ref, gain_ref,
    out_ref, held, state,
):
    n = query_ref.shape[0]
    place = lax.axis_index("y")
    for shift, ref in enumerate((one_ref, two_ref, three_ref)):
        held[(place + (3 - shift)) % 4] = ref[...]

    def push(pair, value):
        hi, lo = split(value)
        return mm(pair[:, :n], hi) + mm(pair[:, :n], lo) + pair[:, n:].astype(F32)

    @pl.when(place == 0)
    def _():
        state[...] = jnp.zeros_like(state)

    @pl.when(place > 0)
    def _():
        state[...] = held[0, :, n:].astype(F32)

    for turn in (1, 2):
        @pl.when(place > turn)
        def _():
            state[...] = push(held[turn], state[...])

    @pl.when(lax.axis_index("xh") + lax.axis_index("xl") > 0)
    def _():
        state[...] = push(prefix_ref[...], state[...])

    @pl.when(lax.axis_index("core") > 0)
    def _():
        state[...] = push(other_ref[...], state[...])

    read = local_ref[...] + mm3(split(query_ref[...]), split(state[...]))
    read = read * lax.rsqrt(jnp.mean(read * read, axis=-1, keepdims=True) + 1e-06)
    flat = (read * gain_ref[...]).astype(BF16)
    out_ref[0] = flat
    out_ref[1] = flat


def take_kernel(whole_ref, out_ref, sem):
    width = out_ref.shape[1]
    block = lax.axis_index("core") * 2 + lax.axis_index("xl")
    columns = pl.ds(pl.multiple_of(block * width, width), width)
    copy = pltpu.make_async_copy(whole_ref.at[:, columns], out_ref, sem)
    copy.start()
    copy.wait()


def mix_kernel(own_ref, other_ref, *refs):
    weights, outs = refs[:8], refs[8:]
    core, half, head = lax.axis_index("core"), lax.axis_index("xl"), lax.axis_index("head")
    rows = own_ref.shape[2]
    for shift, ref in enumerate(weights):
        source = (head + (8 - shift)) % 8
        block = []
        for place in (half, 1 - half):
            for ref_x in (own_ref, other_ref):
                block.append(ref_x[place, source])
        part = mm(jnp.concatenate(block, axis=0), ref[...])
        total = part if shift == 0 else total + part
    total = total.astype(BF16)
    for k, ref in enumerate(outs):
        ref[...] = total[k * rows : (k + 1) * rows]


def lay_kernel(mine_ref, core_ref, half_ref, far_ref, out_ref):
    width = mine_ref.shape[1]
    block = lax.axis_index("core") * 2 + lax.axis_index("xl")
    for flip, ref in ((0, mine_ref), (2, core_ref), (1, half_ref), (3, far_ref)):
        place = pl.multiple_of((block ^ flip) * width, width)
        out_ref[:, pl.ds(place, width)] = ref[...]


def vmem():
    return pl.BlockSpec(memory_space=pltpu.VMEM)


def per_device(
    frames, norm_gain, qkv_weight, gate_weight, beta_scale, decay_rate, resets, out_gain, out_weight
):
    rows, width = frames.shape
    n = qkv_weight.shape[2]
    weight = qkv_weight.transpose(1, 0, 2)
    gate = gate_weight.transpose(2, 1, 0).reshape(2, width)
    whole = lambda shape: pl.BlockSpec(shape, lambda i: (0,) * len(shape), pipeline_mode=pl.Buffered(1))
    carry, local, query = pl.pallas_call(
        chunk_kernel,
        name="chunk",
        grid=(width // KB,),
        in_specs=[
            whole((1, 1)),
            whole((1, 1)),
            whole((rows, width)),
            whole((1, width)),
            pl.BlockSpec((3, KB, n), lambda i: (0, i, 0)),
            pl.BlockSpec((2, KB), lambda i: (0, i)),
            whole((1, rows)),
        ],
        out_specs=[whole((n, 2 * n)), whole((rows, n)), whole((rows, n))],
        out_shape=[
            jax.ShapeDtypeStruct((n, 2 * n), BF16),
            jax.ShapeDtypeStruct((rows, n), F32),
            jax.ShapeDtypeStruct((rows, n), F32),
        ],
        scratch_shapes=[
            pltpu.VMEM((rows, width), BF16),
            pltpu.VMEM((3, rows, n), F32),
            pltpu.VMEM((2, rows), F32),
        ],
        compiler_params=LARGE,
    )(beta_scale.reshape(1, 1), decay_rate.reshape(1, 1), frames, norm_gain.reshape(1, width), weight, gate, resets.reshape(1, rows))

    count = 32

    def moved(value, place_of):
        return lax.ppermute(value, SEQ, [(i, place_of(i)) for i in range(count)])

    def along_x(shift):
        return lambda i: (i // 8) * 8 + (i + 2 * shift) % 8

    def along_y(shift):
        return lambda i: (i + 8 * shift) % 32

    def flip(bits):
        return lambda i: i ^ bits

    def along_z(value, shift):
        return lax.ppermute(value, "head", [(i, (i + shift) % 8) for i in range(8)])

    def later(values, gate):
        return lax.optimization_barrier((values, gate))[0]

    quarter = out_weight.shape[1] // 4
    mine = pl.pallas_call(
        take_kernel,
        name="take",
        in_specs=[pl.BlockSpec(memory_space=pl.ANY)],
        out_specs=vmem(),
        out_shape=jax.ShapeDtypeStruct((n, quarter), BF16),
        scratch_shapes=[pltpu.SemaphoreType.DMA],
        compiler_params=LARGE,
    )(out_weight)
    up = [along_z(mine, 1)]
    down = [along_z(mine, -1)]

    pair_shape = jax.ShapeDtypeStruct((n, 2 * n), BF16)
    other = moved(carry, flip(1))
    pair = pl.pallas_call(
        pair_kernel,
        name="pair",
        in_specs=[vmem()] * 2,
        out_specs=vmem(),
        out_shape=pair_shape,
        compiler_params=SMALL,
    )(carry, other)
    near = [moved(pair, along_x(s)) for s in (1, 2, 3)]
    ahead, behind = later((up[-1], down[-1]), other)
    up.append(along_z(ahead, 1))
    down.append(along_z(behind, -1))
    total, prefix = pl.pallas_call(
        row_kernel,
        name="row",
        in_specs=[vmem()] * 4,
        out_specs=[vmem()] * 2,
        out_shape=[pair_shape] * 2,
        scratch_shapes=[pltpu.VMEM((4, n, 2 * n), BF16)],
        compiler_params=SMALL,
    )(pair, *near)
    far = [moved(total, along_y(s)) for s in (1, 2, 3)]
    ahead, behind = later((up[-1], down[-1]), total)
    up.append(along_z(ahead, 1))
    down.append(along_z(behind, -1))
    flat = pl.pallas_call(
        read_kernel,
        name="read",
        in_specs=[vmem()] * 8,
        out_specs=vmem(),
        out_shape=jax.ShapeDtypeStruct((2, rows, n), BF16),
        scratch_shapes=[pltpu.VMEM((4, n, 2 * n), BF16), pltpu.VMEM((n, n), F32)],
        compiler_params=SMALL,
    )(*far, prefix, other, query, local, out_gain.reshape(1, n))
    ahead = later(up[-1], far[-1])
    up.append(along_z(ahead, 1))
    part = rows // 8
    reads = lax.all_to_all(
        flat.reshape(16, part, n), ("xl", "head"), 0, 0, tiled=True
    ).reshape(2, 8, part, n)
    beside = moved(reads, flip(1))
    piece = jax.ShapeDtypeStruct((part, quarter), BF16)
    kept, to_core, to_half, to_far = pl.pallas_call(
        mix_kernel,
        name="mix",
        in_specs=[vmem()] * 10,
        out_specs=[vmem()] * 4,
        out_shape=[piece] * 4,
        compiler_params=MIDDLE,
    )(reads, beside, mine, *up, *down[::-1])
    return pl.pallas_call(
        lay_kernel,
        name="lay",
        in_specs=[vmem()] * 4,
        out_specs=vmem(),
        out_shape=jax.ShapeDtypeStruct((part, 4 * quarter), BF16),
        compiler_params=SMALL,
    )(kept, moved(to_core, flip(1)), moved(to_half, flip(2)), moved(to_far, flip(3)))


def solution(mesh):
    fine = Mesh(mesh.devices.reshape(4, 2, 2, 2, 8), SEQ + ("head",))
    in_specs = (
        P(SEQ, None),
        P(),
        P(None, None, "head"),
        P(None, None, "head"),
        P("head"),
        P("head"),
        P(SEQ),
        P("head"),
        P("head", None),
    )
    out_specs = P(SEQ + ("head",), None)
    return jax.shard_map(
        per_device, mesh=fine, in_specs=in_specs, out_specs=out_specs, check_vma=False
    )
```

```python
import jax
import jax.numpy as jnp
from jax import lax
from jax.experimental import pallas as pl
from jax.experimental.pallas import tpu as pltpu
from jax.sharding import Mesh
from jax.sharding import PartitionSpec as P

KB = 1024
F32 = jnp.float32
BF16 = jnp.bfloat16
NN = (((1,), (0,)), ((), ()))
NT = (((1,), (1,)), ((), ()))
TN = (((0,), (0,)), ((), ()))
SEQ = ("y", "xh", "xl", "core")
SMALL = pltpu.CompilerParams(vmem_limit_bytes=8 << 20)
MIDDLE = pltpu.CompilerParams(vmem_limit_bytes=16 << 20)
LARGE = pltpu.CompilerParams(vmem_limit_bytes=57 << 20)


def mm(a, b, dims=NN):
    return lax.dot_general(a, b, dims, preferred_element_type=F32)


def split(a):
    hi = a.astype(BF16)
    return hi, (a - hi.astype(F32)).astype(BF16)


def mm3(a, b, dims=NN):
    (ah, al), (bh, bl) = a, b
    return mm(ah, bh, dims) + (mm(ah, bl, dims) + mm(al, bh, dims))


def unit_rows(vectors):
    return vectors * lax.rsqrt(jnp.sum(vectors * vectors, axis=-1, keepdims=True) + 1e-06)


def chunk_kernel(
    scale_ref, rate_ref, x_ref, gain_ref, w_ref, gate_ref, resets_ref,
    carry_ref, local_ref, query_ref,
    xn_ref, acc_ref, gating_ref,
):
    step = pl.program_id(0)
    n = x_ref.shape[0]

    @pl.when(step == 0)
    def _():
        x = x_ref[...].astype(F32)
        rs = lax.rsqrt(jnp.mean(x * x, axis=-1, keepdims=True) + 1e-06)
        xn_ref[...] = (x * rs * gain_ref[...]).astype(BF16)

    xb = xn_ref[:, pl.ds(pl.multiple_of(step * KB, KB), KB)]
    parts = [mm(xb, w_ref[j]) for j in range(3)]
    gating = mm(gate_ref[...], xb, NT)

    @pl.when(step == 0)
    def _():
        for j in range(3):
            acc_ref[j] = parts[j]
        gating_ref[...] = gating

    @pl.when(step > 0)
    def _():
        for j in range(3):
            acc_ref[j] = acc_ref[j] + parts[j]
        gating_ref[...] = gating_ref[...] + gating

    @pl.when(step == pl.num_programs(0) - 1)
    def _():
        query = unit_rows(acc_ref[0])
        key = unit_rows(acc_ref[1])
        value = acc_ref[2]
        gating = gating_ref[...]
        beta_row = scale_ref[...] * jax.nn.sigmoid(gating[0:1])
        logf_row = -rate_ref[...] * jax.nn.softplus(gating[1:2])
        reset_row = resets_ref[...].astype(F32)
        t = lax.broadcasted_iota(jnp.int32, (n, n), 0)
        s = lax.broadcasted_iota(jnp.int32, (n, n), 1)
        causal = t >= s
        eye = t == s

        def to_col(row):
            return jnp.sum(jnp.where(eye, row, 0.0), axis=1, keepdims=True)

        def to_row(col):
            return jnp.sum(jnp.where(eye, col, 0.0), axis=0, keepdims=True)

        beta = to_col(beta_row)
        cum = jnp.sum(jnp.where(causal, logf_row, 0.0), axis=1, keepdims=True)
        seg = jnp.sum(jnp.where(causal, reset_row, 0.0), axis=1, keepdims=True)
        cum_row = to_row(cum)
        seg_row = to_row(seg)
        same = (seg == seg_row) & causal
        decay = jnp.where(same, jnp.exp(jnp.where(same, cum - cum_row, 0.0)), 0.0)
        gamma = jnp.where(seg == 0.0, jnp.exp(cum), 0.0)
        cum_last, seg_last = cum[n - 1 : n], seg[n - 1 : n]
        tail = jnp.where(seg == seg_last, jnp.exp(cum_last - cum), 0.0)
        gamma_last = gamma[n - 1 : n]

        ks = split(key)
        gram = mm3(ks, ks, NT)
        low = jnp.where(t > s, beta * decay * gram, 0.0)
        apart = t ^ s
        inv = jnp.where(eye, 1.0, jnp.where(apart == 1, -low, 0.0))
        for level in range(1, n.bit_length() - 1):
            part = jnp.where((apart >> level) == 1, low, 0.0)
            vs = split(inv)
            inv = inv - mm3(vs, split(mm3(split(part), vs)))
        rhs = jnp.concatenate([(beta * gamma) * key, beta * value], axis=1)
        solved = split(mm3(split(inv), split(rhs)))
        folded = mm3(split(key * tail), solved, TN)
        carry_ref[:, :n] = (jnp.where(eye, gamma_last, 0.0) - folded[:, :n]).astype(BF16)
        carry_ref[:, n:] = folded[:, n:].astype(BF16)
        scores = mm3(split(query), ks, NT) * decay
        seen = mm3(split(scores), solved)
        query_ref[...] = gamma * query - seen[:, :n]
        local_ref[...] = seen[:, n:]


def after(later, earlier, n):
    both = mm(later[:, :n], earlier)
    return both[:, :n], both[:, n:] + later[:, n:].astype(F32)


def own_half(ref):
    half = ref.shape[0] // 2
    return ref[pl.ds(pl.multiple_of(lax.axis_index("core") * half, half), half)]


def hold(held, place, near_ref, swap_ref):
    half = near_ref.shape[0]
    core = lax.axis_index("core")
    held[place, pl.ds(pl.multiple_of(core * half, half), half)] = near_ref[...]
    held[place, pl.ds(pl.multiple_of((1 - core) * half, half), half)] = swap_ref[...]


def pair_kernel(own_ref, other_ref, out_ref, half_ref):
    n = own_ref.shape[0]
    first = lax.axis_index("core") == 0
    own, other = own_ref[...], other_ref[...]
    earlier = jnp.where(first, own, other)
    later = jnp.where(first, other, own)
    a, b = after(later, earlier, n)
    out_ref[:, :n] = a.astype(BF16)
    out_ref[:, n:] = b.astype(BF16)
    half_ref[...] = own_half(out_ref)


def row_kernel(own_ref, *refs):
    near, swapped, (half_ref, prefix_ref, held, total_ref) = refs[:3], refs[3:6], refs[6:]
    n = own_ref.shape[0]
    place = lax.axis_index("xh") * 2 + lax.axis_index("xl")
    held[place] = own_ref[...]
    for shift, ref, swap in zip((1, 2, 3), near, swapped):
        hold(held, (place + (4 - shift)) % 4, ref, swap)

    def joined(later, earlier):
        a, b = after(later, earlier, n)
        return jnp.concatenate([a, b], axis=1).astype(BF16)

    low = joined(held[1], held[0])
    high = joined(held[3], held[2])
    a, b = after(high, low, n)
    total_ref[:, :n] = a.astype(BF16)
    total_ref[:, n:] = b.astype(BF16)
    half_ref[...] = own_half(total_ref)

    @pl.when(place == 0)
    def _():
        prefix_ref[...] = jnp.zeros_like(prefix_ref)

    @pl.when(place == 1)
    def _():
        prefix_ref[...] = held[0]

    @pl.when(place == 2)
    def _():
        prefix_ref[...] = low

    @pl.when(place == 3)
    def _():
        prefix_ref[...] = joined(held[2], low)


def read_kernel(*refs):
    near, swapped = refs[:3], refs[3:6]
    prefix_ref, other_ref, query_ref, local_ref, gain_ref, out_ref, held, state = refs[6:]
    n = query_ref.shape[0]
    place = lax.axis_index("y")
    for shift, ref, swap in zip((1, 2, 3), near, swapped):
        hold(held, (place + (4 - shift)) % 4, ref, swap)

    def push(pair, value):
        hi, lo = split(value)
        return mm(pair[:, :n], hi) + mm(pair[:, :n], lo) + pair[:, n:].astype(F32)

    @pl.when(place == 0)
    def _():
        state[...] = jnp.zeros_like(state)

    @pl.when(place > 0)
    def _():
        state[...] = held[0, :, n:].astype(F32)

    for turn in (1, 2):
        @pl.when(place > turn)
        def _():
            state[...] = push(held[turn], state[...])

    @pl.when(lax.axis_index("xh") + lax.axis_index("xl") > 0)
    def _():
        state[...] = push(prefix_ref[...], state[...])

    @pl.when(lax.axis_index("core") > 0)
    def _():
        state[...] = push(other_ref[...], state[...])

    read = local_ref[...] + mm3(split(query_ref[...]), split(state[...]))
    read = read * lax.rsqrt(jnp.mean(read * read, axis=-1, keepdims=True) + 1e-06)
    flat = (read * gain_ref[...]).astype(BF16)
    out_ref[0] = flat
    out_ref[1] = flat


def mix_kernel(own_ref, other_ref, *refs):
    weights, across, outs = refs[:7], refs[7:9], refs[9:]
    core, half, head = lax.axis_index("core"), lax.axis_index("xl"), lax.axis_index("head")
    rows = own_ref.shape[2]
    for shift, refs in zip((0, 1, 2, 3, 5, 6, 7, 4), [(ref,) for ref in weights] + [across]):
        source = (head + (8 - shift)) % 8
        block = []
        for place in (half, 1 - half):
            for ref_x in (own_ref, other_ref):
                block.append(ref_x[place, source])
        block = jnp.concatenate(block, axis=0)
        part = jnp.concatenate([mm(block, ref[...]) for ref in refs], axis=1)
        total = part if shift == 0 else total + part
    total = total.astype(BF16)
    for k, ref in enumerate(outs):
        ref[...] = total[k * rows : (k + 1) * rows]


def lay_kernel(mine_ref, core_ref, half_ref, far_ref, out_ref):
    width = mine_ref.shape[1]
    block = lax.axis_index("core") * 2 + lax.axis_index("xl")
    for flip, ref in ((0, mine_ref), (2, core_ref), (1, half_ref), (3, far_ref)):
        place = pl.multiple_of((block ^ flip) * width, width)
        out_ref[:, pl.ds(place, width)] = ref[...]


def vmem():
    return pl.BlockSpec(memory_space=pltpu.VMEM)


def per_device(
    frames, norm_gain, qkv_weight, gate_weight, beta_scale, decay_rate, resets, out_gain, out_weight
):
    rows, width = frames.shape
    n = qkv_weight.shape[2]
    weight = qkv_weight.transpose(1, 0, 2)
    gate = gate_weight.transpose(2, 1, 0).reshape(2, width)
    whole = lambda shape: pl.BlockSpec(shape, lambda i: (0,) * len(shape), pipeline_mode=pl.Buffered(1))
    carry, local, query = pl.pallas_call(
        chunk_kernel,
        name="chunk",
        grid=(width // KB,),
        in_specs=[
            whole((1, 1)),
            whole((1, 1)),
            whole((rows, width)),
            whole((1, width)),
            pl.BlockSpec((3, KB, n), lambda i: (0, i, 0)),
            pl.BlockSpec((2, KB), lambda i: (0, i)),
            whole((1, rows)),
        ],
        out_specs=[whole((n, 2 * n)), whole((rows, n)), whole((rows, n))],
        out_shape=[
            jax.ShapeDtypeStruct((n, 2 * n), BF16),
            jax.ShapeDtypeStruct((rows, n), F32),
            jax.ShapeDtypeStruct((rows, n), F32),
        ],
        scratch_shapes=[
            pltpu.VMEM((rows, width), BF16),
            pltpu.VMEM((3, rows, n), F32),
            pltpu.VMEM((2, rows), F32),
        ],
        compiler_params=LARGE,
    )(beta_scale.reshape(1, 1), decay_rate.reshape(1, 1), frames, norm_gain.reshape(1, width), weight, gate, resets.reshape(1, rows))

    count = 32

    def moved(value, place_of):
        return lax.ppermute(value, SEQ, [(i, place_of(i)) for i in range(count)])

    def along_x(shift):
        return lambda i: (i // 8) * 8 + (i + 2 * shift) % 8

    def along_y(shift):
        return lambda i: (i + 8 * shift) % 32

    def flip(bits):
        return lambda i: i ^ bits

    def along_z(value, shift):
        return lax.ppermute(value, "head", [(i, (i + shift) % 8) for i in range(8)])

    def later(values, gate):
        return lax.optimization_barrier((values, gate))[0]

    quarter = out_weight.shape[1] // 4
    block = lax.axis_index("core") * 2 + lax.axis_index("xl")
    mine = lax.dynamic_slice_in_dim(out_weight, block * quarter, quarter, 1)
    up_one, down_one = along_z(mine, 1), along_z(mine, -1)

    pair_shape = jax.ShapeDtypeStruct((n, 2 * n), BF16)
    half_shape = jax.ShapeDtypeStruct((n // 2, 2 * n), BF16)
    other = moved(carry, flip(1))
    pair, half = pl.pallas_call(
        pair_kernel,
        name="pair",
        in_specs=[vmem()] * 2,
        out_specs=[vmem()] * 2,
        out_shape=[pair_shape, half_shape],
        compiler_params=SMALL,
    )(carry, other)
    near = [moved(half, along_x(s)) for s in (1, 2, 3)]
    swapped = [moved(value, flip(1)) for value in near]
    ahead, behind = later((up_one, down_one), near)
    up_two, down_two = along_z(ahead, 1), along_z(behind, -1)
    half, prefix = pl.pallas_call(
        row_kernel,
        name="row",
        in_specs=[vmem()] * 7,
        out_specs=[vmem()] * 2,
        out_shape=[half_shape, pair_shape],
        scratch_shapes=[pltpu.VMEM((4, n, 2 * n), BF16), pltpu.VMEM((n, 2 * n), BF16)],
        compiler_params=SMALL,
    )(pair, *near, *swapped)
    near = [moved(half, along_y(s)) for s in (1, 2, 3)]
    swapped = [moved(value, flip(1)) for value in near]
    ahead, behind = later((up_two, down_two), near)
    up_three, down_three = along_z(ahead, 1), along_z(behind, -1)
    flat = pl.pallas_call(
        read_kernel,
        name="read",
        in_specs=[vmem()] * 11,
        out_specs=vmem(),
        out_shape=jax.ShapeDtypeStruct((2, rows, n), BF16),
        scratch_shapes=[pltpu.VMEM((4, n, 2 * n), BF16), pltpu.VMEM((n, n), F32)],
        compiler_params=SMALL,
    )(*near, *swapped, prefix, other, query, local, out_gain.reshape(1, n))
    across = [
        along_z(up_three[:, : quarter // 2], 1),
        along_z(down_three[:, quarter // 2 :], -1),
    ]
    part = rows // 8
    reads = lax.all_to_all(
        flat.reshape(16, part, n), ("xl", "head"), 0, 0, tiled=True
    ).reshape(2, 8, part, n)
    beside = moved(reads, flip(1))
    piece = jax.ShapeDtypeStruct((part, quarter), BF16)
    kept, to_core, to_half, to_far = pl.pallas_call(
        mix_kernel,
        name="mix",
        in_specs=[vmem()] * 11,
        out_specs=[vmem()] * 4,
        out_shape=[piece] * 4,
        compiler_params=MIDDLE,
    )(reads, beside, mine, up_one, up_two, up_three, down_three, down_two, down_one, *across)
    return pl.pallas_call(
        lay_kernel,
        name="lay",
        in_specs=[vmem()] * 4,
        out_specs=vmem(),
        out_shape=jax.ShapeDtypeStruct((part, 4 * quarter), BF16),
        compiler_params=SMALL,
    )(kept, moved(to_core, flip(1)), moved(to_half, flip(2)), moved(to_far, flip(3)))


def solution(mesh):
    fine = Mesh(mesh.devices.reshape(4, 2, 2, 2, 8), SEQ + ("head",))
    in_specs = (
        P(SEQ, None),
        P(),
        P(None, None, "head"),
        P(None, None, "head"),
        P("head"),
        P("head"),
        P(SEQ),
        P("head"),
        P("head", None),
    )
    out_specs = P(SEQ + ("head",), None)
    return jax.shard_map(
        per_device, mesh=fine, in_specs=in_specs, out_specs=out_specs, check_vma=False
    )
```

```python
import jax
import jax.numpy as jnp
from jax import lax
from jax.experimental import pallas as pl
from jax.experimental.pallas import tpu as pltpu
from jax.sharding import Mesh
from jax.sharding import PartitionSpec as P

KB = 1024
F32 = jnp.float32
BF16 = jnp.bfloat16
NN = (((1,), (0,)), ((), ()))
NT = (((1,), (1,)), ((), ()))
TN = (((0,), (0,)), ((), ()))
SEQ = ("y", "xh", "xl", "core")
SMALL = pltpu.CompilerParams(vmem_limit_bytes=8 << 20)
MIDDLE = pltpu.CompilerParams(vmem_limit_bytes=16 << 20)
LARGE = pltpu.CompilerParams(vmem_limit_bytes=57 << 20)


def mm(a, b, dims=NN):
    return lax.dot_general(a, b, dims, preferred_element_type=F32)


def split(a):
    hi = a.astype(BF16)
    return hi, (a - hi.astype(F32)).astype(BF16)


def mm3(a, b, dims=NN):
    (ah, al), (bh, bl) = a, b
    return mm(ah, bh, dims) + (mm(ah, bl, dims) + mm(al, bh, dims))


def unit_rows(vectors):
    return vectors * lax.rsqrt(jnp.sum(vectors * vectors, axis=-1, keepdims=True) + 1e-06)


def chunk_kernel(
    scale_ref, rate_ref, x_ref, gain_ref, w_ref, gate_ref, resets_ref,
    carry_ref, local_ref, query_ref,
    xn_ref, acc_ref, gating_ref,
):
    step = pl.program_id(0)
    n = x_ref.shape[0]

    @pl.when(step == 0)
    def _():
        x = x_ref[...].astype(F32)
        rs = lax.rsqrt(jnp.mean(x * x, axis=-1, keepdims=True) + 1e-06)
        xn_ref[...] = (x * rs * gain_ref[...]).astype(BF16)

    xb = xn_ref[:, pl.ds(pl.multiple_of(step * KB, KB), KB)]
    parts = [mm(xb, w_ref[j]) for j in range(3)]
    gating = mm(gate_ref[...], xb, NT)

    @pl.when(step == 0)
    def _():
        for j in range(3):
            acc_ref[j] = parts[j]
        gating_ref[...] = gating

    @pl.when(step > 0)
    def _():
        for j in range(3):
            acc_ref[j] = acc_ref[j] + parts[j]
        gating_ref[...] = gating_ref[...] + gating

    @pl.when(step == pl.num_programs(0) - 1)
    def _():
        query = unit_rows(acc_ref[0])
        key = unit_rows(acc_ref[1])
        value = acc_ref[2]
        gating = gating_ref[...]
        beta_row = scale_ref[0] * jax.nn.sigmoid(gating[0:1])
        logf_row = -rate_ref[0] * jax.nn.softplus(gating[1:2])
        reset_row = resets_ref[...].astype(F32)
        t = lax.broadcasted_iota(jnp.int32, (n, n), 0)
        s = lax.broadcasted_iota(jnp.int32, (n, n), 1)
        causal = t >= s
        eye = t == s

        def to_col(row):
            return jnp.sum(jnp.where(eye, row, 0.0), axis=1, keepdims=True)

        def to_row(col):
            return jnp.sum(jnp.where(eye, col, 0.0), axis=0, keepdims=True)

        beta = to_col(beta_row)
        cum = jnp.sum(jnp.where(causal, logf_row, 0.0), axis=1, keepdims=True)
        seg = jnp.sum(jnp.where(causal, reset_row, 0.0), axis=1, keepdims=True)
        cum_row = to_row(cum)
        seg_row = to_row(seg)
        same = (seg == seg_row) & causal
        decay = jnp.where(same, jnp.exp(jnp.where(same, cum - cum_row, 0.0)), 0.0)
        gamma = jnp.where(seg == 0.0, jnp.exp(cum), 0.0)
        cum_last, seg_last = cum[n - 1 : n], seg[n - 1 : n]
        tail = jnp.where(seg == seg_last, jnp.exp(cum_last - cum), 0.0)
        gamma_last = gamma[n - 1 : n]

        ks = split(key)
        gram = mm3(ks, ks, NT)
        low = jnp.where(t > s, beta * decay * gram, 0.0)
        apart = t ^ s
        inv = jnp.where(eye, 1.0, jnp.where(apart == 1, -low, 0.0))
        for level in range(1, n.bit_length() - 1):
            part = jnp.where((apart >> level) == 1, low, 0.0)
            vs = split(inv)
            inv = inv - mm3(vs, split(mm3(split(part), vs)))
        rhs = jnp.concatenate([(beta * gamma) * key, beta * value], axis=1)
        solved = split(mm3(split(inv), split(rhs)))
        folded = mm3(split(key * tail), solved, TN)
        carry_ref[:, :n] = (jnp.where(eye, gamma_last, 0.0) - folded[:, :n]).astype(BF16)
        carry_ref[:, n:] = folded[:, n:].astype(BF16)
        scores = mm3(split(query), ks, NT) * decay
        seen = mm3(split(scores), solved)
        query_ref[...] = gamma * query - seen[:, :n]
        local_ref[...] = seen[:, n:]


def after(later, earlier, n):
    both = mm(later[:, :n], earlier)
    return both[:, :n], both[:, n:] + later[:, n:].astype(F32)


def own_half(ref):
    half = ref.shape[0] // 2
    return ref[pl.ds(pl.multiple_of(lax.axis_index("core") * half, half), half)]


def hold(held, place, near_ref, swap_ref):
    half = near_ref.shape[0]
    core = lax.axis_index("core")
    held[place, pl.ds(pl.multiple_of(core * half, half), half)] = near_ref[...]
    held[place, pl.ds(pl.multiple_of((1 - core) * half, half), half)] = swap_ref[...]


def pair_kernel(own_ref, other_ref, out_ref, half_ref):
    n = own_ref.shape[0]
    first = lax.axis_index("core") == 0
    own, other = own_ref[...], other_ref[...]
    earlier = jnp.where(first, own, other)
    later = jnp.where(first, other, own)
    a, b = after(later, earlier, n)
    out_ref[:, :n] = a.astype(BF16)
    out_ref[:, n:] = b.astype(BF16)
    half_ref[...] = own_half(out_ref)


def row_kernel(own_ref, *refs):
    near, swapped, (half_ref, prefix_ref, held, total_ref) = refs[:3], refs[3:6], refs[6:]
    n = own_ref.shape[0]
    place = lax.axis_index("xh") * 2 + lax.axis_index("xl")
    held[place] = own_ref[...]
    for shift, ref, swap in zip((1, 2, 3), near, swapped):
        hold(held, (place + (4 - shift)) % 4, ref, swap)

    def joined(later, earlier):
        a, b = after(later, earlier, n)
        return jnp.concatenate([a, b], axis=1).astype(BF16)

    low = joined(held[1], held[0])
    high = joined(held[3], held[2])
    a, b = after(high, low, n)
    total_ref[:, :n] = a.astype(BF16)
    total_ref[:, n:] = b.astype(BF16)
    half_ref[...] = own_half(total_ref)

    @pl.when(place == 0)
    def _():
        prefix_ref[...] = jnp.zeros_like(prefix_ref)

    @pl.when(place == 1)
    def _():
        prefix_ref[...] = held[0]

    @pl.when(place == 2)
    def _():
        prefix_ref[...] = low

    @pl.when(place == 3)
    def _():
        prefix_ref[...] = joined(held[2], low)


def read_kernel(*refs):
    near, swapped = refs[:3], refs[3:6]
    prefix_ref, other_ref, query_ref, local_ref, gain_ref, out_ref, held, state = refs[6:]
    n = query_ref.shape[0]
    place = lax.axis_index("y")
    for shift, ref, swap in zip((1, 2, 3), near, swapped):
        hold(held, (place + (4 - shift)) % 4, ref, swap)

    def push(pair, value):
        hi, lo = split(value)
        return mm(pair[:, :n], hi) + mm(pair[:, :n], lo) + pair[:, n:].astype(F32)

    @pl.when(place == 0)
    def _():
        state[...] = jnp.zeros_like(state)

    @pl.when(place > 0)
    def _():
        state[...] = held[0, :, n:].astype(F32)

    for turn in (1, 2):
        @pl.when(place > turn)
        def _():
            state[...] = push(held[turn], state[...])

    @pl.when(lax.axis_index("xh") + lax.axis_index("xl") > 0)
    def _():
        state[...] = push(prefix_ref[...], state[...])

    @pl.when(lax.axis_index("core") > 0)
    def _():
        state[...] = push(other_ref[...], state[...])

    read = local_ref[...] + mm3(split(query_ref[...]), split(state[...]))
    read = read * lax.rsqrt(jnp.mean(read * read, axis=-1, keepdims=True) + 1e-06)
    flat = (read * gain_ref[...]).astype(BF16)
    out_ref[0] = flat
    out_ref[1] = flat


def mix_kernel(own_ref, other_ref, weight_ref, *outs):
    half = lax.axis_index("xl")
    rows = own_ref.shape[2]
    for head in range(weight_ref.shape[0]):
        block = [ref[place, head] for place in (half, 1 - half) for ref in (own_ref, other_ref)]
        part = mm(jnp.concatenate(block, axis=0), weight_ref[head])
        total = part if head == 0 else total + part
    total = total.astype(BF16)
    for k, ref in enumerate(outs):
        ref[...] = total[k * rows : (k + 1) * rows]


def lay_kernel(mine_ref, core_ref, half_ref, far_ref, out_ref):
    width = mine_ref.shape[1]
    block = lax.axis_index("core") * 2 + lax.axis_index("xl")
    for flip, ref in ((0, mine_ref), (2, core_ref), (1, half_ref), (3, far_ref)):
        place = pl.multiple_of((block ^ flip) * width, width)
        out_ref[:, pl.ds(place, width)] = ref[...]


def vmem():
    return pl.BlockSpec(memory_space=pltpu.VMEM)


def per_device(
    frames, norm_gain, qkv_weight, gate_weight, beta_scale, decay_rate, resets, out_gain, out_weight
):
    rows, width = frames.shape
    n = qkv_weight.shape[2]
    weight = qkv_weight.transpose(1, 0, 2)
    gate = gate_weight.transpose(2, 1, 0).reshape(2, width)
    whole = lambda shape: pl.BlockSpec(shape, lambda i: (0,) * len(shape), pipeline_mode=pl.Buffered(1))
    carry, local, query = pl.pallas_call(
        chunk_kernel,
        name="chunk",
        grid=(width // KB,),
        in_specs=[
            pl.BlockSpec(memory_space=pltpu.SMEM),
            pl.BlockSpec(memory_space=pltpu.SMEM),
            whole((rows, width)),
            whole((1, width)),
            pl.BlockSpec((3, KB, n), lambda i: (0, i, 0)),
            pl.BlockSpec((2, KB), lambda i: (0, i)),
            whole((1, rows)),
        ],
        out_specs=[whole((n, 2 * n)), whole((rows, n)), whole((rows, n))],
        out_shape=[
            jax.ShapeDtypeStruct((n, 2 * n), BF16),
            jax.ShapeDtypeStruct((rows, n), F32),
            jax.ShapeDtypeStruct((rows, n), F32),
        ],
        scratch_shapes=[
            pltpu.VMEM((rows, width), BF16),
            pltpu.VMEM((3, rows, n), F32),
            pltpu.VMEM((2, rows), F32),
        ],
        compiler_params=LARGE,
    )(beta_scale, decay_rate, frames, norm_gain.reshape(1, width), weight, gate, resets.reshape(1, rows))

    count = 32

    def moved(value, place_of):
        return lax.ppermute(value, SEQ, [(i, place_of(i)) for i in range(count)])

    def along_x(shift):
        return lambda i: (i // 8) * 8 + (i + 2 * shift) % 8

    def along_y(shift):
        return lambda i: (i + 8 * shift) % 32

    def flip(bits):
        return lambda i: i ^ bits

    quarter = out_weight.shape[1] // 4
    block = lax.axis_index("core") * 2 + lax.axis_index("xl")
    mine = lax.dynamic_slice_in_dim(out_weight, block * quarter, quarter, 1)
    columns = lax.all_gather(mine, "head", tiled=False)

    pair_shape = jax.ShapeDtypeStruct((n, 2 * n), BF16)
    half_shape = jax.ShapeDtypeStruct((n // 2, 2 * n), BF16)
    other = moved(carry, flip(1))
    pair, half = pl.pallas_call(
        pair_kernel,
        name="pair",
        in_specs=[vmem()] * 2,
        out_specs=[vmem()] * 2,
        out_shape=[pair_shape, half_shape],
        compiler_params=SMALL,
    )(carry, other)
    near = [moved(half, along_x(s)) for s in (1, 2, 3)]
    swapped = [moved(value, flip(1)) for value in near]
    half, prefix = pl.pallas_call(
        row_kernel,
        name="row",
        in_specs=[vmem()] * 7,
        out_specs=[vmem()] * 2,
        out_shape=[half_shape, pair_shape],
        scratch_shapes=[pltpu.VMEM((4, n, 2 * n), BF16), pltpu.VMEM((n, 2 * n), BF16)],
        compiler_params=SMALL,
    )(pair, *near, *swapped)
    near = [moved(half, along_y(s)) for s in (1, 2, 3)]
    swapped = [moved(value, flip(1)) for value in near]
    flat = pl.pallas_call(
        read_kernel,
        name="read",
        in_specs=[vmem()] * 11,
        out_specs=vmem(),
        out_shape=jax.ShapeDtypeStruct((2, rows, n), BF16),
        scratch_shapes=[pltpu.VMEM((4, n, 2 * n), BF16), pltpu.VMEM((n, n), F32)],
        compiler_params=SMALL,
    )(*near, *swapped, prefix, other, query, local, out_gain.reshape(1, n))
    part = rows // 8
    reads = lax.all_to_all(
        flat.reshape(16, part, n), ("xl", "head"), 0, 0, tiled=True
    ).reshape(2, 8, part, n)
    beside = moved(reads, flip(1))
    piece = jax.ShapeDtypeStruct((part, quarter), BF16)
    kept, to_core, to_half, to_far = pl.pallas_call(
        mix_kernel,
        name="mix",
        in_specs=[vmem()] * 3,
        out_specs=[vmem()] * 4,
        out_shape=[piece] * 4,
        compiler_params=MIDDLE,
    )(reads, beside, columns)
    return pl.pallas_call(
        lay_kernel,
        name="lay",
        in_specs=[vmem()] * 4,
        out_specs=vmem(),
        out_shape=jax.ShapeDtypeStruct((part, 4 * quarter), BF16),
        compiler_params=SMALL,
    )(kept, moved(to_core, flip(1)), moved(to_half, flip(2)), moved(to_far, flip(3)))


def solution(mesh):
    fine = Mesh(mesh.devices.reshape(4, 2, 2, 2, 8), SEQ + ("head",))
    in_specs = (
        P(SEQ, None),
        P(),
        P(None, None, "head"),
        P(None, None, "head"),
        P("head"),
        P("head"),
        P(SEQ),
        P("head"),
        P("head", None),
    )
    out_specs = P(SEQ + ("head",), None)
    return jax.shard_map(
        per_device, mesh=fine, in_specs=in_specs, out_specs=out_specs, check_vma=False
    )
```

```python
import jax
import jax.numpy as jnp
from jax import lax
from jax.experimental import pallas as pl
from jax.experimental.pallas import tpu as pltpu
from jax.sharding import Mesh
from jax.sharding import PartitionSpec as P

F32 = jnp.float32
BF16 = jnp.bfloat16
NN = (((1,), (0,)), ((), ()))
NT = (((1,), (1,)), ((), ()))
TN = (((0,), (0,)), ((), ()))
SEQ = ("y", "xh", "xl", "core")
SMALL = pltpu.CompilerParams(vmem_limit_bytes=8 << 20)
MIDDLE = pltpu.CompilerParams(vmem_limit_bytes=16 << 20)
LARGE = pltpu.CompilerParams(vmem_limit_bytes=60 << 20)


def mm(a, b, dims=NN):
    return lax.dot_general(a, b, dims, preferred_element_type=F32)


def split(a):
    hi = a.astype(BF16)
    return hi, (a - hi.astype(F32)).astype(BF16)


def mm3(a, b, dims=NN):
    (ah, al), (bh, bl) = a, b
    return mm(ah, bh, dims) + (mm(ah, bl, dims) + mm(al, bh, dims))


def unit_rows(vectors):
    return vectors * lax.rsqrt(jnp.sum(vectors * vectors, axis=-1, keepdims=True) + 1e-06)


def norm_rows(x_ref, gain):
    x = x_ref[...].astype(F32)
    rs = lax.rsqrt(jnp.mean(x * x, axis=-1, keepdims=True) + 1e-06)
    return (x * rs * gain).astype(BF16)


def copies(x_hbm, w_hbm, slots, x_buf, w_buf, sems):
    halves = x_buf.shape[0] // 2
    depth = w_buf.shape[1] // 2
    rows = [pl.ds(i * halves, halves) for i in range(2)]
    parts = [pl.ds(i * depth, depth) for i in range(2)]
    found = [(x_hbm.at[part], x_buf.at[part]) for part in rows]
    for slot, j in enumerate(slots):
        found += [(w_hbm.at[j, part], w_buf.at[slot, part]) for part in parts]
    found = [pltpu.make_async_copy(a, b, sems.at[i]) for i, (a, b) in enumerate(found)]
    for copy in found:
        copy.start()
    return found


def normalise(found, x_buf, xn_buf, gain):
    half = x_buf.shape[0] // 2
    for i in range(2):
        found[i].wait()
        part = slice(i * half, (i + 1) * half)
        xn_buf[part] = norm_rows(x_buf.at[part], gain)


def project(found, xn_buf, w_buf, slot):
    depth = w_buf.shape[1] // 2
    total = None
    for i in range(2):
        found[2 + 2 * slot + i].wait()
        part = slice(i * depth, (i + 1) * depth)
        product = mm(xn_buf[:, part], w_buf[slot, part])
        total = product if total is None else total + product
    return total


def fold_kernel(
    scale_ref, rate_ref, x_hbm, gain_ref, w_hbm, gate_ref, resets_ref,
    carry_ref, key_ref, solved_ref, decay_ref, gamma_ref,
    x_buf, xn_buf, w_buf, sems,
):
    found = copies(x_hbm, w_hbm, (1, 2), x_buf, w_buf, sems)
    normalise(found, x_buf, xn_buf, gain_ref[...])
    n = x_buf.shape[0]
    gating = mm(xn_buf[...], gate_ref[...], NT)
    key = unit_rows(project(found, xn_buf, w_buf, 0))
    beta = scale_ref[0] * jax.nn.sigmoid(gating[:, 0:1])
    logf = -rate_ref[0] * jax.nn.softplus(gating[:, 1:2])
    reset_row = resets_ref[...].astype(F32)
    t = lax.broadcasted_iota(jnp.int32, (n, n), 0)
    s = lax.broadcasted_iota(jnp.int32, (n, n), 1)
    causal = t >= s
    eye = t == s

    def to_row(col):
        return jnp.sum(jnp.where(eye, col, 0.0), axis=0, keepdims=True)

    cum = jnp.sum(jnp.where(causal, to_row(logf), 0.0), axis=1, keepdims=True)
    seg = jnp.sum(jnp.where(causal, reset_row, 0.0), axis=1, keepdims=True)
    cum_row = to_row(cum)
    seg_row = to_row(seg)
    same = (seg == seg_row) & causal
    decay = jnp.where(same, jnp.exp(jnp.where(same, cum - cum_row, 0.0)), 0.0)
    gamma = jnp.where(seg == 0.0, jnp.exp(cum), 0.0)
    cum_last, seg_last = cum[n - 1 : n], seg[n - 1 : n]
    tail = jnp.where(seg == seg_last, jnp.exp(cum_last - cum), 0.0)
    gamma_last = gamma[n - 1 : n]
    decay_ref[...] = decay
    gamma_ref[...] = gamma
    key_ref[...] = key

    ks = split(key)
    low = jnp.where(t > s, beta * decay * mm3(ks, ks, NT), 0.0)
    apart = t ^ s
    inv = jnp.where(eye, 1.0, jnp.where(apart == 1, -low, 0.0))
    for level in range(1, n.bit_length() - 1):
        part = jnp.where((apart >> level) == 1, low, 0.0).astype(BF16)
        rough = inv.astype(BF16)
        inv = inv - mm(rough, mm(part, rough).astype(BF16))
    vs = split(inv)
    left = jnp.where(eye, 1.0, 0.0) - inv - mm3(split(low), vs)
    inv = inv + mm(vs[0], left.astype(BF16))

    value = project(found, xn_buf, w_buf, 1)
    rhs = jnp.concatenate([(beta * gamma) * key, beta * value], axis=1)
    solved = mm3(split(inv), split(rhs))
    solved_ref[...] = solved
    folded = mm3(split(key * tail), split(solved), TN)
    carry_ref[:, :n] = (jnp.where(eye, gamma_last, 0.0) - folded[:, :n]).astype(BF16)
    carry_ref[:, n:] = folded[:, n:].astype(BF16)


def look_kernel(
    x_hbm, gain_ref, w_hbm, key_ref, solved_ref, decay_ref, gamma_ref,
    query_ref, local_ref,
    x_buf, xn_buf, w_buf, sems,
):
    found = copies(x_hbm, w_hbm, (0,), x_buf, w_buf, sems)
    normalise(found, x_buf, xn_buf, gain_ref[...])
    n = x_buf.shape[0]
    query = unit_rows(project(found, xn_buf, w_buf, 0))
    scores = mm3(split(query), split(key_ref[...]), NT) * decay_ref[...]
    seen = mm3(split(scores), split(solved_ref[...]))
    query_ref[...] = gamma_ref[...] * query - seen[:, :n]
    local_ref[...] = seen[:, n:]


def after(later, earlier, n):
    both = mm(later[:, :n], earlier)
    return both[:, :n], both[:, n:] + later[:, n:].astype(F32)


def own_half(ref):
    half = ref.shape[0] // 2
    return ref[pl.ds(pl.multiple_of(lax.axis_index("core") * half, half), half)]


def hold(held, place, near_ref, swap_ref):
    half = near_ref.shape[0]
    core = lax.axis_index("core")
    held[place, pl.ds(pl.multiple_of(core * half, half), half)] = near_ref[...]
    held[place, pl.ds(pl.multiple_of((1 - core) * half, half), half)] = swap_ref[...]


def pair_kernel(own_ref, other_ref, out_ref, half_ref):
    n = own_ref.shape[0]
    first = lax.axis_index("core") == 0
    own, other = own_ref[...], other_ref[...]
    earlier = jnp.where(first, own, other)
    later = jnp.where(first, other, own)
    a, b = after(later, earlier, n)
    out_ref[:, :n] = a.astype(BF16)
    out_ref[:, n:] = b.astype(BF16)
    half_ref[...] = own_half(out_ref)


def row_kernel(own_ref, *refs):
    near, swapped, (half_ref, prefix_ref, held, total_ref) = refs[:3], refs[3:6], refs[6:]
    n = own_ref.shape[0]
    place = lax.axis_index("xh") * 2 + lax.axis_index("xl")
    held[place] = own_ref[...]
    for shift, ref, swap in zip((1, 2, 3), near, swapped):
        hold(held, (place + (4 - shift)) % 4, ref, swap)

    def joined(later, earlier):
        a, b = after(later, earlier, n)
        return jnp.concatenate([a, b], axis=1).astype(BF16)

    low = joined(held[1], held[0])
    high = joined(held[3], held[2])
    a, b = after(high, low, n)
    total_ref[:, :n] = a.astype(BF16)
    total_ref[:, n:] = b.astype(BF16)
    half_ref[...] = own_half(total_ref)

    @pl.when(place == 0)
    def _():
        prefix_ref[...] = jnp.zeros_like(prefix_ref)

    @pl.when(place == 1)
    def _():
        prefix_ref[...] = held[0]

    @pl.when(place == 2)
    def _():
        prefix_ref[...] = low

    @pl.when(place == 3)
    def _():
        prefix_ref[...] = joined(held[2], low)


def read_kernel(*refs):
    near, swapped = refs[:3], refs[3:6]
    prefix_ref, other_ref, query_ref, local_ref, gain_ref, out_ref, held, state = refs[6:]
    n = query_ref.shape[0]
    place = lax.axis_index("y")
    for shift, ref, swap in zip((1, 2, 3), near, swapped):
        hold(held, (place + (4 - shift)) % 4, ref, swap)

    def push(pair, value):
        hi, lo = split(value)
        return mm(pair[:, :n], hi) + mm(pair[:, :n], lo) + pair[:, n:].astype(F32)

    @pl.when(place == 0)
    def _():
        state[...] = jnp.zeros_like(state)

    @pl.when(place > 0)
    def _():
        state[...] = held[0, :, n:].astype(F32)

    for turn in (1, 2):
        @pl.when(place > turn)
        def _():
            state[...] = push(held[turn], state[...])

    @pl.when(lax.axis_index("xh") + lax.axis_index("xl") > 0)
    def _():
        state[...] = push(prefix_ref[...], state[...])

    @pl.when(lax.axis_index("core") > 0)
    def _():
        state[...] = push(other_ref[...], state[...])

    read = local_ref[...] + mm3(split(query_ref[...]), split(state[...]))
    read = read * lax.rsqrt(jnp.mean(read * read, axis=-1, keepdims=True) + 1e-06)
    flat = (read * gain_ref[...]).astype(BF16)
    out_ref[0] = flat
    out_ref[1] = flat


def mix_kernel(own_ref, other_ref, weight_ref, *outs):
    half = lax.axis_index("xl")
    rows = own_ref.shape[2]
    for head in range(weight_ref.shape[0]):
        block = [ref[place, head] for place in (half, 1 - half) for ref in (own_ref, other_ref)]
        part = mm(jnp.concatenate(block, axis=0), weight_ref[head])
        total = part if head == 0 else total + part
    total = total.astype(BF16)
    for k, ref in enumerate(outs):
        ref[...] = total[k * rows : (k + 1) * rows]


def lay_kernel(mine_ref, core_ref, half_ref, far_ref, out_ref):
    width = mine_ref.shape[1]
    block = lax.axis_index("core") * 2 + lax.axis_index("xl")
    for flip, ref in ((0, mine_ref), (2, core_ref), (1, half_ref), (3, far_ref)):
        place = pl.multiple_of((block ^ flip) * width, width)
        out_ref[:, pl.ds(place, width)] = ref[...]


def hbm():
    return pl.BlockSpec(memory_space=pltpu.HBM)


def vmem():
    return pl.BlockSpec(memory_space=pltpu.VMEM)


def per_device(
    frames, norm_gain, qkv_weight, gate_weight, beta_scale, decay_rate, resets, out_gain, out_weight
):
    rows, width = frames.shape
    n = qkv_weight.shape[2]
    weight = qkv_weight.transpose(1, 0, 2)
    gate = gate_weight.transpose(2, 1, 0).reshape(2, width)
    square = jax.ShapeDtypeStruct((rows, n), F32)
    gain = norm_gain.reshape(1, width)

    def buffers(matrices):
        return [
            pltpu.VMEM((rows, width), BF16),
            pltpu.VMEM((rows, width), BF16),
            pltpu.VMEM((matrices, width, n), BF16),
            pltpu.SemaphoreType.DMA((2 + 2 * matrices,)),
        ]

    scalar = pl.BlockSpec(memory_space=pltpu.SMEM)
    carry, key, solved, decay, gamma = pl.pallas_call(
        fold_kernel,
        name="fold",
        in_specs=[scalar, scalar, hbm(), vmem(), hbm(), vmem(), vmem()],
        out_specs=[vmem()] * 5,
        out_shape=[
            jax.ShapeDtypeStruct((n, 2 * n), BF16),
            square,
            jax.ShapeDtypeStruct((rows, 2 * n), F32),
            square,
            jax.ShapeDtypeStruct((rows, 1), F32),
        ],
        scratch_shapes=buffers(2),
        compiler_params=LARGE,
    )(beta_scale, decay_rate, frames, gain, weight, gate, resets.reshape(1, rows))

    def look():
        return pl.pallas_call(
            look_kernel,
            name="look",
            in_specs=[hbm(), vmem(), hbm()] + [vmem()] * 4,
            out_specs=[vmem()] * 2,
            out_shape=[square] * 2,
            scratch_shapes=buffers(1),
            compiler_params=MIDDLE,
            cost_estimate=pl.CostEstimate(
                flops=4 * rows * width * n, bytes_accessed=16 << 20, transcendentals=0
            ),
        )(frames, gain, weight, key, solved, decay, gamma)

    count = 32

    def moved(value, place_of):
        return lax.ppermute(value, SEQ, [(i, place_of(i)) for i in range(count)])

    def along_x(shift):
        return lambda i: (i // 8) * 8 + (i + 2 * shift) % 8

    def along_y(shift):
        return lambda i: (i + 8 * shift) % 32

    def flip(bits):
        return lambda i: i ^ bits

    quarter = out_weight.shape[1] // 4
    block = lax.axis_index("core") * 2 + lax.axis_index("xl")
    mine = lax.dynamic_slice_in_dim(out_weight, block * quarter, quarter, 1)
    columns = lax.all_gather(mine, "head", tiled=False)

    pair_shape = jax.ShapeDtypeStruct((n, 2 * n), BF16)
    half_shape = jax.ShapeDtypeStruct((n // 2, 2 * n), BF16)
    other = moved(carry, flip(1))
    pair, half = pl.pallas_call(
        pair_kernel,
        name="pair",
        in_specs=[vmem()] * 2,
        out_specs=[vmem()] * 2,
        out_shape=[pair_shape, half_shape],
        compiler_params=SMALL,
    )(carry, other)
    near = [moved(half, along_x(s)) for s in (1, 2, 3)]
    query, local = look()
    swapped = [moved(value, flip(1)) for value in near]
    half, prefix = pl.pallas_call(
        row_kernel,
        name="row",
        in_specs=[vmem()] * 7,
        out_specs=[vmem()] * 2,
        out_shape=[half_shape, pair_shape],
        scratch_shapes=[pltpu.VMEM((4, n, 2 * n), BF16), pltpu.VMEM((n, 2 * n), BF16)],
        compiler_params=SMALL,
    )(pair, *near, *swapped)
    near = [moved(half, along_y(s)) for s in (1, 2, 3)]
    swapped = [moved(value, flip(1)) for value in near]
    flat = pl.pallas_call(
        read_kernel,
        name="read",
        in_specs=[vmem()] * 11,
        out_specs=vmem(),
        out_shape=jax.ShapeDtypeStruct((2, rows, n), BF16),
        scratch_shapes=[pltpu.VMEM((4, n, 2 * n), BF16), pltpu.VMEM((n, n), F32)],
        compiler_params=SMALL,
    )(*near, *swapped, prefix, other, query, local, out_gain.reshape(1, n))
    part = rows // 8
    reads = lax.all_to_all(
        flat.reshape(16, part, n), ("xl", "head"), 0, 0, tiled=True
    ).reshape(2, 8, part, n)
    beside = moved(reads, flip(1))
    piece = jax.ShapeDtypeStruct((part, quarter), BF16)
    kept, to_core, to_half, to_far = pl.pallas_call(
        mix_kernel,
        name="mix",
        in_specs=[vmem()] * 3,
        out_specs=[vmem()] * 4,
        out_shape=[piece] * 4,
        compiler_params=MIDDLE,
    )(reads, beside, columns)
    return pl.pallas_call(
        lay_kernel,
        name="lay",
        in_specs=[vmem()] * 4,
        out_specs=vmem(),
        out_shape=jax.ShapeDtypeStruct((part, 4 * quarter), BF16),
        compiler_params=SMALL,
    )(kept, moved(to_core, flip(1)), moved(to_half, flip(2)), moved(to_far, flip(3)))


def solution(mesh):
    fine = Mesh(mesh.devices.reshape(4, 2, 2, 2, 8), SEQ + ("head",))
    in_specs = (
        P(SEQ, None),
        P(),
        P(None, None, "head"),
        P(None, None, "head"),
        P("head"),
        P("head"),
        P(SEQ),
        P("head"),
        P("head", None),
    )
    out_specs = P(SEQ + ("head",), None)
    return jax.shard_map(
        per_device, mesh=fine, in_specs=in_specs, out_specs=out_specs, check_vma=False
    )
```

```python
import jax
import jax.numpy as jnp
from jax import lax
from jax.experimental import pallas as pl
from jax.experimental.pallas import tpu as pltpu
from jax.sharding import Mesh
from jax.sharding import PartitionSpec as P

F32 = jnp.float32
BF16 = jnp.bfloat16
NN = (((1,), (0,)), ((), ()))
NT = (((1,), (1,)), ((), ()))
TN = (((0,), (0,)), ((), ()))
SEQ = ("y", "xh", "xl", "core")
SMALL = pltpu.CompilerParams(vmem_limit_bytes=8 << 20)
MIDDLE = pltpu.CompilerParams(vmem_limit_bytes=16 << 20)
LARGE = pltpu.CompilerParams(vmem_limit_bytes=60 << 20)


def mm(a, b, dims=NN):
    return lax.dot_general(a, b, dims, preferred_element_type=F32)


def split(a):
    hi = a.astype(BF16)
    return hi, (a - hi.astype(F32)).astype(BF16)


def mm3(a, b, dims=NN):
    (ah, al), (bh, bl) = a, b
    return mm(ah, bh, dims) + (mm(ah, bl, dims) + mm(al, bh, dims))


def unit_rows(vectors):
    return vectors * lax.rsqrt(jnp.sum(vectors * vectors, axis=-1, keepdims=True) + 1e-06)


def norm_rows(x_ref, gain):
    x = x_ref[...].astype(F32)
    rs = lax.rsqrt(jnp.mean(x * x, axis=-1, keepdims=True) + 1e-06)
    return (x * rs * gain).astype(BF16)


def copies(x_hbm, w_hbm, slots, x_buf, w_buf, sems):
    halves = x_buf.shape[0] // 2
    depth = w_buf.shape[1] // 2
    rows = [pl.ds(i * halves, halves) for i in range(2)]
    parts = [pl.ds(i * depth, depth) for i in range(2)]
    found = [(x_hbm.at[part], x_buf.at[part]) for part in rows]
    for slot, j in enumerate(slots):
        found += [(w_hbm.at[j, part], w_buf.at[slot, part]) for part in parts]
    found = [pltpu.make_async_copy(a, b, sems.at[i]) for i, (a, b) in enumerate(found)]
    for copy in found:
        copy.start()
    return found


def normalise(found, x_buf, xn_buf, gain):
    half = x_buf.shape[0] // 2
    for i in range(2):
        found[i].wait()
        part = slice(i * half, (i + 1) * half)
        xn_buf[part] = norm_rows(x_buf.at[part], gain)


def project(found, xn_buf, w_buf, slot):
    depth = w_buf.shape[1] // 2
    total = None
    for i in range(2):
        found[2 + 2 * slot + i].wait()
        part = slice(i * depth, (i + 1) * depth)
        product = mm(xn_buf[:, part], w_buf[slot, part])
        total = product if total is None else total + product
    return total


def fold_kernel(
    scale_hbm, rate_hbm, x_hbm, gain_ref, w_hbm, gate_ref, resets_ref,
    carry_ref, key_ref, solved_ref, decay_ref, gamma_ref,
    x_buf, xn_buf, w_buf, sems, scale_ref, rate_ref, scalar_sems,
):
    scalars = [
        pltpu.make_async_copy(a, b, scalar_sems.at[i])
        for i, (a, b) in enumerate(((scale_hbm, scale_ref), (rate_hbm, rate_ref)))
    ]
    for copy in scalars:
        copy.start()
    found = copies(x_hbm, w_hbm, (1, 2), x_buf, w_buf, sems)
    normalise(found, x_buf, xn_buf, gain_ref[...])
    n = x_buf.shape[0]
    gating = mm(xn_buf[...], gate_ref[...], NT)
    key = unit_rows(project(found, xn_buf, w_buf, 0))
    for copy in scalars:
        copy.wait()
    beta = scale_ref[0] * jax.nn.sigmoid(gating[:, 0:1])
    logf = -rate_ref[0] * jax.nn.softplus(gating[:, 1:2])
    reset_row = resets_ref[...].astype(F32)
    t = lax.broadcasted_iota(jnp.int32, (n, n), 0)
    s = lax.broadcasted_iota(jnp.int32, (n, n), 1)
    causal = t >= s
    eye = t == s

    def to_row(col):
        return jnp.sum(jnp.where(eye, col, 0.0), axis=0, keepdims=True)

    cum = jnp.sum(jnp.where(causal, to_row(logf), 0.0), axis=1, keepdims=True)
    seg = jnp.sum(jnp.where(causal, reset_row, 0.0), axis=1, keepdims=True)
    cum_row = to_row(cum)
    seg_row = to_row(seg)
    same = (seg == seg_row) & causal
    decay = jnp.where(same, jnp.exp(jnp.where(same, cum - cum_row, 0.0)), 0.0)
    gamma = jnp.where(seg == 0.0, jnp.exp(cum), 0.0)
    cum_last, seg_last = cum[n - 1 : n], seg[n - 1 : n]
    tail = jnp.where(seg == seg_last, jnp.exp(cum_last - cum), 0.0)
    gamma_last = gamma[n - 1 : n]
    decay_ref[...] = decay
    gamma_ref[...] = gamma
    key_ref[...] = key

    ks = split(key)
    low = jnp.where(t > s, beta * decay * mm3(ks, ks, NT), 0.0)
    apart = t ^ s
    inv = jnp.where(eye, 1.0, jnp.where(apart == 1, -low, 0.0))
    for level in range(1, n.bit_length() - 1):
        part = jnp.where((apart >> level) == 1, low, 0.0).astype(BF16)
        rough = inv.astype(BF16)
        inv = inv - mm(rough, mm(part, rough).astype(BF16))
    vs = split(inv)
    left = jnp.where(eye, 1.0, 0.0) - inv - mm3(split(low), vs)
    inv = inv + mm(vs[0], left.astype(BF16))

    value = project(found, xn_buf, w_buf, 1)
    rhs = jnp.concatenate([(beta * gamma) * key, beta * value], axis=1)
    solved = mm3(split(inv), split(rhs))
    solved_ref[...] = solved
    folded = mm3(split(key * tail), split(solved), TN)
    carry_ref[:, :n] = (jnp.where(eye, gamma_last, 0.0) - folded[:, :n]).astype(BF16)
    carry_ref[:, n:] = folded[:, n:].astype(BF16)


def look_kernel(
    x_hbm, gain_ref, w_hbm, key_ref, solved_ref, decay_ref, gamma_ref,
    query_ref, local_ref,
    x_buf, xn_buf, w_buf, sems,
):
    found = copies(x_hbm, w_hbm, (0,), x_buf, w_buf, sems)
    normalise(found, x_buf, xn_buf, gain_ref[...])
    n = x_buf.shape[0]
    query = unit_rows(project(found, xn_buf, w_buf, 0))
    scores = mm3(split(query), split(key_ref[...]), NT) * decay_ref[...]
    seen = mm3(split(scores), split(solved_ref[...]))
    query_ref[...] = gamma_ref[...] * query - seen[:, :n]
    local_ref[...] = seen[:, n:]


def after(later, earlier, n):
    both = mm(later[:, :n], earlier)
    return both[:, :n], both[:, n:] + later[:, n:].astype(F32)


def own_half(ref):
    half = ref.shape[0] // 2
    return ref[pl.ds(pl.multiple_of(lax.axis_index("core") * half, half), half)]


def hold(held, place, near_ref, swap_ref):
    half = near_ref.shape[0]
    core = lax.axis_index("core")
    held[place, pl.ds(pl.multiple_of(core * half, half), half)] = near_ref[...]
    held[place, pl.ds(pl.multiple_of((1 - core) * half, half), half)] = swap_ref[...]


def pair_kernel(own_ref, other_ref, out_ref, half_ref):
    n = own_ref.shape[0]
    first = lax.axis_index("core") == 0
    own, other = own_ref[...], other_ref[...]
    earlier = jnp.where(first, own, other)
    later = jnp.where(first, other, own)
    a, b = after(later, earlier, n)
    out_ref[:, :n] = a.astype(BF16)
    out_ref[:, n:] = b.astype(BF16)
    half_ref[...] = own_half(out_ref)


def row_kernel(own_ref, *refs):
    near, swapped, (half_ref, prefix_ref, held, total_ref) = refs[:3], refs[3:6], refs[6:]
    n = own_ref.shape[0]
    place = lax.axis_index("xh") * 2 + lax.axis_index("xl")
    held[place] = own_ref[...]
    for shift, ref, swap in zip((1, 2, 3), near, swapped):
        hold(held, (place + (4 - shift)) % 4, ref, swap)

    def joined(later, earlier):
        a, b = after(later, earlier, n)
        return jnp.concatenate([a, b], axis=1).astype(BF16)

    low = joined(held[1], held[0])
    high = joined(held[3], held[2])
    a, b = after(high, low, n)
    total_ref[:, :n] = a.astype(BF16)
    total_ref[:, n:] = b.astype(BF16)
    half_ref[...] = own_half(total_ref)

    @pl.when(place == 0)
    def _():
        prefix_ref[...] = jnp.zeros_like(prefix_ref)

    @pl.when(place == 1)
    def _():
        prefix_ref[...] = held[0]

    @pl.when(place == 2)
    def _():
        prefix_ref[...] = low

    @pl.when(place == 3)
    def _():
        prefix_ref[...] = joined(held[2], low)


def read_kernel(*refs):
    near, swapped = refs[:3], refs[3:6]
    prefix_ref, other_ref, query_ref, local_ref, gain_ref, out_ref, held, state = refs[6:]
    n = query_ref.shape[0]
    place = lax.axis_index("y")
    for shift, ref, swap in zip((1, 2, 3), near, swapped):
        hold(held, (place + (4 - shift)) % 4, ref, swap)

    def push(pair, value):
        hi, lo = split(value)
        return mm(pair[:, :n], hi) + mm(pair[:, :n], lo) + pair[:, n:].astype(F32)

    @pl.when(place == 0)
    def _():
        state[...] = jnp.zeros_like(state)

    @pl.when(place > 0)
    def _():
        state[...] = held[0, :, n:].astype(F32)

    for turn in (1, 2):
        @pl.when(place > turn)
        def _():
            state[...] = push(held[turn], state[...])

    @pl.when(lax.axis_index("xh") + lax.axis_index("xl") > 0)
    def _():
        state[...] = push(prefix_ref[...], state[...])

    @pl.when(lax.axis_index("core") > 0)
    def _():
        state[...] = push(other_ref[...], state[...])

    read = local_ref[...] + mm3(split(query_ref[...]), split(state[...]))
    read = read * lax.rsqrt(jnp.mean(read * read, axis=-1, keepdims=True) + 1e-06)
    flat = (read * gain_ref[...]).astype(BF16)
    out_ref[0] = flat
    out_ref[1] = flat


def take_kernel(whole_ref, out_ref):
    out_ref[...] = whole_ref[...]


def mix_kernel(
    own_ref, other_ref, mine_ref, one_ref, two_ref, three_ref, four_ref, keep_ref, send_ref, total
):
    core, half, head = lax.axis_index("core"), lax.axis_index("xl"), lax.axis_index("head")
    kept = keep_ref.shape[0]
    width = four_ref.shape[1]

    def rows(steps):
        source = (head + (2 * core - 1) * steps + 8) % 8
        block = [ref[place, source] for ref in (own_ref, other_ref) for place in (half, 1 - half)]
        return jnp.concatenate(block, axis=0)

    total[...] = mm(rows(1), one_ref[...]) + mm(rows(2), two_ref[...]) + mm(rows(3), three_ref[...])

    @pl.when(core == 0)
    def _():
        total[...] = total[...] + mm(rows(0), mine_ref[...])

    part = pl.ds(pl.multiple_of(core * width, width), width)
    total[:, part] = total[:, part] + mm(rows(4), four_ref[...])
    keep_ref[...] = total[:kept]
    send_ref[...] = total[kept:].astype(BF16)


def add_kernel(keep_ref, come_ref, mine_ref, send_ref):
    total = (keep_ref[...] + come_ref[...].astype(F32)).astype(BF16)
    rows = mine_ref.shape[0]
    mine_ref[...] = total[:rows]
    send_ref[...] = total[rows:]


def lay_kernel(mine_ref, come_ref, out_ref):
    width = mine_ref.shape[1]
    half = lax.axis_index("xl")
    out_ref[:, pl.ds(pl.multiple_of(half * width, width), width)] = mine_ref[...]
    out_ref[:, pl.ds(pl.multiple_of((1 - half) * width, width), width)] = come_ref[...]


def hbm():
    return pl.BlockSpec(memory_space=pltpu.HBM)


def vmem():
    return pl.BlockSpec(memory_space=pltpu.VMEM)


def per_device(
    frames, norm_gain, qkv_weight, gate_weight, beta_scale, decay_rate, resets, out_gain, out_weight
):
    rows, width = frames.shape
    n = qkv_weight.shape[2]
    weight = qkv_weight.transpose(1, 0, 2)
    gate = gate_weight.transpose(2, 1, 0).reshape(2, width)
    square = jax.ShapeDtypeStruct((rows, n), F32)
    gain = norm_gain.reshape(1, width)

    def buffers(matrices):
        return [
            pltpu.VMEM((rows, width), BF16),
            pltpu.VMEM((rows, width), BF16),
            pltpu.VMEM((matrices, width, n), BF16),
            pltpu.SemaphoreType.DMA((2 + 2 * matrices,)),
        ]

    carry, key, solved, decay, gamma = pl.pallas_call(
        fold_kernel,
        name="fold",
        in_specs=[hbm(), hbm(), hbm(), vmem(), hbm(), vmem(), vmem()],
        out_specs=[vmem()] * 5,
        out_shape=[
            jax.ShapeDtypeStruct((n, 2 * n), BF16),
            square,
            jax.ShapeDtypeStruct((rows, 2 * n), F32),
            square,
            jax.ShapeDtypeStruct((rows, 1), F32),
        ],
        scratch_shapes=buffers(2)
        + [pltpu.SMEM((1,), F32), pltpu.SMEM((1,), F32), pltpu.SemaphoreType.DMA((2,))],
        compiler_params=LARGE,
    )(beta_scale, decay_rate, frames, gain, weight, gate, resets.reshape(1, rows))

    def look():
        return pl.pallas_call(
            look_kernel,
            name="look",
            in_specs=[hbm(), vmem(), hbm()] + [vmem()] * 4,
            out_specs=[vmem()] * 2,
            out_shape=[square] * 2,
            scratch_shapes=buffers(1),
            compiler_params=LARGE,
            cost_estimate=pl.CostEstimate(
                flops=4 * rows * width * n, bytes_accessed=16 << 20, transcendentals=0
            ),
        )(frames, gain, weight, key, solved, decay, gamma)

    count = 32

    def moved(value, place_of):
        return lax.ppermute(value, SEQ, [(i, place_of(i)) for i in range(count)])

    def along_x(shift):
        return lambda i: (i // 8) * 8 + (i + 2 * shift) % 8

    def along_y(shift):
        return lambda i: (i + 8 * shift) % 32

    def flip(bits):
        return lambda i: i ^ bits

    def around(value):
        up = [(z, (z + 1) % 8) for z in range(8)]
        down = [(8 + z, 8 + (z + 7) % 8) for z in range(8)]
        return lax.ppermute(value, ("core", "head"), up + down)

    def later(value, gate):
        return lax.optimization_barrier((value, gate))[0]

    wide = out_weight.shape[1] // 2
    mine = pl.pallas_call(
        take_kernel,
        name="take",
        grid=(4,),
        in_specs=[pl.BlockSpec((n // 4, wide), lambda i: (i, lax.axis_index("xl")))],
        out_specs=pl.BlockSpec((n // 4, wide), lambda i: (i, 0)),
        out_shape=jax.ShapeDtypeStruct((n, wide), BF16),
        compiler_params=LARGE,
    )(out_weight)
    one = around(mine)

    pair_shape = jax.ShapeDtypeStruct((n, 2 * n), BF16)
    half_shape = jax.ShapeDtypeStruct((n // 2, 2 * n), BF16)
    other = moved(carry, flip(1))
    pair, half = pl.pallas_call(
        pair_kernel,
        name="pair",
        in_specs=[vmem()] * 2,
        out_specs=[vmem()] * 2,
        out_shape=[pair_shape, half_shape],
        compiler_params=SMALL,
    )(carry, other)
    two = around(later(one, half))
    near = [moved(half, along_x(s)) for s in (1, 2, 3)]
    near, (query, local) = lax.optimization_barrier((near, look()))
    swapped = [moved(value, flip(1)) for value in near]
    half, prefix = pl.pallas_call(
        row_kernel,
        name="row",
        in_specs=[vmem()] * 7,
        out_specs=[vmem()] * 2,
        out_shape=[half_shape, pair_shape],
        scratch_shapes=[pltpu.VMEM((4, n, 2 * n), BF16), pltpu.VMEM((n, 2 * n), BF16)],
        compiler_params=SMALL,
    )(pair, *near, *swapped)
    three = around(later(two, half))
    near = [moved(half, along_y(s)) for s in (1, 2, 3)]
    swapped = [moved(value, flip(1)) for value in near]
    flat = pl.pallas_call(
        read_kernel,
        name="read",
        in_specs=[vmem()] * 11,
        out_specs=vmem(),
        out_shape=jax.ShapeDtypeStruct((2, rows, n), BF16),
        scratch_shapes=[pltpu.VMEM((4, n, 2 * n), BF16), pltpu.VMEM((n, n), F32)],
        compiler_params=SMALL,
    )(*near, *swapped, prefix, other, query, local, out_gain.reshape(1, n))
    part = rows // 8
    flat, three = lax.optimization_barrier((flat, three))
    four = around(
        lax.dynamic_slice_in_dim(three, lax.axis_index("core") * (wide // 2), wide // 2, 1)
    )
    reads = lax.all_to_all(
        flat.reshape(16, part, n), ("xl", "head"), 0, 0, tiled=True
    ).reshape(2, 8, part, n)
    beside = moved(reads, flip(1))
    keep, send = pl.pallas_call(
        mix_kernel,
        name="mix",
        in_specs=[vmem()] * 7,
        out_specs=[vmem()] * 2,
        out_shape=[
            jax.ShapeDtypeStruct((2 * part, wide), F32),
            jax.ShapeDtypeStruct((2 * part, wide), BF16),
        ],
        scratch_shapes=[pltpu.VMEM((4 * part, wide), F32)],
        compiler_params=MIDDLE,
    )(reads, beside, mine, one, two, three, four)
    piece = jax.ShapeDtypeStruct((part, wide), BF16)
    kept, send = pl.pallas_call(
        add_kernel,
        name="add",
        in_specs=[vmem()] * 2,
        out_specs=[vmem()] * 2,
        out_shape=[piece] * 2,
        compiler_params=SMALL,
    )(keep, moved(send, flip(1)))
    return pl.pallas_call(
        lay_kernel,
        name="lay",
        in_specs=[vmem()] * 2,
        out_specs=vmem(),
        out_shape=jax.ShapeDtypeStruct((part, 2 * wide), BF16),
        compiler_params=SMALL,
    )(kept, moved(send, flip(2)))


def solution(mesh):
    fine = Mesh(mesh.devices.reshape(4, 2, 2, 2, 8), SEQ + ("head",))
    in_specs = (
        P(SEQ, None),
        P(),
        P(None, None, "head"),
        P(None, None, "head"),
        P("head"),
        P("head"),
        P(SEQ),
        P("head"),
        P("head", None),
    )
    out_specs = P(SEQ + ("head",), None)
    return jax.shard_map(
        per_device, mesh=fine, in_specs=in_specs, out_specs=out_specs, check_vma=False
    )
```

```python
import jax
import jax.numpy as jnp
from jax import lax
from jax.experimental import pallas as pl
from jax.experimental.pallas import tpu as pltpu
from jax.sharding import Mesh
from jax.sharding import PartitionSpec as P

F32 = jnp.float32
BF16 = jnp.bfloat16
NN = (((1,), (0,)), ((), ()))
NT = (((1,), (1,)), ((), ()))
TN = (((0,), (0,)), ((), ()))
SEQ = ("y", "xh", "xl", "core")
SMALL = pltpu.CompilerParams(vmem_limit_bytes=8 << 20)
MIDDLE = pltpu.CompilerParams(vmem_limit_bytes=16 << 20)
LARGE = pltpu.CompilerParams(vmem_limit_bytes=58 << 20)


def mm(a, b, dims=NN):
    return lax.dot_general(a, b, dims, preferred_element_type=F32)


def split(a):
    hi = a.astype(BF16)
    return hi, (a - hi.astype(F32)).astype(BF16)


def mm3(a, b, dims=NN):
    (ah, al), (bh, bl) = a, b
    return mm(ah, bh, dims) + (mm(ah, bl, dims) + mm(al, bh, dims))


def unit_rows(vectors):
    return vectors * lax.rsqrt(jnp.sum(vectors * vectors, axis=-1, keepdims=True) + 1e-06)


def norm_rows(x_ref, gain):
    x = x_ref[...].astype(F32)
    rs = lax.rsqrt(jnp.mean(x * x, axis=-1, keepdims=True) + 1e-06)
    return (x * rs * gain).astype(BF16)


def copies(x_hbm, w_hbm, slots, x_buf, w_buf, sems):
    halves = x_buf.shape[0] // 2
    depth = w_buf.shape[1] // 2
    rows = [pl.ds(i * halves, halves) for i in range(2)]
    parts = [pl.ds(i * depth, depth) for i in range(2)]
    found = [(x_hbm.at[part], x_buf.at[part]) for part in rows]
    for slot, j in enumerate(slots):
        found += [(w_hbm.at[j, part], w_buf.at[slot, part]) for part in parts]
    found = [pltpu.make_async_copy(a, b, sems.at[i]) for i, (a, b) in enumerate(found)]
    for copy in found:
        copy.start()
    return found


def normalise(found, x_buf, xn_buf, gain):
    half = x_buf.shape[0] // 2
    for i in range(2):
        found[i].wait()
        part = slice(i * half, (i + 1) * half)
        xn_buf[part] = norm_rows(x_buf.at[part], gain)


def project(found, xn_buf, w_buf, slot):
    depth = w_buf.shape[1] // 2
    total = None
    for i in range(2):
        found[2 + 2 * slot + i].wait()
        part = slice(i * depth, (i + 1) * depth)
        product = mm(xn_buf[:, part], w_buf[slot, part])
        total = product if total is None else total + product
    return total


def fold_kernel(
    scale_hbm, rate_hbm, x_hbm, gain_ref, w_hbm, gate_ref, resets_ref,
    carry_ref, key_ref, solved_ref, decay_ref, gamma_ref,
    x_buf, xn_buf, w_buf, sems, scale_ref, rate_ref, scalar_sems,
):
    scalars = [
        pltpu.make_async_copy(a, b, scalar_sems.at[i])
        for i, (a, b) in enumerate(((scale_hbm, scale_ref), (rate_hbm, rate_ref)))
    ]
    for copy in scalars:
        copy.start()
    found = copies(x_hbm, w_hbm, (1, 2), x_buf, w_buf, sems)
    normalise(found, x_buf, xn_buf, gain_ref[...])
    n = x_buf.shape[0]
    gating = mm(xn_buf[...], gate_ref[...], NT)
    key = unit_rows(project(found, xn_buf, w_buf, 0))
    for copy in scalars:
        copy.wait()
    beta = scale_ref[0] * jax.nn.sigmoid(gating[:, 0:1])
    logf = -rate_ref[0] * jax.nn.softplus(gating[:, 1:2])
    reset_row = resets_ref[...].astype(F32)
    t = lax.broadcasted_iota(jnp.int32, (n, n), 0)
    s = lax.broadcasted_iota(jnp.int32, (n, n), 1)
    causal = t >= s
    eye = t == s

    def to_row(col):
        return jnp.sum(jnp.where(eye, col, 0.0), axis=0, keepdims=True)

    cum = jnp.sum(jnp.where(causal, to_row(logf), 0.0), axis=1, keepdims=True)
    seg = jnp.sum(jnp.where(causal, reset_row, 0.0), axis=1, keepdims=True)
    cum_row = to_row(cum)
    seg_row = to_row(seg)
    same = (seg == seg_row) & causal
    decay = jnp.where(same, jnp.exp(jnp.where(same, cum - cum_row, 0.0)), 0.0)
    gamma = jnp.where(seg == 0.0, jnp.exp(cum), 0.0)
    cum_last, seg_last = cum[n - 1 : n], seg[n - 1 : n]
    tail = jnp.where(seg == seg_last, jnp.exp(cum_last - cum), 0.0)
    gamma_last = gamma[n - 1 : n]
    decay_ref[...] = decay
    gamma_ref[...] = gamma
    key_ref[...] = key

    ks = split(key)
    low = jnp.where(t > s, beta * decay * mm3(ks, ks, NT), 0.0)
    apart = t ^ s
    inv = jnp.where(eye, 1.0, jnp.where(apart == 1, -low, 0.0))
    for level in range(1, n.bit_length() - 1):
        part = jnp.where((apart >> level) == 1, low, 0.0).astype(BF16)
        rough = inv.astype(BF16)
        inv = inv - mm(rough, mm(part, rough).astype(BF16))
    vs = split(inv)
    left = jnp.where(eye, 1.0, 0.0) - inv - mm3(split(low), vs)
    inv = inv + mm(vs[0], left.astype(BF16))

    value = project(found, xn_buf, w_buf, 1)
    rhs = jnp.concatenate([(beta * gamma) * key, beta * value], axis=1)
    solved = mm3(split(inv), split(rhs))
    solved_ref[...] = solved
    folded = mm3(split(key * tail), split(solved), TN)
    carry_ref[:, :n] = (jnp.where(eye, gamma_last, 0.0) - folded[:, :n]).astype(BF16)
    carry_ref[:, n:] = folded[:, n:].astype(BF16)


def look_kernel(
    x_hbm, gain_ref, w_hbm, key_ref, solved_ref, decay_ref, gamma_ref,
    out_ref,
    x_buf, xn_buf, w_buf, sems,
):
    found = copies(x_hbm, w_hbm, (0,), x_buf, w_buf, sems)
    normalise(found, x_buf, xn_buf, gain_ref[...])
    n = x_buf.shape[0]
    query = unit_rows(project(found, xn_buf, w_buf, 0))
    scores = mm3(split(query), split(key_ref[...]), NT) * decay_ref[...]
    seen = mm3(split(scores), split(solved_ref[...]))
    out_ref[:, :n] = gamma_ref[...] * query - seen[:, :n]
    out_ref[:, n:] = seen[:, n:]


def after(later, earlier, n):
    both = mm(later[:, :n], earlier)
    return both[:, :n], both[:, n:] + later[:, n:].astype(F32)


def own_half(ref):
    half = ref.shape[0] // 2
    return ref[pl.ds(pl.multiple_of(lax.axis_index("core") * half, half), half)]


def hold(held, place, near_ref, swap_ref):
    half = near_ref.shape[0]
    core = lax.axis_index("core")
    held[place, pl.ds(pl.multiple_of(core * half, half), half)] = near_ref[...]
    held[place, pl.ds(pl.multiple_of((1 - core) * half, half), half)] = swap_ref[...]


def pair_kernel(own_ref, other_ref, out_ref, half_ref):
    n = own_ref.shape[0]
    first = lax.axis_index("core") == 0
    own, other = own_ref[...], other_ref[...]
    earlier = jnp.where(first, own, other)
    later = jnp.where(first, other, own)
    a, b = after(later, earlier, n)
    out_ref[:, :n] = a.astype(BF16)
    out_ref[:, n:] = b.astype(BF16)
    half_ref[...] = own_half(out_ref)


def row_kernel(own_ref, *refs):
    near, swapped, (half_ref, prefix_ref, held, total_ref) = refs[:3], refs[3:6], refs[6:]
    n = own_ref.shape[0]
    place = lax.axis_index("xh") * 2 + lax.axis_index("xl")
    held[place] = own_ref[...]
    for shift, ref, swap in zip((1, 2, 3), near, swapped):
        hold(held, (place + (4 - shift)) % 4, ref, swap)

    def joined(later, earlier):
        a, b = after(later, earlier, n)
        return jnp.concatenate([a, b], axis=1).astype(BF16)

    low = joined(held[1], held[0])
    high = joined(held[3], held[2])
    a, b = after(high, low, n)
    total_ref[:, :n] = a.astype(BF16)
    total_ref[:, n:] = b.astype(BF16)
    half_ref[...] = own_half(total_ref)

    @pl.when(place == 0)
    def _():
        prefix_ref[...] = jnp.zeros_like(prefix_ref)

    @pl.when(place == 1)
    def _():
        prefix_ref[...] = held[0]

    @pl.when(place == 2)
    def _():
        prefix_ref[...] = low

    @pl.when(place == 3)
    def _():
        prefix_ref[...] = joined(held[2], low)


def read_kernel(*refs):
    near, swapped = refs[:3], refs[3:6]
    prefix_ref, other_ref, look_ref, gain_ref, out_ref, held, state = refs[6:]
    n = look_ref.shape[0]
    place = lax.axis_index("y")
    for shift, ref, swap in zip((1, 2, 3), near, swapped):
        hold(held, (place + (4 - shift)) % 4, ref, swap)

    def push(pair, value):
        hi, lo = split(value)
        return mm(pair[:, :n], hi) + mm(pair[:, :n], lo) + pair[:, n:].astype(F32)

    @pl.when(place == 0)
    def _():
        state[...] = jnp.zeros_like(state)

    @pl.when(place > 0)
    def _():
        state[...] = held[0, :, n:].astype(F32)

    for turn in (1, 2):
        @pl.when(place > turn)
        def _():
            state[...] = push(held[turn], state[...])

    @pl.when(lax.axis_index("xh") + lax.axis_index("xl") > 0)
    def _():
        state[...] = push(prefix_ref[...], state[...])

    @pl.when(lax.axis_index("core") > 0)
    def _():
        state[...] = push(other_ref[...], state[...])

    read = look_ref[:, n:] + mm3(split(look_ref[:, :n]), split(state[...]))
    read = read * lax.rsqrt(jnp.mean(read * read, axis=-1, keepdims=True) + 1e-06)
    flat = (read * gain_ref[...]).astype(BF16)
    out_ref[0] = flat
    out_ref[1] = flat


def take_kernel(whole_ref, out_ref, sem):
    width = out_ref.shape[1]
    columns = pl.ds(pl.multiple_of(lax.axis_index("xl") * width, width), width)
    copy = pltpu.make_async_copy(whole_ref.at[:, columns], out_ref, sem)
    copy.start()
    copy.wait()


def mix_kernel(
    own_ref, other_ref, mine_ref, one_ref, two_ref, three_ref, four_ref, keep_ref, send_ref, total
):
    core, half, head = lax.axis_index("core"), lax.axis_index("xl"), lax.axis_index("head")
    kept = keep_ref.shape[0]
    width = four_ref.shape[1]

    def rows(steps):
        source = (head + (2 * core - 1) * steps + 8) % 8
        block = [ref[place, source] for ref in (own_ref, other_ref) for place in (half, 1 - half)]
        return jnp.concatenate(block, axis=0)

    total[...] = mm(rows(1), one_ref[...]) + mm(rows(2), two_ref[...]) + mm(rows(3), three_ref[...])

    @pl.when(core == 0)
    def _():
        total[...] = total[...] + mm(rows(0), mine_ref[...])

    part = pl.ds(pl.multiple_of(core * width, width), width)
    total[:, part] = total[:, part] + mm(rows(4), four_ref[...])
    keep_ref[...] = total[:kept]
    send_ref[...] = total[kept:].astype(BF16)


def add_kernel(keep_ref, come_ref, mine_ref, send_ref):
    total = (keep_ref[...] + come_ref[...].astype(F32)).astype(BF16)
    rows = mine_ref.shape[0]
    mine_ref[...] = total[:rows]
    send_ref[...] = total[rows:]


def lay_kernel(mine_ref, come_ref, out_ref):
    width = mine_ref.shape[1]
    half = lax.axis_index("xl")
    out_ref[:, pl.ds(pl.multiple_of(half * width, width), width)] = mine_ref[...]
    out_ref[:, pl.ds(pl.multiple_of((1 - half) * width, width), width)] = come_ref[...]


def hbm():
    return pl.BlockSpec(memory_space=pltpu.HBM)


def vmem():
    return pl.BlockSpec(memory_space=pltpu.VMEM)


def per_device(
    frames, norm_gain, qkv_weight, gate_weight, beta_scale, decay_rate, resets, out_gain, out_weight
):
    rows, width = frames.shape
    n = qkv_weight.shape[2]
    weight = qkv_weight.transpose(1, 0, 2)
    gate = gate_weight.transpose(2, 1, 0).reshape(2, width)
    square = jax.ShapeDtypeStruct((rows, n), F32)
    gain = norm_gain.reshape(1, width)

    def buffers(matrices):
        return [
            pltpu.VMEM((rows, width), BF16),
            pltpu.VMEM((rows, width), BF16),
            pltpu.VMEM((matrices, width, n), BF16),
            pltpu.SemaphoreType.DMA((2 + 2 * matrices,)),
        ]

    carry, key, solved, decay, gamma = pl.pallas_call(
        fold_kernel,
        name="fold",
        in_specs=[hbm(), hbm(), hbm(), vmem(), hbm(), vmem(), vmem()],
        out_specs=[vmem()] * 5,
        out_shape=[
            jax.ShapeDtypeStruct((n, 2 * n), BF16),
            square,
            jax.ShapeDtypeStruct((rows, 2 * n), F32),
            square,
            jax.ShapeDtypeStruct((rows, 1), F32),
        ],
        scratch_shapes=buffers(2)
        + [pltpu.SMEM((1,), F32), pltpu.SMEM((1,), F32), pltpu.SemaphoreType.DMA((2,))],
        compiler_params=LARGE,
    )(beta_scale, decay_rate, frames, gain, weight, gate, resets.reshape(1, rows))

    def look():
        return pl.pallas_call(
            look_kernel,
            name="look",
            in_specs=[hbm(), vmem(), hbm()] + [vmem()] * 4,
            out_specs=vmem(),
            out_shape=jax.ShapeDtypeStruct((rows, 2 * n), F32),
            scratch_shapes=buffers(1),
            compiler_params=LARGE,
            cost_estimate=pl.CostEstimate(
                flops=4 * rows * width * n, bytes_accessed=16 << 20, transcendentals=0
            ),
        )(frames, gain, weight, key, solved, decay, gamma)

    count = 32

    def moved(value, place_of):
        return lax.ppermute(value, SEQ, [(i, place_of(i)) for i in range(count)])

    def along_x(shift):
        return lambda i: (i // 8) * 8 + (i + 2 * shift) % 8

    def along_y(shift):
        return lambda i: (i + 8 * shift) % 32

    def flip(bits):
        return lambda i: i ^ bits

    def around(value):
        up = [(z, (z + 1) % 8) for z in range(8)]
        down = [(8 + z, 8 + (z + 7) % 8) for z in range(8)]
        return lax.ppermute(value, ("core", "head"), up + down)

    def later(value, gate):
        return lax.optimization_barrier((value, gate))[0]

    wide = out_weight.shape[1] // 2
    mine = pl.pallas_call(
        take_kernel,
        name="take",
        in_specs=[hbm()],
        out_specs=vmem(),
        out_shape=jax.ShapeDtypeStruct((n, wide), BF16),
        scratch_shapes=[pltpu.SemaphoreType.DMA],
        compiler_params=LARGE,
    )(out_weight)
    one = around(mine)

    pair_shape = jax.ShapeDtypeStruct((n, 2 * n), BF16)
    half_shape = jax.ShapeDtypeStruct((n // 2, 2 * n), BF16)
    other = moved(carry, flip(1))
    two = around(later(one, other))
    pair, half = pl.pallas_call(
        pair_kernel,
        name="pair",
        in_specs=[vmem()] * 2,
        out_specs=[vmem()] * 2,
        out_shape=[pair_shape, half_shape],
        compiler_params=SMALL,
    )(carry, other)
    near = [moved(half, along_x(s)) for s in (1, 2, 3)]
    near, looked = lax.optimization_barrier((near, look()))
    three = around(later(two, near))
    swapped = [moved(value, flip(1)) for value in near]
    half, prefix = pl.pallas_call(
        row_kernel,
        name="row",
        in_specs=[vmem()] * 7,
        out_specs=[vmem()] * 2,
        out_shape=[half_shape, pair_shape],
        scratch_shapes=[pltpu.VMEM((4, n, 2 * n), BF16), pltpu.VMEM((n, 2 * n), BF16)],
        compiler_params=SMALL,
    )(pair, *near, *swapped)
    near = [moved(half, along_y(s)) for s in (1, 2, 3)]
    four = around(
        later(
            lax.dynamic_slice_in_dim(three, lax.axis_index("core") * (wide // 2), wide // 2, 1), near
        )
    )
    swapped = [moved(value, flip(1)) for value in near]
    flat = pl.pallas_call(
        read_kernel,
        name="read",
        in_specs=[vmem()] * 10,
        out_specs=vmem(),
        out_shape=jax.ShapeDtypeStruct((2, rows, n), BF16),
        scratch_shapes=[pltpu.VMEM((4, n, 2 * n), BF16), pltpu.VMEM((n, n), F32)],
        compiler_params=SMALL,
    )(*near, *swapped, prefix, other, looked, out_gain.reshape(1, n))
    part = rows // 8
    flat, four = lax.optimization_barrier((flat, four))
    reads = lax.all_to_all(
        flat.reshape(16, part, n), ("xl", "head"), 0, 0, tiled=True
    ).reshape(2, 8, part, n)
    beside = moved(reads, flip(1))
    keep, send = pl.pallas_call(
        mix_kernel,
        name="mix",
        in_specs=[vmem()] * 7,
        out_specs=[vmem()] * 2,
        out_shape=[
            jax.ShapeDtypeStruct((2 * part, wide), F32),
            jax.ShapeDtypeStruct((2 * part, wide), BF16),
        ],
        scratch_shapes=[pltpu.VMEM((4 * part, wide), F32)],
        compiler_params=MIDDLE,
    )(reads, beside, mine, one, two, three, four)
    piece = jax.ShapeDtypeStruct((part, wide), BF16)
    kept, send = pl.pallas_call(
        add_kernel,
        name="add",
        in_specs=[vmem()] * 2,
        out_specs=[vmem()] * 2,
        out_shape=[piece] * 2,
        compiler_params=SMALL,
    )(keep, moved(send, flip(1)))
    return pl.pallas_call(
        lay_kernel,
        name="lay",
        in_specs=[vmem()] * 2,
        out_specs=vmem(),
        out_shape=jax.ShapeDtypeStruct((part, 2 * wide), BF16),
        compiler_params=SMALL,
    )(kept, moved(send, flip(2)))


def solution(mesh):
    fine = Mesh(mesh.devices.reshape(4, 2, 2, 2, 8), SEQ + ("head",))
    in_specs = (
        P(SEQ, None),
        P(),
        P(None, None, "head"),
        P(None, None, "head"),
        P("head"),
        P("head"),
        P(SEQ),
        P("head"),
        P("head", None),
    )
    out_specs = P(SEQ + ("head",), None)
    return jax.shard_map(
        per_device, mesh=fine, in_specs=in_specs, out_specs=out_specs, check_vma=False
    )
```

```python
import jax
import jax.numpy as jnp
from jax import lax
from jax.experimental import pallas as pl
from jax.experimental.pallas import tpu as pltpu
from jax.sharding import Mesh
from jax.sharding import PartitionSpec as P

F32 = jnp.float32
BF16 = jnp.bfloat16
NN = (((1,), (0,)), ((), ()))
NT = (((1,), (1,)), ((), ()))
TN = (((0,), (0,)), ((), ()))
SEQ = ("y", "xh", "xl", "core")
SMALL = pltpu.CompilerParams(vmem_limit_bytes=8 << 20)
MIDDLE = pltpu.CompilerParams(vmem_limit_bytes=16 << 20)
LARGE = pltpu.CompilerParams(vmem_limit_bytes=58 << 20)


def mm(a, b, dims=NN):
    return lax.dot_general(a, b, dims, preferred_element_type=F32)


def split(a):
    hi = a.astype(BF16)
    return hi, (a - hi.astype(F32)).astype(BF16)


def mm3(a, b, dims=NN):
    (ah, al), (bh, bl) = a, b
    return mm(ah, bh, dims) + (mm(ah, bl, dims) + mm(al, bh, dims))


def unit_rows(vectors):
    return vectors * lax.rsqrt(jnp.sum(vectors * vectors, axis=-1, keepdims=True) + 1e-06)


def norm_rows(x_ref, gain):
    x = x_ref[...].astype(F32)
    rs = lax.rsqrt(jnp.mean(x * x, axis=-1, keepdims=True) + 1e-06)
    return (x * rs * gain).astype(BF16)


def copies(x_hbm, w_hbm, slots, x_buf, w_buf, sems):
    halves = x_buf.shape[0] // 2
    depth = w_buf.shape[1] // 2
    rows = [pl.ds(i * halves, halves) for i in range(2)]
    parts = [pl.ds(i * depth, depth) for i in range(2)]
    found = [(x_hbm.at[part], x_buf.at[part]) for part in rows]
    for slot, j in enumerate(slots):
        found += [(w_hbm.at[j, part], w_buf.at[slot, part]) for part in parts]
    found = [pltpu.make_async_copy(a, b, sems.at[i]) for i, (a, b) in enumerate(found)]
    for copy in found:
        copy.start()
    return found


def normalise(found, x_buf, xn_buf, gain):
    half = x_buf.shape[0] // 2
    for i in range(2):
        found[i].wait()
        part = slice(i * half, (i + 1) * half)
        xn_buf[part] = norm_rows(x_buf.at[part], gain)


def project(found, xn_buf, w_buf, slot):
    depth = w_buf.shape[1] // 2
    total = None
    for i in range(2):
        found[2 + 2 * slot + i].wait()
        part = slice(i * depth, (i + 1) * depth)
        product = mm(xn_buf[:, part], w_buf[slot, part])
        total = product if total is None else total + product
    return total


def fold_kernel(
    scale_hbm, rate_hbm, x_hbm, gain_hbm, w_hbm, gate_hbm, resets_hbm,
    carry_ref, key_hbm, solved_hbm, decay_hbm, gamma_hbm,
    x_buf, xn_buf, w_buf, sems, scale_ref, rate_ref, gain_ref, gate_ref, resets_ref, small_sems,
    key_ref, solved_ref, decay_ref, gamma_ref, out_sems,
):
    small = [
        pltpu.make_async_copy(a, b, small_sems.at[i])
        for i, (a, b) in enumerate(
            (
                (gain_hbm, gain_ref),
                (gate_hbm, gate_ref),
                (resets_hbm, resets_ref),
                (scale_hbm, scale_ref),
                (rate_hbm, rate_ref),
            )
        )
    ]
    for copy in small:
        copy.start()
    found = copies(x_hbm, w_hbm, (1, 2), x_buf, w_buf, sems)
    small[0].wait()
    normalise(found, x_buf, xn_buf, gain_ref[...])
    n = x_buf.shape[0]
    for copy in small[1:] + found[2:]:
        copy.wait()
    kept = []

    def keep(value, ref, target):
        ref[...] = value
        kept.append(pltpu.make_async_copy(ref, target, out_sems.at[len(kept)]))
        kept[-1].start()

    gating = mm(xn_buf[...], gate_ref[...], NT)
    key = unit_rows(mm(xn_buf[...], w_buf[0]))
    beta = scale_ref[0] * jax.nn.sigmoid(gating[:, 0:1])
    logf = -rate_ref[0] * jax.nn.softplus(gating[:, 1:2])
    reset_row = resets_ref[...].astype(F32)
    t = lax.broadcasted_iota(jnp.int32, (n, n), 0)
    s = lax.broadcasted_iota(jnp.int32, (n, n), 1)
    causal = t >= s
    eye = t == s

    def to_row(col):
        return jnp.sum(jnp.where(eye, col, 0.0), axis=0, keepdims=True)

    cum = jnp.sum(jnp.where(causal, to_row(logf), 0.0), axis=1, keepdims=True)
    seg = jnp.sum(jnp.where(causal, reset_row, 0.0), axis=1, keepdims=True)
    cum_row = to_row(cum)
    seg_row = to_row(seg)
    same = (seg == seg_row) & causal
    decay = jnp.where(same, jnp.exp(jnp.where(same, cum - cum_row, 0.0)), 0.0)
    gamma = jnp.where(seg == 0.0, jnp.exp(cum), 0.0)
    cum_last, seg_last = cum[n - 1 : n], seg[n - 1 : n]
    tail = jnp.where(seg == seg_last, jnp.exp(cum_last - cum), 0.0)
    gamma_last = gamma[n - 1 : n]
    keep(key, key_ref, key_hbm)
    keep(decay, decay_ref, decay_hbm)
    keep(gamma, gamma_ref, gamma_hbm)

    ks = split(key)
    low = jnp.where(t > s, beta * decay * mm3(ks, ks, NT), 0.0)
    apart = t ^ s
    inv = jnp.where(eye, 1.0, jnp.where(apart == 1, -low, 0.0))
    levels = range(1, n.bit_length() - 1)
    depth = xn_buf.shape[1] // (len(levels) + 1)
    value = mm(xn_buf[:, :depth], w_buf[1, :depth])
    for level in levels:
        part = jnp.where((apart >> level) == 1, low, 0.0).astype(BF16)
        rough = inv.astype(BF16)
        inner = mm(part, rough).astype(BF16)
        chunk = slice(level * depth, (level + 1) * depth)
        value = value + mm(xn_buf[:, chunk], w_buf[1, chunk])
        inv = inv - mm(rough, inner)
    vs = split(inv)
    left = jnp.where(eye, 1.0, 0.0) - inv - mm3(split(low), vs)
    inv = inv + mm(vs[0], left.astype(BF16))

    rhs = jnp.concatenate([(beta * gamma) * key, beta * value], axis=1)
    solved = mm3(split(inv), split(rhs))
    keep(solved, solved_ref, solved_hbm)
    folded = mm3(split(key * tail), split(solved), TN)
    carry_ref[:, :n] = (jnp.where(eye, gamma_last, 0.0) - folded[:, :n]).astype(BF16)
    carry_ref[:, n:] = folded[:, n:].astype(BF16)
    for copy in kept:
        copy.wait()


def look_kernel(
    x_hbm, gain_ref, w_hbm, key_ref, solved_ref, decay_ref, gamma_ref,
    out_ref,
    x_buf, xn_buf, w_buf, sems,
):
    found = copies(x_hbm, w_hbm, (0,), x_buf, w_buf, sems)
    normalise(found, x_buf, xn_buf, gain_ref[...])
    n = x_buf.shape[0]
    query = unit_rows(project(found, xn_buf, w_buf, 0))
    scores = mm3(split(query), split(key_ref[...]), NT) * decay_ref[...]
    seen = mm3(split(scores), split(solved_ref[...]))
    out_ref[:, :n] = gamma_ref[...] * query - seen[:, :n]
    out_ref[:, n:] = seen[:, n:]


def after(later, earlier, n):
    both = mm(later[:, :n], earlier)
    return both[:, :n], both[:, n:] + later[:, n:].astype(F32)


def own_half(ref):
    half = ref.shape[0] // 2
    return ref[pl.ds(pl.multiple_of(lax.axis_index("core") * half, half), half)]


def hold(held, place, near_ref, swap_ref):
    half = near_ref.shape[0]
    core = lax.axis_index("core")
    held[place, pl.ds(pl.multiple_of(core * half, half), half)] = near_ref[...]
    held[place, pl.ds(pl.multiple_of((1 - core) * half, half), half)] = swap_ref[...]


def pair_kernel(own_ref, other_ref, out_ref, half_ref):
    n = own_ref.shape[0]
    first = lax.axis_index("core") == 0
    own, other = own_ref[...], other_ref[...]
    earlier = jnp.where(first, own, other)
    later = jnp.where(first, other, own)
    a, b = after(later, earlier, n)
    out_ref[:, :n] = a.astype(BF16)
    out_ref[:, n:] = b.astype(BF16)
    half_ref[...] = own_half(out_ref)


def row_kernel(own_ref, *refs):
    near, swapped, (half_ref, prefix_ref, held, total_ref) = refs[:3], refs[3:6], refs[6:]
    n = own_ref.shape[0]
    place = lax.axis_index("xh") * 2 + lax.axis_index("xl")
    held[place] = own_ref[...]
    for shift, ref, swap in zip((1, 2, 3), near, swapped):
        hold(held, (place + (4 - shift)) % 4, ref, swap)

    def joined(later, earlier):
        a, b = after(later, earlier, n)
        return jnp.concatenate([a, b], axis=1).astype(BF16)

    low = joined(held[1], held[0])
    high = joined(held[3], held[2])
    a, b = after(high, low, n)
    total_ref[:, :n] = a.astype(BF16)
    total_ref[:, n:] = b.astype(BF16)
    half_ref[...] = own_half(total_ref)

    @pl.when(place == 0)
    def _():
        prefix_ref[...] = jnp.zeros_like(prefix_ref)

    @pl.when(place == 1)
    def _():
        prefix_ref[...] = held[0]

    @pl.when(place == 2)
    def _():
        prefix_ref[...] = low

    @pl.when(place == 3)
    def _():
        prefix_ref[...] = joined(held[2], low)


def read_kernel(*refs):
    near, swapped = refs[:3], refs[3:6]
    prefix_ref, other_ref, look_ref, gain_ref, out_ref, held, state = refs[6:]
    n = look_ref.shape[0]
    place = lax.axis_index("y")
    for shift, ref, swap in zip((1, 2, 3), near, swapped):
        hold(held, (place + (4 - shift)) % 4, ref, swap)

    def push(pair, value):
        hi, lo = split(value)
        return mm(pair[:, :n], hi) + mm(pair[:, :n], lo) + pair[:, n:].astype(F32)

    @pl.when(place == 0)
    def _():
        state[...] = jnp.zeros_like(state)

    @pl.when(place > 0)
    def _():
        state[...] = held[0, :, n:].astype(F32)

    for turn in (1, 2):
        @pl.when(place > turn)
        def _():
            state[...] = push(held[turn], state[...])

    @pl.when(lax.axis_index("xh") + lax.axis_index("xl") > 0)
    def _():
        state[...] = push(prefix_ref[...], state[...])

    @pl.when(lax.axis_index("core") > 0)
    def _():
        state[...] = push(other_ref[...], state[...])

    read = look_ref[:, n:] + mm3(split(look_ref[:, :n]), split(state[...]))
    read = read * lax.rsqrt(jnp.mean(read * read, axis=-1, keepdims=True) + 1e-06)
    flat = (read * gain_ref[...]).astype(BF16)
    out_ref[0] = flat
    out_ref[1] = flat


def take_kernel(whole_ref, out_ref, sem):
    width = out_ref.shape[1]
    columns = pl.ds(pl.multiple_of(lax.axis_index("xl") * width, width), width)
    copy = pltpu.make_async_copy(whole_ref.at[:, columns], out_ref, sem)
    copy.start()
    copy.wait()


def mix_kernel(
    own_ref, other_ref, mine_ref, one_ref, two_ref, three_ref, four_ref, keep_ref, send_ref, total
):
    core, half, head = lax.axis_index("core"), lax.axis_index("xl"), lax.axis_index("head")
    kept = keep_ref.shape[0]
    width = four_ref.shape[1]

    def rows(steps):
        source = (head + (2 * core - 1) * steps + 8) % 8
        block = [ref[place, source] for ref in (own_ref, other_ref) for place in (half, 1 - half)]
        return jnp.concatenate(block, axis=0)

    total[...] = mm(rows(1), one_ref[...]) + mm(rows(2), two_ref[...]) + mm(rows(3), three_ref[...])

    @pl.when(core == 0)
    def _():
        total[...] = total[...] + mm(rows(0), mine_ref[...])

    part = pl.ds(pl.multiple_of(core * width, width), width)
    total[:, part] = total[:, part] + mm(rows(4), four_ref[...])
    keep_ref[...] = total[:kept]
    send_ref[...] = total[kept:].astype(BF16)


def add_kernel(keep_ref, come_ref, mine_ref, send_ref):
    total = (keep_ref[...] + come_ref[...].astype(F32)).astype(BF16)
    rows = mine_ref.shape[0]
    mine_ref[...] = total[:rows]
    send_ref[...] = total[rows:]


def lay_kernel(mine_ref, come_ref, out_ref):
    width = mine_ref.shape[1]
    half = lax.axis_index("xl")
    out_ref[:, pl.ds(pl.multiple_of(half * width, width), width)] = mine_ref[...]
    out_ref[:, pl.ds(pl.multiple_of((1 - half) * width, width), width)] = come_ref[...]


def hbm():
    return pl.BlockSpec(memory_space=pltpu.HBM)


def vmem():
    return pl.BlockSpec(memory_space=pltpu.VMEM)


def per_device(
    frames, norm_gain, qkv_weight, gate_weight, beta_scale, decay_rate, resets, out_gain, out_weight
):
    rows, width = frames.shape
    n = qkv_weight.shape[2]
    weight = qkv_weight.transpose(1, 0, 2)
    gate = gate_weight.transpose(2, 1, 0).reshape(2, width)
    square = jax.ShapeDtypeStruct((rows, n), F32)
    gain = norm_gain.reshape(1, width)

    def buffers(matrices):
        return [
            pltpu.VMEM((rows, width), BF16),
            pltpu.VMEM((rows, width), BF16),
            pltpu.VMEM((matrices, width, n), BF16),
            pltpu.SemaphoreType.DMA((2 + 2 * matrices,)),
        ]

    carry, key, solved, decay, gamma = pl.pallas_call(
        fold_kernel,
        name="fold",
        in_specs=[hbm()] * 7,
        out_specs=[vmem()] + [hbm()] * 4,
        out_shape=[
            jax.ShapeDtypeStruct((n, 2 * n), BF16),
            square,
            jax.ShapeDtypeStruct((rows, 2 * n), F32),
            square,
            jax.ShapeDtypeStruct((rows, 1), F32),
        ],
        scratch_shapes=buffers(2)
        + [
            pltpu.SMEM((1,), F32),
            pltpu.SMEM((1,), F32),
            pltpu.VMEM((1, width), F32),
            pltpu.VMEM((2, width), BF16),
            pltpu.VMEM((1, rows), jnp.int32),
            pltpu.SemaphoreType.DMA((5,)),
            pltpu.VMEM((rows, n), F32),
            pltpu.VMEM((rows, 2 * n), F32),
            pltpu.VMEM((rows, n), F32),
            pltpu.VMEM((rows, 1), F32),
            pltpu.SemaphoreType.DMA((4,)),
        ],
        compiler_params=LARGE,
    )(beta_scale, decay_rate, frames, gain, weight, gate, resets.reshape(1, rows))

    def look():
        return pl.pallas_call(
            look_kernel,
            name="look",
            in_specs=[hbm(), vmem(), hbm()] + [vmem()] * 4,
            out_specs=vmem(),
            out_shape=jax.ShapeDtypeStruct((rows, 2 * n), F32),
            scratch_shapes=buffers(1),
            compiler_params=LARGE,
            cost_estimate=pl.CostEstimate(
                flops=4 * rows * width * n, bytes_accessed=16 << 20, transcendentals=0
            ),
        )(frames, gain, weight, key, solved, decay, gamma)

    count = 32

    def moved(value, place_of):
        return lax.ppermute(value, SEQ, [(i, place_of(i)) for i in range(count)])

    def along_x(shift):
        return lambda i: (i // 8) * 8 + (i + 2 * shift) % 8

    def along_y(shift):
        return lambda i: (i + 8 * shift) % 32

    def flip(bits):
        return lambda i: i ^ bits

    def around(value):
        up = [(z, (z + 1) % 8) for z in range(8)]
        down = [(8 + z, 8 + (z + 7) % 8) for z in range(8)]
        return lax.ppermute(value, ("core", "head"), up + down)

    def later(value, gate):
        return lax.optimization_barrier((value, gate))[0]

    wide = out_weight.shape[1] // 2
    mine = pl.pallas_call(
        take_kernel,
        name="take",
        in_specs=[hbm()],
        out_specs=vmem(),
        out_shape=jax.ShapeDtypeStruct((n, wide), BF16),
        scratch_shapes=[pltpu.SemaphoreType.DMA],
        compiler_params=LARGE,
    )(out_weight)
    one = around(mine)

    pair_shape = jax.ShapeDtypeStruct((n, 2 * n), BF16)
    half_shape = jax.ShapeDtypeStruct((n // 2, 2 * n), BF16)
    other = moved(carry, flip(1))
    two = around(later(one, other))
    pair, half = pl.pallas_call(
        pair_kernel,
        name="pair",
        in_specs=[vmem()] * 2,
        out_specs=[vmem()] * 2,
        out_shape=[pair_shape, half_shape],
        compiler_params=SMALL,
    )(carry, other)
    near = [moved(half, along_x(s)) for s in (1, 2, 3)]
    near, looked = lax.optimization_barrier((near, look()))
    swapped = [moved(value, flip(1)) for value in near]
    half, prefix = pl.pallas_call(
        row_kernel,
        name="row",
        in_specs=[vmem()] * 7,
        out_specs=[vmem()] * 2,
        out_shape=[half_shape, pair_shape],
        scratch_shapes=[pltpu.VMEM((4, n, 2 * n), BF16), pltpu.VMEM((n, 2 * n), BF16)],
        compiler_params=SMALL,
    )(pair, *near, *swapped)
    three = around(later(two, half))
    near = [moved(half, along_y(s)) for s in (1, 2, 3)]
    swapped = [moved(value, flip(1)) for value in near]
    flat = pl.pallas_call(
        read_kernel,
        name="read",
        in_specs=[vmem()] * 10,
        out_specs=vmem(),
        out_shape=jax.ShapeDtypeStruct((2, rows, n), BF16),
        scratch_shapes=[pltpu.VMEM((4, n, 2 * n), BF16), pltpu.VMEM((n, n), F32)],
        compiler_params=SMALL,
    )(*near, *swapped, prefix, other, looked, out_gain.reshape(1, n))
    part = rows // 8
    part_three = lax.dynamic_slice_in_dim(
        three, lax.axis_index("core") * (wide // 2), wide // 2, 1
    )
    flat, part_three = lax.optimization_barrier((flat, part_three))
    four = around(part_three)
    reads = lax.all_to_all(
        flat.reshape(16, part, n), ("xl", "head"), 0, 0, tiled=True
    ).reshape(2, 8, part, n)
    beside = moved(reads, flip(1))
    keep, send = pl.pallas_call(
        mix_kernel,
        name="mix",
        in_specs=[vmem()] * 7,
        out_specs=[vmem()] * 2,
        out_shape=[
            jax.ShapeDtypeStruct((2 * part, wide), F32),
            jax.ShapeDtypeStruct((2 * part, wide), BF16),
        ],
        scratch_shapes=[pltpu.VMEM((4 * part, wide), F32)],
        compiler_params=MIDDLE,
    )(reads, beside, mine, one, two, three, four)
    piece = jax.ShapeDtypeStruct((part, wide), BF16)
    kept, send = pl.pallas_call(
        add_kernel,
        name="add",
        in_specs=[vmem()] * 2,
        out_specs=[vmem()] * 2,
        out_shape=[piece] * 2,
        compiler_params=SMALL,
    )(keep, moved(send, flip(1)))
    return pl.pallas_call(
        lay_kernel,
        name="lay",
        in_specs=[vmem()] * 2,
        out_specs=vmem(),
        out_shape=jax.ShapeDtypeStruct((part, 2 * wide), BF16),
        compiler_params=SMALL,
    )(kept, moved(send, flip(2)))


def solution(mesh):
    fine = Mesh(mesh.devices.reshape(4, 2, 2, 2, 8), SEQ + ("head",))
    in_specs = (
        P(SEQ, None),
        P(),
        P(None, None, "head"),
        P(None, None, "head"),
        P("head"),
        P("head"),
        P(SEQ),
        P("head"),
        P("head", None),
    )
    out_specs = P(SEQ + ("head",), None)
    return jax.shard_map(
        per_device, mesh=fine, in_specs=in_specs, out_specs=out_specs, check_vma=False
    )
```

```python
import jax
import jax.numpy as jnp
from jax import lax
from jax.experimental import pallas as pl
from jax.experimental.pallas import tpu as pltpu
from jax.sharding import Mesh
from jax.sharding import PartitionSpec as P

F32 = jnp.float32
BF16 = jnp.bfloat16
NN = (((1,), (0,)), ((), ()))
NT = (((1,), (1,)), ((), ()))
TN = (((0,), (0,)), ((), ()))
SEQ = ("y", "xh", "xl", "core")
SMALL = pltpu.CompilerParams(vmem_limit_bytes=8 << 20)
WHOLE = pltpu.CompilerParams(vmem_limit_bytes=52 << 20)
LARGE = pltpu.CompilerParams(vmem_limit_bytes=58 << 20)


def mm(a, b, dims=NN):
    return lax.dot_general(a, b, dims, preferred_element_type=F32)


def split(a):
    hi = a.astype(BF16)
    return hi, (a - hi.astype(F32)).astype(BF16)


def mm3(a, b, dims=NN):
    (ah, al), (bh, bl) = a, b
    return mm(ah, bh, dims) + (mm(ah, bl, dims) + mm(al, bh, dims))


def unit_rows(vectors):
    return vectors * lax.rsqrt(jnp.sum(vectors * vectors, axis=-1, keepdims=True) + 1e-06)


def norm_rows(x_ref, gain):
    x = x_ref[...].astype(F32)
    rs = lax.rsqrt(jnp.mean(x * x, axis=-1, keepdims=True) + 1e-06)
    return (x * rs * gain).astype(BF16)


def copies(x_hbm, w_hbm, slots, x_buf, w_buf, sems):
    halves = x_buf.shape[0] // 2
    depth = w_buf.shape[1] // 2
    rows = [pl.ds(i * halves, halves) for i in range(2)]
    parts = [pl.ds(i * depth, depth) for i in range(2)]
    found = [(x_hbm.at[part], x_buf.at[part]) for part in rows]
    for slot, j in enumerate(slots):
        found += [(w_hbm.at[j, part], w_buf.at[slot, part]) for part in parts]
    found = [pltpu.make_async_copy(a, b, sems.at[i]) for i, (a, b) in enumerate(found)]
    for copy in found:
        copy.start()
    return found


def normalise(found, x_buf, xn_buf, gain):
    half = x_buf.shape[0] // 2
    for i in range(2):
        found[i].wait()
        part = slice(i * half, (i + 1) * half)
        xn_buf[part] = norm_rows(x_buf.at[part], gain)


def project(found, xn_buf, w_buf, slot):
    depth = w_buf.shape[1] // 2
    total = None
    for i in range(2):
        found[2 + 2 * slot + i].wait()
        part = slice(i * depth, (i + 1) * depth)
        product = mm(xn_buf[:, part], w_buf[slot, part])
        total = product if total is None else total + product
    return total


def fold_kernel(
    scale_hbm, rate_hbm, x_hbm, gain_hbm, w_hbm, gate_hbm, resets_hbm,
    carry_ref, key_hbm, solved_hbm, decay_hbm, gamma_hbm,
    x_buf, xn_buf, w_buf, sems, scale_ref, rate_ref, gain_ref, gate_ref, resets_ref, small_sems,
    key_ref, solved_ref, decay_ref, gamma_ref, out_sems,
):
    small = [
        pltpu.make_async_copy(a, b, small_sems.at[i])
        for i, (a, b) in enumerate(
            (
                (gain_hbm, gain_ref),
                (gate_hbm, gate_ref),
                (resets_hbm, resets_ref),
                (scale_hbm, scale_ref),
                (rate_hbm, rate_ref),
            )
        )
    ]
    for copy in small:
        copy.start()
    found = copies(x_hbm, w_hbm, (1, 2), x_buf, w_buf, sems)
    small[0].wait()
    normalise(found, x_buf, xn_buf, gain_ref[...])
    n = x_buf.shape[0]
    for copy in small[1:] + found[2:]:
        copy.wait()
    kept = []

    def keep(value, ref, target):
        ref[...] = value
        kept.append(pltpu.make_async_copy(ref, target, out_sems.at[len(kept)]))
        kept[-1].start()

    gating = mm(xn_buf[...], gate_ref[...], NT)
    key = unit_rows(mm(xn_buf[...], w_buf[0]))
    beta = scale_ref[0] * jax.nn.sigmoid(gating[:, 0:1])
    logf = -rate_ref[0] * jax.nn.softplus(gating[:, 1:2])
    reset_row = resets_ref[...].astype(F32)
    t = lax.broadcasted_iota(jnp.int32, (n, n), 0)
    s = lax.broadcasted_iota(jnp.int32, (n, n), 1)
    causal = t >= s
    eye = t == s

    def to_row(col):
        return jnp.sum(jnp.where(eye, col, 0.0), axis=0, keepdims=True)

    cum = jnp.sum(jnp.where(causal, to_row(logf), 0.0), axis=1, keepdims=True)
    seg = jnp.sum(jnp.where(causal, reset_row, 0.0), axis=1, keepdims=True)
    cum_row = to_row(cum)
    seg_row = to_row(seg)
    same = (seg == seg_row) & causal
    decay = jnp.where(same, jnp.exp(jnp.where(same, cum - cum_row, 0.0)), 0.0)
    gamma = jnp.where(seg == 0.0, jnp.exp(cum), 0.0)
    cum_last, seg_last = cum[n - 1 : n], seg[n - 1 : n]
    tail = jnp.where(seg == seg_last, jnp.exp(cum_last - cum), 0.0)
    gamma_last = gamma[n - 1 : n]
    keep(key, key_ref, key_hbm)
    keep(decay, decay_ref, decay_hbm)
    keep(gamma, gamma_ref, gamma_hbm)

    ks = split(key)
    low = jnp.where(t > s, beta * decay * mm3(ks, ks, NT), 0.0)
    apart = t ^ s
    inv = jnp.where(eye, 1.0, jnp.where(apart == 1, -low, 0.0))
    levels = range(1, n.bit_length() - 1)
    depth = xn_buf.shape[1] // (len(levels) + 1)
    value = mm(xn_buf[:, :depth], w_buf[1, :depth])
    for level in levels:
        part = jnp.where((apart >> level) == 1, low, 0.0).astype(BF16)
        rough = inv.astype(BF16)
        inner = mm(part, rough).astype(BF16)
        chunk = slice(level * depth, (level + 1) * depth)
        value = value + mm(xn_buf[:, chunk], w_buf[1, chunk])
        inv = inv - mm(rough, inner)
    vs = split(inv)
    left = jnp.where(eye, 1.0, 0.0) - inv - mm3(split(low), vs)
    inv = inv + mm(vs[0], left.astype(BF16))

    rhs = jnp.concatenate([(beta * gamma) * key, beta * value], axis=1)
    solved = mm3(split(inv), split(rhs))
    keep(solved, solved_ref, solved_hbm)
    folded = mm3(split(key * tail), split(solved), TN)
    carry_ref[:, :n] = (jnp.where(eye, gamma_last, 0.0) - folded[:, :n]).astype(BF16)
    carry_ref[:, n:] = folded[:, n:].astype(BF16)
    for copy in kept:
        copy.wait()


def look_kernel(
    x_hbm, gain_ref, w_hbm, key_ref, solved_ref, decay_ref, gamma_ref,
    out_ref,
    x_buf, xn_buf, w_buf, sems,
):
    found = copies(x_hbm, w_hbm, (0,), x_buf, w_buf, sems)
    normalise(found, x_buf, xn_buf, gain_ref[...])
    n = x_buf.shape[0]
    query = unit_rows(project(found, xn_buf, w_buf, 0))
    scores = mm3(split(query), split(key_ref[...]), NT) * decay_ref[...]
    seen = mm3(split(scores), split(solved_ref[...]))
    out_ref[:, :n] = gamma_ref[...] * query - seen[:, :n]
    out_ref[:, n:] = seen[:, n:]


def after(later, earlier, n):
    both = mm(later[:, :n], earlier)
    return both[:, :n], both[:, n:] + later[:, n:].astype(F32)


def own_half(ref):
    half = ref.shape[0] // 2
    return ref[pl.ds(pl.multiple_of(lax.axis_index("core") * half, half), half)]


def hold(held, place, near_ref, swap_ref):
    half = near_ref.shape[0]
    core = lax.axis_index("core")
    held[place, pl.ds(pl.multiple_of(core * half, half), half)] = near_ref[...]
    held[place, pl.ds(pl.multiple_of((1 - core) * half, half), half)] = swap_ref[...]


def pair_kernel(own_ref, other_ref, out_ref, half_ref):
    n = own_ref.shape[0]
    first = lax.axis_index("core") == 0
    own, other = own_ref[...], other_ref[...]
    earlier = jnp.where(first, own, other)
    later = jnp.where(first, other, own)
    a, b = after(later, earlier, n)
    out_ref[:, :n] = a.astype(BF16)
    out_ref[:, n:] = b.astype(BF16)
    half_ref[...] = own_half(out_ref)


def row_kernel(own_ref, *refs):
    near, swapped, (half_ref, prefix_ref, held, total_ref) = refs[:3], refs[3:6], refs[6:]
    n = own_ref.shape[0]
    place = lax.axis_index("xh") * 2 + lax.axis_index("xl")
    held[place] = own_ref[...]
    for shift, ref, swap in zip((1, 2, 3), near, swapped):
        hold(held, (place + (4 - shift)) % 4, ref, swap)

    def joined(later, earlier):
        a, b = after(later, earlier, n)
        return jnp.concatenate([a, b], axis=1).astype(BF16)

    low = joined(held[1], held[0])
    high = joined(held[3], held[2])
    a, b = after(high, low, n)
    total_ref[:, :n] = a.astype(BF16)
    total_ref[:, n:] = b.astype(BF16)
    half_ref[...] = own_half(total_ref)

    @pl.when(place == 0)
    def _():
        prefix_ref[...] = jnp.zeros_like(prefix_ref)

    @pl.when(place == 1)
    def _():
        prefix_ref[...] = held[0]

    @pl.when(place == 2)
    def _():
        prefix_ref[...] = low

    @pl.when(place == 3)
    def _():
        prefix_ref[...] = joined(held[2], low)


def read_kernel(*refs):
    near, swapped = refs[:3], refs[3:6]
    prefix_ref, other_ref, look_ref, gain_ref, out_ref, held, state = refs[6:]
    n = look_ref.shape[0]
    place = lax.axis_index("y")
    for shift, ref, swap in zip((1, 2, 3), near, swapped):
        hold(held, (place + (4 - shift)) % 4, ref, swap)

    def push(pair, value):
        hi, lo = split(value)
        return mm(pair[:, :n], hi) + mm(pair[:, :n], lo) + pair[:, n:].astype(F32)

    @pl.when(place == 0)
    def _():
        state[...] = jnp.zeros_like(state)

    @pl.when(place > 0)
    def _():
        state[...] = held[0, :, n:].astype(F32)

    for turn in (1, 2):
        @pl.when(place > turn)
        def _():
            state[...] = push(held[turn], state[...])

    @pl.when(lax.axis_index("xh") + lax.axis_index("xl") > 0)
    def _():
        state[...] = push(prefix_ref[...], state[...])

    @pl.when(lax.axis_index("core") > 0)
    def _():
        state[...] = push(other_ref[...], state[...])

    read = look_ref[:, n:] + mm3(split(look_ref[:, :n]), split(state[...]))
    read = read * lax.rsqrt(jnp.mean(read * read, axis=-1, keepdims=True) + 1e-06)
    flat = (read * gain_ref[...]).astype(BF16)
    out_ref[0] = flat
    out_ref[1] = flat


def take_kernel(whole_ref, out_ref, sem):
    width = out_ref.shape[1]
    block = lax.axis_index("core") * 2 + lax.axis_index("xl")
    columns = pl.ds(pl.multiple_of(block * width, width), width)
    copy = pltpu.make_async_copy(whole_ref.at[:, columns], out_ref, sem)
    copy.start()
    copy.wait()


def mix_kernel(own_ref, other_ref, weight_hbm, *refs):
    outs, weight_ref, sems = refs[:-2], refs[-2], refs[-1]
    found = [
        pltpu.make_async_copy(weight_hbm.at[head], weight_ref.at[head], sems.at[head])
        for head in range(weight_ref.shape[0])
    ]
    for copy in found:
        copy.start()
    half = lax.axis_index("xl")
    rows = own_ref.shape[2]
    for head, copy in enumerate(found):
        block = [ref[place, head] for place in (half, 1 - half) for ref in (own_ref, other_ref)]
        copy.wait()
        part = mm(jnp.concatenate(block, axis=0), weight_ref[head])
        total = part if head == 0 else total + part
    total = total.astype(BF16)
    for k, ref in enumerate(outs):
        ref[...] = total[k * rows : (k + 1) * rows]


def lay_kernel(mine_ref, core_ref, half_ref, far_ref, out_ref):
    width = mine_ref.shape[1]
    block = lax.axis_index("core") * 2 + lax.axis_index("xl")
    for flip, ref in ((0, mine_ref), (2, core_ref), (1, half_ref), (3, far_ref)):
        place = pl.multiple_of((block ^ flip) * width, width)
        out_ref[:, pl.ds(place, width)] = ref[...]


def hbm():
    return pl.BlockSpec(memory_space=pltpu.HBM)


def vmem():
    return pl.BlockSpec(memory_space=pltpu.VMEM)


def per_device(
    frames, norm_gain, qkv_weight, gate_weight, beta_scale, decay_rate, resets, out_gain, out_weight
):
    rows, width = frames.shape
    n = qkv_weight.shape[2]
    weight = qkv_weight.transpose(1, 0, 2)
    gate = gate_weight.transpose(2, 1, 0).reshape(2, width)
    square = jax.ShapeDtypeStruct((rows, n), F32)
    gain = norm_gain.reshape(1, width)

    def buffers(matrices):
        return [
            pltpu.VMEM((rows, width), BF16),
            pltpu.VMEM((rows, width), BF16),
            pltpu.VMEM((matrices, width, n), BF16),
            pltpu.SemaphoreType.DMA((2 + 2 * matrices,)),
        ]

    carry, key, solved, decay, gamma = pl.pallas_call(
        fold_kernel,
        name="fold",
        in_specs=[hbm()] * 7,
        out_specs=[vmem()] + [hbm()] * 4,
        out_shape=[
            jax.ShapeDtypeStruct((n, 2 * n), BF16),
            square,
            jax.ShapeDtypeStruct((rows, 2 * n), F32),
            square,
            jax.ShapeDtypeStruct((rows, 1), F32),
        ],
        scratch_shapes=buffers(2)
        + [
            pltpu.SMEM((1,), F32),
            pltpu.SMEM((1,), F32),
            pltpu.VMEM((1, width), F32),
            pltpu.VMEM((2, width), BF16),
            pltpu.VMEM((1, rows), jnp.int32),
            pltpu.SemaphoreType.DMA((5,)),
            pltpu.VMEM((rows, n), F32),
            pltpu.VMEM((rows, 2 * n), F32),
            pltpu.VMEM((rows, n), F32),
            pltpu.VMEM((rows, 1), F32),
            pltpu.SemaphoreType.DMA((4,)),
        ],
        compiler_params=LARGE,
    )(beta_scale, decay_rate, frames, gain, weight, gate, resets.reshape(1, rows))

    def look():
        return pl.pallas_call(
            look_kernel,
            name="look",
            in_specs=[hbm(), vmem(), hbm()] + [vmem()] * 4,
            out_specs=vmem(),
            out_shape=jax.ShapeDtypeStruct((rows, 2 * n), F32),
            scratch_shapes=buffers(1),
            compiler_params=LARGE,
            cost_estimate=pl.CostEstimate(
                flops=4 * rows * width * n, bytes_accessed=16 << 20, transcendentals=0
            ),
        )(frames, gain, weight, key, solved, decay, gamma)

    count = 32

    def moved(value, place_of):
        return lax.ppermute(value, SEQ, [(i, place_of(i)) for i in range(count)])

    def along_x(shift):
        return lambda i: (i // 8) * 8 + (i + 2 * shift) % 8

    def along_y(shift):
        return lambda i: (i + 8 * shift) % 32

    def flip(bits):
        return lambda i: i ^ bits

    quarter = out_weight.shape[1] // 4
    mine = pl.pallas_call(
        take_kernel,
        name="take",
        in_specs=[hbm()],
        out_specs=vmem(),
        out_shape=jax.ShapeDtypeStruct((n, quarter), BF16),
        scratch_shapes=[pltpu.SemaphoreType.DMA],
        compiler_params=LARGE,
    )(out_weight)
    columns = lax.all_gather(mine, "head", tiled=False)

    pair_shape = jax.ShapeDtypeStruct((n, 2 * n), BF16)
    half_shape = jax.ShapeDtypeStruct((n // 2, 2 * n), BF16)
    other = moved(carry, flip(1))
    pair, half = pl.pallas_call(
        pair_kernel,
        name="pair",
        in_specs=[vmem()] * 2,
        out_specs=[vmem()] * 2,
        out_shape=[pair_shape, half_shape],
        compiler_params=SMALL,
    )(carry, other)
    near = [moved(half, along_x(s)) for s in (1, 2, 3)]
    near, looked = lax.optimization_barrier((near, look()))
    swapped = [moved(value, flip(1)) for value in near]
    half, prefix = pl.pallas_call(
        row_kernel,
        name="row",
        in_specs=[vmem()] * 7,
        out_specs=[vmem()] * 2,
        out_shape=[half_shape, pair_shape],
        scratch_shapes=[pltpu.VMEM((4, n, 2 * n), BF16), pltpu.VMEM((n, 2 * n), BF16)],
        compiler_params=SMALL,
    )(pair, *near, *swapped)
    near = [moved(half, along_y(s)) for s in (1, 2, 3)]
    swapped = [moved(value, flip(1)) for value in near]
    flat = pl.pallas_call(
        read_kernel,
        name="read",
        in_specs=[vmem()] * 10,
        out_specs=vmem(),
        out_shape=jax.ShapeDtypeStruct((2, rows, n), BF16),
        scratch_shapes=[pltpu.VMEM((4, n, 2 * n), BF16), pltpu.VMEM((n, n), F32)],
        compiler_params=SMALL,
    )(*near, *swapped, prefix, other, looked, out_gain.reshape(1, n))
    part = rows // 8
    reads = lax.all_to_all(
        flat.reshape(16, part, n), ("xl", "head"), 0, 0, tiled=True
    ).reshape(2, 8, part, n)
    beside = moved(reads, flip(1))
    piece = jax.ShapeDtypeStruct((part, quarter), BF16)
    kept, to_core, to_half, to_far = pl.pallas_call(
        mix_kernel,
        name="mix",
        in_specs=[vmem(), vmem(), hbm()],
        out_specs=[vmem()] * 4,
        out_shape=[piece] * 4,
        scratch_shapes=[pltpu.VMEM((8, n, quarter), BF16), pltpu.SemaphoreType.DMA((8,))],
        compiler_params=WHOLE,
    )(reads, beside, columns)
    return pl.pallas_call(
        lay_kernel,
        name="lay",
        in_specs=[vmem()] * 4,
        out_specs=vmem(),
        out_shape=jax.ShapeDtypeStruct((part, 4 * quarter), BF16),
        compiler_params=SMALL,
    )(kept, moved(to_core, flip(1)), moved(to_half, flip(2)), moved(to_far, flip(3)))


def solution(mesh):
    fine = Mesh(mesh.devices.reshape(4, 2, 2, 2, 8), SEQ + ("head",))
    in_specs = (
        P(SEQ, None),
        P(),
        P(None, None, "head"),
        P(None, None, "head"),
        P("head"),
        P("head"),
        P(SEQ),
        P("head"),
        P("head", None),
    )
    out_specs = P(SEQ + ("head",), None)
    return jax.shard_map(
        per_device, mesh=fine, in_specs=in_specs, out_specs=out_specs, check_vma=False
    )
```

```python
import jax
import jax.numpy as jnp
from jax import lax
from jax.experimental import pallas as pl
from jax.experimental.pallas import tpu as pltpu
from jax.sharding import Mesh
from jax.sharding import PartitionSpec as P

F32 = jnp.float32
BF16 = jnp.bfloat16
NN = (((1,), (0,)), ((), ()))
NT = (((1,), (1,)), ((), ()))
TN = (((0,), (0,)), ((), ()))
SEQ = ("yh", "yl", "xh", "xl", "core")
SMALL = pltpu.CompilerParams(vmem_limit_bytes=8 << 20)
MIDDLE = pltpu.CompilerParams(vmem_limit_bytes=16 << 20)
LARGE = pltpu.CompilerParams(vmem_limit_bytes=58 << 20)


def mm(a, b, dims=NN):
    return lax.dot_general(a, b, dims, preferred_element_type=F32)


def split(a):
    hi = a.astype(BF16)
    return hi, (a - hi.astype(F32)).astype(BF16)


def mm3(a, b, dims=NN):
    (ah, al), (bh, bl) = a, b
    return mm(ah, bh, dims) + (mm(ah, bl, dims) + mm(al, bh, dims))


def unit_rows(vectors):
    return vectors * lax.rsqrt(jnp.sum(vectors * vectors, axis=-1, keepdims=True) + 1e-06)


def norm_rows(x_ref, gain):
    x = x_ref[...].astype(F32)
    rs = lax.rsqrt(jnp.mean(x * x, axis=-1, keepdims=True) + 1e-06)
    return (x * rs * gain).astype(BF16)


def copies(x_hbm, w_hbm, slots, x_buf, w_buf, sems):
    halves = x_buf.shape[0] // 2
    depth = w_buf.shape[1] // 2
    rows = [pl.ds(i * halves, halves) for i in range(2)]
    parts = [pl.ds(i * depth, depth) for i in range(2)]
    found = [(x_hbm.at[part], x_buf.at[part]) for part in rows]
    for slot, j in enumerate(slots):
        found += [(w_hbm.at[j, part], w_buf.at[slot, part]) for part in parts]
    found = [pltpu.make_async_copy(a, b, sems.at[i]) for i, (a, b) in enumerate(found)]
    for copy in found:
        copy.start()
    return found


def normalise(found, x_buf, xn_buf, gain):
    half = x_buf.shape[0] // 2
    for i in range(2):
        found[i].wait()
        part = slice(i * half, (i + 1) * half)
        xn_buf[part] = norm_rows(x_buf.at[part], gain)


def project(found, xn_buf, w_buf, slot):
    depth = w_buf.shape[1] // 2
    total = None
    for i in range(2):
        found[2 + 2 * slot + i].wait()
        part = slice(i * depth, (i + 1) * depth)
        product = mm(xn_buf[:, part], w_buf[slot, part])
        total = product if total is None else total + product
    return total


def fold_kernel(
    scale_hbm, rate_hbm, x_hbm, gain_hbm, w_hbm, gate_hbm, resets_hbm,
    carry_ref, key_hbm, solved_hbm, decay_hbm, gamma_hbm,
    x_buf, xn_buf, w_buf, sems, scale_ref, rate_ref, gain_ref, gate_ref, resets_ref, small_sems,
    key_ref, solved_ref, decay_ref, gamma_ref, out_sems,
):
    small = [
        pltpu.make_async_copy(a, b, small_sems.at[i])
        for i, (a, b) in enumerate(
            (
                (gain_hbm, gain_ref),
                (gate_hbm, gate_ref),
                (resets_hbm, resets_ref),
                (scale_hbm, scale_ref),
                (rate_hbm, rate_ref),
            )
        )
    ]
    for copy in small:
        copy.start()
    found = copies(x_hbm, w_hbm, (1, 2), x_buf, w_buf, sems)
    small[0].wait()
    normalise(found, x_buf, xn_buf, gain_ref[...])
    n = x_buf.shape[0]
    for copy in small[1:] + found[2:]:
        copy.wait()
    kept = []

    def keep(value, ref, target):
        ref[...] = value
        kept.append(pltpu.make_async_copy(ref, target, out_sems.at[len(kept)]))
        kept[-1].start()

    gating = mm(xn_buf[...], gate_ref[...], NT)
    key = unit_rows(mm(xn_buf[...], w_buf[0]))
    beta = scale_ref[0] * jax.nn.sigmoid(gating[:, 0:1])
    logf = -rate_ref[0] * jax.nn.softplus(gating[:, 1:2])
    reset_row = resets_ref[...].astype(F32)
    t = lax.broadcasted_iota(jnp.int32, (n, n), 0)
    s = lax.broadcasted_iota(jnp.int32, (n, n), 1)
    causal = t >= s
    eye = t == s

    def to_row(col):
        return jnp.sum(jnp.where(eye, col, 0.0), axis=0, keepdims=True)

    cum = jnp.sum(jnp.where(causal, to_row(logf), 0.0), axis=1, keepdims=True)
    seg = jnp.sum(jnp.where(causal, reset_row, 0.0), axis=1, keepdims=True)
    cum_row = to_row(cum)
    seg_row = to_row(seg)
    same = (seg == seg_row) & causal
    decay = jnp.where(same, jnp.exp(jnp.where(same, cum - cum_row, 0.0)), 0.0)
    gamma = jnp.where(seg == 0.0, jnp.exp(cum), 0.0)
    cum_last, seg_last = cum[n - 1 : n], seg[n - 1 : n]
    tail = jnp.where(seg == seg_last, jnp.exp(cum_last - cum), 0.0)
    gamma_last = gamma[n - 1 : n]
    keep(key, key_ref, key_hbm)
    keep(decay, decay_ref, decay_hbm)
    keep(gamma, gamma_ref, gamma_hbm)

    ks = split(key)
    low = jnp.where(t > s, beta * decay * mm3(ks, ks, NT), 0.0)
    apart = t ^ s
    inv = jnp.where(eye, 1.0, jnp.where(apart == 1, -low, 0.0))
    levels = range(1, n.bit_length() - 1)
    depth = xn_buf.shape[1] // (len(levels) + 1)
    value = mm(xn_buf[:, :depth], w_buf[1, :depth])
    for level in levels:
        part = jnp.where((apart >> level) == 1, low, 0.0).astype(BF16)
        rough = inv.astype(BF16)
        inner = mm(part, rough).astype(BF16)
        chunk = slice(level * depth, (level + 1) * depth)
        value = value + mm(xn_buf[:, chunk], w_buf[1, chunk])
        inv = inv - mm(rough, inner)
    vs = split(inv)
    left = jnp.where(eye, 1.0, 0.0) - inv - mm3(split(low), vs)
    inv = inv + mm(vs[0], left.astype(BF16))

    rhs = jnp.concatenate([(beta * gamma) * key, beta * value], axis=1)
    solved = mm3(split(inv), split(rhs))
    keep(solved, solved_ref, solved_hbm)
    folded = mm3(split(key * tail), split(solved), TN)
    carry_ref[:, :n] = (jnp.where(eye, gamma_last, 0.0) - folded[:, :n]).astype(BF16)
    carry_ref[:, n:] = folded[:, n:].astype(BF16)
    for copy in kept:
        copy.wait()


def look_kernel(
    x_hbm, gain_ref, w_hbm, key_ref, solved_ref, decay_ref, gamma_ref,
    out_ref,
    x_buf, xn_buf, w_buf, sems,
):
    found = copies(x_hbm, w_hbm, (0,), x_buf, w_buf, sems)
    normalise(found, x_buf, xn_buf, gain_ref[...])
    n = x_buf.shape[0]
    query = unit_rows(project(found, xn_buf, w_buf, 0))
    scores = mm3(split(query), split(key_ref[...]), NT) * decay_ref[...]
    seen = mm3(split(scores), split(solved_ref[...]))
    out_ref[:, :n] = gamma_ref[...] * query - seen[:, :n]
    out_ref[:, n:] = seen[:, n:]


def after(later, earlier, n):
    both = mm(later[:, :n], earlier)
    return both[:, :n], both[:, n:] + later[:, n:].astype(F32)


def own_half(ref):
    half = ref.shape[0] // 2
    return ref[pl.ds(pl.multiple_of(lax.axis_index("core") * half, half), half)]


def hold(held, place, near_ref, swap_ref):
    half = near_ref.shape[0]
    core = lax.axis_index("core")
    held[place, pl.ds(pl.multiple_of(core * half, half), half)] = near_ref[...]
    held[place, pl.ds(pl.multiple_of((1 - core) * half, half), half)] = swap_ref[...]


def pair_kernel(own_ref, other_ref, out_ref, half_ref):
    n = own_ref.shape[0]
    first = lax.axis_index("core") == 0
    own, other = own_ref[...], other_ref[...]
    earlier = jnp.where(first, own, other)
    later = jnp.where(first, other, own)
    a, b = after(later, earlier, n)
    out_ref[:, :n] = a.astype(BF16)
    out_ref[:, n:] = b.astype(BF16)
    half_ref[...] = own_half(out_ref)


def row_kernel(own_ref, *refs):
    near, swapped, (half_ref, prefix_ref, held, total_ref) = refs[:3], refs[3:6], refs[6:]
    n = own_ref.shape[0]
    place = lax.axis_index("xh") * 2 + lax.axis_index("xl")
    held[place] = own_ref[...]
    for shift, ref, swap in zip((1, 2, 3), near, swapped):
        hold(held, (place + (4 - shift)) % 4, ref, swap)

    def joined(later, earlier):
        a, b = after(later, earlier, n)
        return jnp.concatenate([a, b], axis=1).astype(BF16)

    low = joined(held[1], held[0])
    high = joined(held[3], held[2])
    a, b = after(high, low, n)
    total_ref[:, :n] = a.astype(BF16)
    total_ref[:, n:] = b.astype(BF16)
    half_ref[...] = own_half(total_ref)

    @pl.when(place == 0)
    def _():
        prefix_ref[...] = jnp.zeros_like(prefix_ref)

    @pl.when(place == 1)
    def _():
        prefix_ref[...] = held[0]

    @pl.when(place == 2)
    def _():
        prefix_ref[...] = low

    @pl.when(place == 3)
    def _():
        prefix_ref[...] = joined(held[2], low)


def read_kernel(*refs):
    near, swapped = refs[:3], refs[3:6]
    prefix_ref, other_ref, look_ref, gain_ref, out_ref, held, state = refs[6:]
    n = look_ref.shape[0]
    place = lax.axis_index("yh") * 2 + lax.axis_index("yl")
    for shift, ref, swap in zip((1, 2, 3), near, swapped):
        hold(held, (place + (4 - shift)) % 4, ref, swap)

    def push(pair, value):
        hi, lo = split(value)
        return mm(pair[:, :n], hi) + mm(pair[:, :n], lo) + pair[:, n:].astype(F32)

    @pl.when(place == 0)
    def _():
        state[...] = jnp.zeros_like(state)

    @pl.when(place > 0)
    def _():
        state[...] = held[0, :, n:].astype(F32)

    for turn in (1, 2):
        @pl.when(place > turn)
        def _():
            state[...] = push(held[turn], state[...])

    @pl.when(lax.axis_index("xh") + lax.axis_index("xl") > 0)
    def _():
        state[...] = push(prefix_ref[...], state[...])

    @pl.when(lax.axis_index("core") > 0)
    def _():
        state[...] = push(other_ref[...], state[...])

    read = look_ref[:, n:] + mm3(split(look_ref[:, :n]), split(state[...]))
    read = read * lax.rsqrt(jnp.mean(read * read, axis=-1, keepdims=True) + 1e-06)
    flat = (read * gain_ref[...]).astype(BF16)
    for copy in range(out_ref.shape[0]):
        out_ref[copy] = flat


def column_block():
    return lax.axis_index("yl") * 2 + lax.axis_index("xl")


def take_kernel(whole_ref, out_ref, sem):
    width = out_ref.shape[1]
    columns = pl.ds(pl.multiple_of(column_block() * width, width), width)
    copy = pltpu.make_async_copy(whole_ref.at[:, columns], out_ref, sem)
    copy.start()
    copy.wait()


def mix_kernel(
    own_ref, other_ref, mine_ref, one_ref, two_ref, three_ref, four_ref, keep_ref, send_ref, total
):
    core, here, head = lax.axis_index("core"), column_block(), lax.axis_index("head")
    kept = keep_ref.shape[0]
    width = four_ref.shape[1]

    def rows(steps):
        source = (head + (2 * core - 1) * steps + 8) % 8
        block = [ref[here ^ k, source] for ref in (own_ref, other_ref) for k in range(4)]
        return jnp.concatenate(block, axis=0)

    total[...] = mm(rows(1), one_ref[...]) + mm(rows(2), two_ref[...]) + mm(rows(3), three_ref[...])

    @pl.when(core == 0)
    def _():
        total[...] = total[...] + mm(rows(0), mine_ref[...])

    part = pl.ds(pl.multiple_of(core * width, width), width)
    total[:, part] = total[:, part] + mm(rows(4), four_ref[...])
    keep_ref[...] = total[:kept]
    send_ref[...] = total[kept:].astype(BF16)


def add_kernel(keep_ref, come_ref, *outs):
    total = (keep_ref[...] + come_ref[...].astype(F32)).astype(BF16)
    rows = outs[0].shape[0]
    for k, ref in enumerate(outs):
        ref[...] = total[k * rows : (k + 1) * rows]


def lay_kernel(*refs):
    pieces, out_ref = refs[:-1], refs[-1]
    width = pieces[0].shape[1]
    here = column_block()
    for k, ref in enumerate(pieces):
        out_ref[:, pl.ds(pl.multiple_of((here ^ k) * width, width), width)] = ref[...]


def hbm():
    return pl.BlockSpec(memory_space=pltpu.HBM)


def vmem():
    return pl.BlockSpec(memory_space=pltpu.VMEM)


def per_device(
    frames, norm_gain, qkv_weight, gate_weight, beta_scale, decay_rate, resets, out_gain, out_weight
):
    rows, width = frames.shape
    n = qkv_weight.shape[2]
    weight = qkv_weight.transpose(1, 0, 2)
    gate = gate_weight.transpose(2, 1, 0).reshape(2, width)
    square = jax.ShapeDtypeStruct((rows, n), F32)
    gain = norm_gain.reshape(1, width)

    def buffers(matrices):
        return [
            pltpu.VMEM((rows, width), BF16),
            pltpu.VMEM((rows, width), BF16),
            pltpu.VMEM((matrices, width, n), BF16),
            pltpu.SemaphoreType.DMA((2 + 2 * matrices,)),
        ]

    carry, key, solved, decay, gamma = pl.pallas_call(
        fold_kernel,
        name="fold",
        in_specs=[hbm()] * 7,
        out_specs=[vmem()] + [hbm()] * 4,
        out_shape=[
            jax.ShapeDtypeStruct((n, 2 * n), BF16),
            square,
            jax.ShapeDtypeStruct((rows, 2 * n), F32),
            square,
            jax.ShapeDtypeStruct((rows, 1), F32),
        ],
        scratch_shapes=buffers(2)
        + [
            pltpu.SMEM((1,), F32),
            pltpu.SMEM((1,), F32),
            pltpu.VMEM((1, width), F32),
            pltpu.VMEM((2, width), BF16),
            pltpu.VMEM((1, rows), jnp.int32),
            pltpu.SemaphoreType.DMA((5,)),
            pltpu.VMEM((rows, n), F32),
            pltpu.VMEM((rows, 2 * n), F32),
            pltpu.VMEM((rows, n), F32),
            pltpu.VMEM((rows, 1), F32),
            pltpu.SemaphoreType.DMA((4,)),
        ],
        compiler_params=LARGE,
    )(beta_scale, decay_rate, frames, gain, weight, gate, resets.reshape(1, rows))

    def look():
        return pl.pallas_call(
            look_kernel,
            name="look",
            in_specs=[hbm(), vmem(), hbm()] + [vmem()] * 4,
            out_specs=vmem(),
            out_shape=jax.ShapeDtypeStruct((rows, 2 * n), F32),
            scratch_shapes=buffers(1),
            compiler_params=LARGE,
            cost_estimate=pl.CostEstimate(
                flops=4 * rows * width * n, bytes_accessed=16 << 20, transcendentals=0
            ),
        )(frames, gain, weight, key, solved, decay, gamma)

    count = 32

    def moved(value, place_of):
        return lax.ppermute(value, SEQ, [(i, place_of(i)) for i in range(count)])

    def along_x(shift):
        return lambda i: (i // 8) * 8 + (i + 2 * shift) % 8

    def along_y(shift):
        return lambda i: (i + 8 * shift) % 32

    def flip(bits):
        return lambda i: i ^ bits

    def around(value):
        up = [(z, (z + 1) % 8) for z in range(8)]
        down = [(8 + z, 8 + (z + 7) % 8) for z in range(8)]
        return lax.ppermute(value, ("core", "head"), up + down)

    def later(value, gate):
        return lax.optimization_barrier((value, gate))[0]

    wide = out_weight.shape[1] // 4
    mine = pl.pallas_call(
        take_kernel,
        name="take",
        in_specs=[hbm()],
        out_specs=vmem(),
        out_shape=jax.ShapeDtypeStruct((n, wide), BF16),
        scratch_shapes=[pltpu.SemaphoreType.DMA],
        compiler_params=LARGE,
    )(out_weight)
    one = around(mine)

    pair_shape = jax.ShapeDtypeStruct((n, 2 * n), BF16)
    half_shape = jax.ShapeDtypeStruct((n // 2, 2 * n), BF16)
    other = moved(carry, flip(1))
    two = around(later(one, other))
    pair, half = pl.pallas_call(
        pair_kernel,
        name="pair",
        in_specs=[vmem()] * 2,
        out_specs=[vmem()] * 2,
        out_shape=[pair_shape, half_shape],
        compiler_params=SMALL,
    )(carry, other)
    near = [moved(half, along_x(s)) for s in (1, 2, 3)]
    near, looked = lax.optimization_barrier((near, look()))
    three = around(later(two, near))
    swapped = [moved(value, flip(1)) for value in near]
    half, prefix = pl.pallas_call(
        row_kernel,
        name="row",
        in_specs=[vmem()] * 7,
        out_specs=[vmem()] * 2,
        out_shape=[half_shape, pair_shape],
        scratch_shapes=[pltpu.VMEM((4, n, 2 * n), BF16), pltpu.VMEM((n, 2 * n), BF16)],
        compiler_params=SMALL,
    )(pair, *near, *swapped)
    near = [moved(half, along_y(s)) for s in (1, 2, 3)]
    part_three = lax.dynamic_slice_in_dim(
        three, lax.axis_index("core") * (wide // 2), wide // 2, 1
    )
    four = around(later(part_three, near))
    swapped = [moved(value, flip(1)) for value in near]
    flat = pl.pallas_call(
        read_kernel,
        name="read",
        in_specs=[vmem()] * 10,
        out_specs=vmem(),
        out_shape=jax.ShapeDtypeStruct((4, rows, n), BF16),
        scratch_shapes=[pltpu.VMEM((4, n, 2 * n), BF16), pltpu.VMEM((n, n), F32)],
        compiler_params=SMALL,
    )(*near, *swapped, prefix, other, looked, out_gain.reshape(1, n))
    part = rows // 8
    flat, four = lax.optimization_barrier((flat, four))
    reads = lax.all_to_all(
        flat.reshape(32, part, n), ("yl", "xl", "head"), 0, 0, tiled=True
    ).reshape(4, 8, part, n)
    beside = moved(reads, flip(1))
    keep, send = pl.pallas_call(
        mix_kernel,
        name="mix",
        in_specs=[vmem()] * 7,
        out_specs=[vmem()] * 2,
        out_shape=[
            jax.ShapeDtypeStruct((4 * part, wide), F32),
            jax.ShapeDtypeStruct((4 * part, wide), BF16),
        ],
        scratch_shapes=[pltpu.VMEM((8 * part, wide), F32)],
        compiler_params=MIDDLE,
    )(reads, beside, mine, one, two, three, four)
    piece = jax.ShapeDtypeStruct((part, wide), BF16)
    kept, to_x, to_y, to_both = pl.pallas_call(
        add_kernel,
        name="add",
        in_specs=[vmem()] * 2,
        out_specs=[vmem()] * 4,
        out_shape=[piece] * 4,
        compiler_params=SMALL,
    )(keep, moved(send, flip(1)))
    return pl.pallas_call(
        lay_kernel,
        name="lay",
        in_specs=[vmem()] * 4,
        out_specs=vmem(),
        out_shape=jax.ShapeDtypeStruct((part, 4 * wide), BF16),
        compiler_params=SMALL,
    )(kept, moved(to_x, flip(2)), moved(to_y, flip(8)), moved(to_both, flip(10)))


def solution(mesh):
    fine = Mesh(mesh.devices.reshape(2, 2, 2, 2, 2, 8), SEQ + ("head",))
    in_specs = (
        P(SEQ, None),
        P(),
        P(None, None, "head"),
        P(None, None, "head"),
        P("head"),
        P("head"),
        P(SEQ),
        P("head"),
        P("head", None),
    )
    out_specs = P(SEQ + ("head",), None)
    return jax.shard_map(
        per_device, mesh=fine, in_specs=in_specs, out_specs=out_specs, check_vma=False
    )
```

```python
import jax
import jax.numpy as jnp
from jax import lax
from jax.experimental import pallas as pl
from jax.experimental.pallas import tpu as pltpu
from jax.sharding import Mesh
from jax.sharding import PartitionSpec as P

F32 = jnp.float32
BF16 = jnp.bfloat16
NN = (((1,), (0,)), ((), ()))
NT = (((1,), (1,)), ((), ()))
TN = (((0,), (0,)), ((), ()))
SEQ = ("yh", "yl", "xh", "xl", "core")
SMALL = pltpu.CompilerParams(vmem_limit_bytes=8 << 20)
MIDDLE = pltpu.CompilerParams(vmem_limit_bytes=16 << 20)
LARGE = pltpu.CompilerParams(vmem_limit_bytes=58 << 20)


def mm(a, b, dims=NN):
    return lax.dot_general(a, b, dims, preferred_element_type=F32)


def split(a):
    hi = a.astype(BF16)
    return hi, (a - hi.astype(F32)).astype(BF16)


def mm3(a, b, dims=NN):
    (ah, al), (bh, bl) = a, b
    return mm(ah, bh, dims) + (mm(ah, bl, dims) + mm(al, bh, dims))


def unit_rows(vectors):
    return vectors * lax.rsqrt(jnp.sum(vectors * vectors, axis=-1, keepdims=True) + 1e-06)


def norm_rows(x_ref, gain):
    x = x_ref[...].astype(F32)
    rs = lax.rsqrt(jnp.mean(x * x, axis=-1, keepdims=True) + 1e-06)
    return (x * rs * gain).astype(BF16)


def copies(x_hbm, w_hbm, slots, x_buf, w_buf, sems):
    halves = x_buf.shape[0] // 2
    depth = w_buf.shape[1] // 2
    rows = [pl.ds(i * halves, halves) for i in range(2)]
    parts = [pl.ds(i * depth, depth) for i in range(2)]
    found = [(x_hbm.at[part], x_buf.at[part]) for part in rows]
    for slot, j in enumerate(slots):
        found += [(w_hbm.at[j, part], w_buf.at[slot, part]) for part in parts]
    found = [pltpu.make_async_copy(a, b, sems.at[i]) for i, (a, b) in enumerate(found)]
    for copy in found:
        copy.start()
    return found


def normalise(found, x_buf, xn_buf, gain):
    half = x_buf.shape[0] // 2
    for i in range(2):
        found[i].wait()
        part = slice(i * half, (i + 1) * half)
        xn_buf[part] = norm_rows(x_buf.at[part], gain)


def project(found, xn_buf, w_buf, slot):
    depth = w_buf.shape[1] // 2
    total = None
    for i in range(2):
        found[2 + 2 * slot + i].wait()
        part = slice(i * depth, (i + 1) * depth)
        product = mm(xn_buf[:, part], w_buf[slot, part])
        total = product if total is None else total + product
    return total


def fold_kernel(
    scale_hbm, rate_hbm, x_hbm, gain_hbm, w_hbm, gate_hbm, resets_hbm,
    carry_ref, key_hbm, solved_hbm, decay_hbm, gamma_hbm,
    x_buf, xn_buf, w_buf, sems, scale_ref, rate_ref, gain_ref, gate_ref, resets_ref, small_sems,
    key_ref, solved_ref, decay_ref, gamma_ref, out_sems,
):
    small = [
        pltpu.make_async_copy(a, b, small_sems.at[i])
        for i, (a, b) in enumerate(
            (
                (gain_hbm, gain_ref),
                (gate_hbm, gate_ref),
                (resets_hbm, resets_ref),
                (scale_hbm, scale_ref),
                (rate_hbm, rate_ref),
            )
        )
    ]
    for copy in small:
        copy.start()
    found = copies(x_hbm, w_hbm, (1, 2), x_buf, w_buf, sems)
    small[0].wait()
    normalise(found, x_buf, xn_buf, gain_ref[...])
    n = x_buf.shape[0]
    for copy in small[1:] + found[2:]:
        copy.wait()
    kept = []

    def keep(value, ref, target):
        ref[...] = value
        kept.append(pltpu.make_async_copy(ref, target, out_sems.at[len(kept)]))
        kept[-1].start()

    gating = mm(xn_buf[...], gate_ref[...], NT)
    key = unit_rows(mm(xn_buf[...], w_buf[0]))
    beta = scale_ref[0] * jax.nn.sigmoid(gating[:, 0:1])
    logf = -rate_ref[0] * jax.nn.softplus(gating[:, 1:2])
    reset_row = resets_ref[...].astype(F32)
    t = lax.broadcasted_iota(jnp.int32, (n, n), 0)
    s = lax.broadcasted_iota(jnp.int32, (n, n), 1)
    causal = t >= s
    eye = t == s

    def to_row(col):
        return jnp.sum(jnp.where(eye, col, 0.0), axis=0, keepdims=True)

    cum = jnp.sum(jnp.where(causal, to_row(logf), 0.0), axis=1, keepdims=True)
    seg = jnp.sum(jnp.where(causal, reset_row, 0.0), axis=1, keepdims=True)
    cum_row = to_row(cum)
    seg_row = to_row(seg)
    same = (seg == seg_row) & causal
    decay = jnp.where(same, jnp.exp(jnp.where(same, cum - cum_row, 0.0)), 0.0)
    gamma = jnp.where(seg == 0.0, jnp.exp(cum), 0.0)
    cum_last, seg_last = cum[n - 1 : n], seg[n - 1 : n]
    tail = jnp.where(seg == seg_last, jnp.exp(cum_last - cum), 0.0)
    gamma_last = gamma[n - 1 : n]
    keep(key, key_ref, key_hbm)
    keep(decay, decay_ref, decay_hbm)
    keep(gamma, gamma_ref, gamma_hbm)

    ks = split(key)
    low = jnp.where(t > s, beta * decay * mm3(ks, ks, NT), 0.0)
    apart = t ^ s
    inv = jnp.where(eye, 1.0, jnp.where(apart == 1, -low, 0.0))
    levels = range(1, n.bit_length() - 1)
    depth = xn_buf.shape[1] // (len(levels) + 1)
    value = mm(xn_buf[:, :depth], w_buf[1, :depth])
    for level in levels:
        part = jnp.where((apart >> level) == 1, low, 0.0).astype(BF16)
        rough = inv.astype(BF16)
        inner = mm(part, rough).astype(BF16)
        chunk = slice(level * depth, (level + 1) * depth)
        value = value + mm(xn_buf[:, chunk], w_buf[1, chunk])
        inv = inv - mm(rough, inner)
    vs = split(inv)
    left = jnp.where(eye, 1.0, 0.0) - inv - mm3(split(low), vs)
    inv = inv + mm(vs[0], left.astype(BF16))

    rhs = jnp.concatenate([(beta * gamma) * key, beta * value], axis=1)
    solved = mm3(split(inv), split(rhs))
    keep(solved, solved_ref, solved_hbm)
    folded = mm3(split(key * tail), split(solved), TN)
    carry_ref[:, :n] = (jnp.where(eye, gamma_last, 0.0) - folded[:, :n]).astype(BF16)
    carry_ref[:, n:] = folded[:, n:].astype(BF16)
    for copy in kept:
        copy.wait()


def look_kernel(
    x_hbm, gain_ref, w_hbm, key_ref, solved_ref, decay_ref, gamma_ref,
    out_ref,
    x_buf, xn_buf, w_buf, sems,
):
    found = copies(x_hbm, w_hbm, (0,), x_buf, w_buf, sems)
    normalise(found, x_buf, xn_buf, gain_ref[...])
    n = x_buf.shape[0]
    query = unit_rows(project(found, xn_buf, w_buf, 0))
    scores = mm3(split(query), split(key_ref[...]), NT) * decay_ref[...]
    seen = mm3(split(scores), split(solved_ref[...]))
    out_ref[:, :n] = gamma_ref[...] * query - seen[:, :n]
    out_ref[:, n:] = seen[:, n:]


def after(later, earlier, n):
    both = mm(later[:, :n], earlier)
    return both[:, :n], both[:, n:] + later[:, n:].astype(F32)


def own_half(ref):
    half = ref.shape[0] // 2
    return ref[pl.ds(pl.multiple_of(lax.axis_index("core") * half, half), half)]


def hold(held, place, near_ref, swap_ref):
    half = near_ref.shape[0]
    core = lax.axis_index("core")
    held[place, pl.ds(pl.multiple_of(core * half, half), half)] = near_ref[...]
    held[place, pl.ds(pl.multiple_of((1 - core) * half, half), half)] = swap_ref[...]


def pair_kernel(own_ref, other_ref, out_ref, half_ref):
    n = own_ref.shape[0]
    first = lax.axis_index("core") == 0
    own, other = own_ref[...], other_ref[...]
    earlier = jnp.where(first, own, other)
    later = jnp.where(first, other, own)
    a, b = after(later, earlier, n)
    out_ref[:, :n] = a.astype(BF16)
    out_ref[:, n:] = b.astype(BF16)
    half_ref[...] = own_half(out_ref)


def row_kernel(own_ref, *refs):
    near, swapped, (half_ref, prefix_ref, held, total_ref) = refs[:3], refs[3:6], refs[6:]
    n = own_ref.shape[0]
    place = lax.axis_index("xh") * 2 + lax.axis_index("xl")
    held[place] = own_ref[...]
    for shift, ref, swap in zip((1, 2, 3), near, swapped):
        hold(held, (place + (4 - shift)) % 4, ref, swap)

    def joined(later, earlier):
        a, b = after(later, earlier, n)
        return jnp.concatenate([a, b], axis=1).astype(BF16)

    low = joined(held[1], held[0])
    high = joined(held[3], held[2])
    a, b = after(high, low, n)
    total_ref[:, :n] = a.astype(BF16)
    total_ref[:, n:] = b.astype(BF16)
    half_ref[...] = own_half(total_ref)

    @pl.when(place == 0)
    def _():
        prefix_ref[...] = jnp.zeros_like(prefix_ref)

    @pl.when(place == 1)
    def _():
        prefix_ref[...] = held[0]

    @pl.when(place == 2)
    def _():
        prefix_ref[...] = low

    @pl.when(place == 3)
    def _():
        prefix_ref[...] = joined(held[2], low)


def read_kernel(*refs):
    near, swapped = refs[:3], refs[3:6]
    prefix_ref, other_ref, look_ref, gain_ref, out_ref, held, state = refs[6:]
    n = look_ref.shape[0]
    place = lax.axis_index("yh") * 2 + lax.axis_index("yl")
    for shift, ref, swap in zip((1, 2, 3), near, swapped):
        hold(held, (place + (4 - shift)) % 4, ref, swap)

    def push(pair, value):
        hi, lo = split(value)
        return mm(pair[:, :n], hi) + mm(pair[:, :n], lo) + pair[:, n:].astype(F32)

    @pl.when(place == 0)
    def _():
        state[...] = jnp.zeros_like(state)

    @pl.when(place > 0)
    def _():
        state[...] = held[0, :, n:].astype(F32)

    for turn in (1, 2):
        @pl.when(place > turn)
        def _():
            state[...] = push(held[turn], state[...])

    @pl.when(lax.axis_index("xh") + lax.axis_index("xl") > 0)
    def _():
        state[...] = push(prefix_ref[...], state[...])

    @pl.when(lax.axis_index("core") > 0)
    def _():
        state[...] = push(other_ref[...], state[...])

    read = look_ref[:, n:] + mm3(split(look_ref[:, :n]), split(state[...]))
    read = read * lax.rsqrt(jnp.mean(read * read, axis=-1, keepdims=True) + 1e-06)
    flat = (read * gain_ref[...]).astype(BF16)
    for copy in range(out_ref.shape[0]):
        out_ref[copy] = flat


def column_block():
    return lax.axis_index("yl") * 2 + lax.axis_index("xl")


def take_kernel(whole_ref, out_ref, sem):
    width = out_ref.shape[1]
    columns = pl.ds(pl.multiple_of(column_block() * width, width), width)
    copy = pltpu.make_async_copy(whole_ref.at[:, columns], out_ref, sem)
    copy.start()
    copy.wait()


def mix_kernel(
    own_ref, other_ref, mine_ref, one_ref, two_ref, three_ref, four_ref, keep_ref, send_ref, total
):
    core, here, head = lax.axis_index("core"), column_block(), lax.axis_index("head")
    kept = keep_ref.shape[0]
    width = four_ref.shape[1]

    def rows(steps):
        source = (head + (2 * core - 1) * steps + 8) % 8
        block = [ref[here ^ k, source] for ref in (own_ref, other_ref) for k in range(4)]
        return jnp.concatenate(block, axis=0)

    total[...] = mm(rows(1), one_ref[...]) + mm(rows(2), two_ref[...]) + mm(rows(3), three_ref[...])

    @pl.when(core == 0)
    def _():
        total[...] = total[...] + mm(rows(0), mine_ref[...])

    part = pl.ds(pl.multiple_of(core * width, width), width)
    total[:, part] = total[:, part] + mm(rows(4), four_ref[...])
    keep_ref[...] = total[:kept]
    send_ref[...] = total[kept:].astype(BF16)


def add_kernel(keep_ref, come_ref, *outs):
    total = (keep_ref[...] + come_ref[...].astype(F32)).astype(BF16)
    rows = outs[0].shape[0]
    for k, ref in enumerate(outs):
        ref[...] = total[k * rows : (k + 1) * rows]


def lay_kernel(*refs):
    pieces, out_ref = refs[:-1], refs[-1]
    width = pieces[0].shape[1]
    here = column_block()
    for k, ref in enumerate(pieces):
        out_ref[:, pl.ds(pl.multiple_of((here ^ k) * width, width), width)] = ref[...]


def hbm():
    return pl.BlockSpec(memory_space=pltpu.HBM)


def vmem():
    return pl.BlockSpec(memory_space=pltpu.VMEM)


def per_device(
    frames, norm_gain, qkv_weight, gate_weight, beta_scale, decay_rate, resets, out_gain, out_weight
):
    rows, width = frames.shape
    n = qkv_weight.shape[2]
    weight = qkv_weight.transpose(1, 0, 2)
    gate = gate_weight.transpose(2, 1, 0).reshape(2, width)
    square = jax.ShapeDtypeStruct((rows, n), F32)
    gain = norm_gain.reshape(1, width)

    def buffers(matrices):
        return [
            pltpu.VMEM((rows, width), BF16),
            pltpu.VMEM((rows, width), BF16),
            pltpu.VMEM((matrices, width, n), BF16),
            pltpu.SemaphoreType.DMA((2 + 2 * matrices,)),
        ]

    carry, key, solved, decay, gamma = pl.pallas_call(
        fold_kernel,
        name="fold",
        in_specs=[hbm()] * 7,
        out_specs=[vmem()] + [hbm()] * 4,
        out_shape=[
            jax.ShapeDtypeStruct((n, 2 * n), BF16),
            square,
            jax.ShapeDtypeStruct((rows, 2 * n), F32),
            square,
            jax.ShapeDtypeStruct((rows, 1), F32),
        ],
        scratch_shapes=buffers(2)
        + [
            pltpu.SMEM((1,), F32),
            pltpu.SMEM((1,), F32),
            pltpu.VMEM((1, width), F32),
            pltpu.VMEM((2, width), BF16),
            pltpu.VMEM((1, rows), jnp.int32),
            pltpu.SemaphoreType.DMA((5,)),
            pltpu.VMEM((rows, n), F32),
            pltpu.VMEM((rows, 2 * n), F32),
            pltpu.VMEM((rows, n), F32),
            pltpu.VMEM((rows, 1), F32),
            pltpu.SemaphoreType.DMA((4,)),
        ],
        compiler_params=LARGE,
    )(beta_scale, decay_rate, frames, gain, weight, gate, resets.reshape(1, rows))

    def look():
        return pl.pallas_call(
            look_kernel,
            name="look",
            in_specs=[hbm(), vmem(), hbm()] + [vmem()] * 4,
            out_specs=vmem(),
            out_shape=jax.ShapeDtypeStruct((rows, 2 * n), F32),
            scratch_shapes=buffers(1),
            compiler_params=LARGE,
            cost_estimate=pl.CostEstimate(
                flops=4 * rows * width * n, bytes_accessed=16 << 20, transcendentals=0
            ),
        )(frames, gain, weight, key, solved, decay, gamma)

    count = 32

    def moved(value, place_of):
        return lax.ppermute(value, SEQ, [(i, place_of(i)) for i in range(count)])

    def along_x(shift):
        return lambda i: (i // 8) * 8 + (i + 2 * shift) % 8

    def along_y(shift):
        return lambda i: (i + 8 * shift) % 32

    def flip(bits):
        return lambda i: i ^ bits

    def around(value, steps):
        up = [(z, (z + steps) % 8) for z in range(8)]
        down = [(8 + z, 8 + (z + 8 - steps) % 8) for z in range(8)]
        return lax.ppermute(value, ("core", "head"), up + down)

    def later(value, gate):
        return lax.optimization_barrier((value, gate))[0]

    wide = out_weight.shape[1] // 4
    mine = pl.pallas_call(
        take_kernel,
        name="take",
        in_specs=[hbm()],
        out_specs=vmem(),
        out_shape=jax.ShapeDtypeStruct((n, wide), BF16),
        scratch_shapes=[pltpu.SemaphoreType.DMA],
        compiler_params=LARGE,
    )(out_weight)
    one = around(mine, 1)
    two = around(mine, 2)

    pair_shape = jax.ShapeDtypeStruct((n, 2 * n), BF16)
    half_shape = jax.ShapeDtypeStruct((n // 2, 2 * n), BF16)
    other = moved(carry, flip(1))
    pair, half = pl.pallas_call(
        pair_kernel,
        name="pair",
        in_specs=[vmem()] * 2,
        out_specs=[vmem()] * 2,
        out_shape=[pair_shape, half_shape],
        compiler_params=SMALL,
    )(carry, other)
    near = [moved(half, along_x(s)) for s in (1, 2, 3)]
    near, looked = lax.optimization_barrier((near, look()))
    ready = later(two, near)
    three = around(ready, 1)
    part_two = lax.dynamic_slice_in_dim(
        ready, lax.axis_index("core") * (wide // 2), wide // 2, 1
    )
    four = around(part_two, 2)
    swapped = [moved(value, flip(1)) for value in near]
    half, prefix = pl.pallas_call(
        row_kernel,
        name="row",
        in_specs=[vmem()] * 7,
        out_specs=[vmem()] * 2,
        out_shape=[half_shape, pair_shape],
        scratch_shapes=[pltpu.VMEM((4, n, 2 * n), BF16), pltpu.VMEM((n, 2 * n), BF16)],
        compiler_params=SMALL,
    )(pair, *near, *swapped)
    near = [moved(half, along_y(s)) for s in (1, 2, 3)]
    near, three, four = lax.optimization_barrier((near, three, four))
    swapped = [moved(value, flip(1)) for value in near]
    flat = pl.pallas_call(
        read_kernel,
        name="read",
        in_specs=[vmem()] * 10,
        out_specs=vmem(),
        out_shape=jax.ShapeDtypeStruct((4, rows, n), BF16),
        scratch_shapes=[pltpu.VMEM((4, n, 2 * n), BF16), pltpu.VMEM((n, n), F32)],
        compiler_params=SMALL,
    )(*near, *swapped, prefix, other, looked, out_gain.reshape(1, n))
    part = rows // 8
    reads = lax.all_to_all(
        flat.reshape(32, part, n), ("yl", "xl", "head"), 0, 0, tiled=True
    ).reshape(4, 8, part, n)
    beside = moved(reads, flip(1))
    keep, send = pl.pallas_call(
        mix_kernel,
        name="mix",
        in_specs=[vmem()] * 7,
        out_specs=[vmem()] * 2,
        out_shape=[
            jax.ShapeDtypeStruct((4 * part, wide), F32),
            jax.ShapeDtypeStruct((4 * part, wide), BF16),
        ],
        scratch_shapes=[pltpu.VMEM((8 * part, wide), F32)],
        compiler_params=MIDDLE,
    )(reads, beside, mine, one, two, three, four)
    piece = jax.ShapeDtypeStruct((part, wide), BF16)
    kept, to_x, to_y, to_both = pl.pallas_call(
        add_kernel,
        name="add",
        in_specs=[vmem()] * 2,
        out_specs=[vmem()] * 4,
        out_shape=[piece] * 4,
        compiler_params=SMALL,
    )(keep, moved(send, flip(1)))
    return pl.pallas_call(
        lay_kernel,
        name="lay",
        in_specs=[vmem()] * 4,
        out_specs=vmem(),
        out_shape=jax.ShapeDtypeStruct((part, 4 * wide), BF16),
        compiler_params=SMALL,
    )(kept, moved(to_x, flip(2)), moved(to_y, flip(8)), moved(to_both, flip(10)))


def solution(mesh):
    fine = Mesh(mesh.devices.reshape(2, 2, 2, 2, 2, 8), SEQ + ("head",))
    in_specs = (
        P(SEQ, None),
        P(),
        P(None, None, "head"),
        P(None, None, "head"),
        P("head"),
        P("head"),
        P(SEQ),
        P("head"),
        P("head", None),
    )
    out_specs = P(SEQ + ("head",), None)
    return jax.shard_map(
        per_device, mesh=fine, in_specs=in_specs, out_specs=out_specs, check_vma=False
    )
```

```python
import jax
import jax.numpy as jnp
from jax import lax
from jax.experimental import pallas as pl
from jax.experimental.pallas import tpu as pltpu
from jax.sharding import Mesh
from jax.sharding import PartitionSpec as P

F32 = jnp.float32
BF16 = jnp.bfloat16
NN = (((1,), (0,)), ((), ()))
NT = (((1,), (1,)), ((), ()))
TN = (((0,), (0,)), ((), ()))
SEQ = ("yh", "yl", "xh", "xl", "core")
SMALL = pltpu.CompilerParams(vmem_limit_bytes=8 << 20)
MIDDLE = pltpu.CompilerParams(vmem_limit_bytes=16 << 20)
LARGE = pltpu.CompilerParams(vmem_limit_bytes=52 << 20)


def mm(a, b, dims=NN):
    return lax.dot_general(a, b, dims, preferred_element_type=F32)


def split(a):
    hi = a.astype(BF16)
    return hi, (a - hi.astype(F32)).astype(BF16)


def mm3(a, b, dims=NN):
    (ah, al), (bh, bl) = a, b
    return mm(ah, bh, dims) + (mm(ah, bl, dims) + mm(al, bh, dims))


def unit_rows(vectors):
    return vectors * lax.rsqrt(jnp.sum(vectors * vectors, axis=-1, keepdims=True) + 1e-06)


def norm_rows(x_ref, gain):
    x = x_ref[...].astype(F32)
    rs = lax.rsqrt(jnp.mean(x * x, axis=-1, keepdims=True) + 1e-06)
    return (x * rs * gain).astype(BF16)


def copies(x_hbm, w_hbm, slots, x_buf, w_buf, sems):
    halves = x_buf.shape[0] // 2
    depth = w_buf.shape[1] // 2
    rows = [pl.ds(i * halves, halves) for i in range(2)]
    parts = [pl.ds(i * depth, depth) for i in range(2)]
    found = [(x_hbm.at[part], x_buf.at[part]) for part in rows]
    for slot, j in enumerate(slots):
        found += [(w_hbm.at[j, part], w_buf.at[slot, part]) for part in parts]
    found = [pltpu.make_async_copy(a, b, sems.at[i]) for i, (a, b) in enumerate(found)]
    for copy in found:
        copy.start()
    return found


def normalise(found, x_buf, xn_buf, gain):
    half = x_buf.shape[0] // 2
    for i in range(2):
        found[i].wait()
        part = slice(i * half, (i + 1) * half)
        xn_buf[part] = norm_rows(x_buf.at[part], gain)


def project(found, xn_buf, w_buf, slot):
    depth = w_buf.shape[1] // 2
    total = None
    for i in range(2):
        found[2 + 2 * slot + i].wait()
        part = slice(i * depth, (i + 1) * depth)
        product = mm(xn_buf[:, part], w_buf[slot, part])
        total = product if total is None else total + product
    return total


def fold_kernel(
    scale_hbm, rate_hbm, x_hbm, gain_hbm, w_hbm, gate_hbm, resets_hbm,
    carry_ref, key_hbm, solved_hbm, decay_hbm, gamma_hbm,
    x_buf, xn_buf, w_buf, sems, scale_ref, rate_ref, gain_ref, gate_ref, resets_ref, small_sems,
    key_ref, solved_ref, decay_ref, gamma_ref, out_sems,
):
    small = [
        pltpu.make_async_copy(a, b, small_sems.at[i])
        for i, (a, b) in enumerate(
            (
                (gain_hbm, gain_ref),
                (gate_hbm, gate_ref),
                (resets_hbm, resets_ref),
                (scale_hbm, scale_ref),
                (rate_hbm, rate_ref),
            )
        )
    ]
    for copy in small:
        copy.start()
    found = copies(x_hbm, w_hbm, (1, 2), x_buf, w_buf, sems)
    small[0].wait()
    normalise(found, x_buf, xn_buf, gain_ref[...])
    n = x_buf.shape[0]
    for copy in small[1:] + found[2:]:
        copy.wait()
    kept = []

    def keep(value, ref, target):
        ref[...] = value
        kept.append(pltpu.make_async_copy(ref, target, out_sems.at[len(kept)]))
        kept[-1].start()

    gating = mm(xn_buf[...], gate_ref[...], NT)
    key = unit_rows(mm(xn_buf[...], w_buf[0]))
    beta = scale_ref[0] * jax.nn.sigmoid(gating[:, 0:1])
    logf = -rate_ref[0] * jax.nn.softplus(gating[:, 1:2])
    reset_row = resets_ref[...].astype(F32)
    t = lax.broadcasted_iota(jnp.int32, (n, n), 0)
    s = lax.broadcasted_iota(jnp.int32, (n, n), 1)
    causal = t >= s
    eye = t == s

    def to_row(col):
        return jnp.sum(jnp.where(eye, col, 0.0), axis=0, keepdims=True)

    cum = jnp.sum(jnp.where(causal, to_row(logf), 0.0), axis=1, keepdims=True)
    seg = jnp.sum(jnp.where(causal, reset_row, 0.0), axis=1, keepdims=True)
    cum_row = to_row(cum)
    seg_row = to_row(seg)
    same = (seg == seg_row) & causal
    decay = jnp.where(same, jnp.exp(jnp.where(same, cum - cum_row, 0.0)), 0.0)
    gamma = jnp.where(seg == 0.0, jnp.exp(cum), 0.0)
    cum_last, seg_last = cum[n - 1 : n], seg[n - 1 : n]
    tail = jnp.where(seg == seg_last, jnp.exp(cum_last - cum), 0.0)
    gamma_last = gamma[n - 1 : n]
    keep(key, key_ref, key_hbm)
    keep(decay, decay_ref, decay_hbm)
    keep(gamma, gamma_ref, gamma_hbm)

    ks = split(key)
    low = jnp.where(t > s, beta * decay * mm3(ks, ks, NT), 0.0)
    apart = t ^ s
    inv = jnp.where(eye, 1.0, jnp.where(apart == 1, -low, 0.0))
    levels = range(1, n.bit_length() - 1)
    depth = xn_buf.shape[1] // (len(levels) + 1)
    value = mm(xn_buf[:, :depth], w_buf[1, :depth])
    for level in levels:
        part = jnp.where((apart >> level) == 1, low, 0.0).astype(BF16)
        rough = inv.astype(BF16)
        inner = mm(part, rough).astype(BF16)
        chunk = slice(level * depth, (level + 1) * depth)
        value = value + mm(xn_buf[:, chunk], w_buf[1, chunk])
        inv = inv - mm(rough, inner)
    vs = split(inv)
    left = jnp.where(eye, 1.0, 0.0) - inv - mm3(split(low), vs)
    inv = inv + mm(vs[0], left.astype(BF16))

    rhs = jnp.concatenate([(beta * gamma) * key, beta * value], axis=1)
    solved = mm3(split(inv), split(rhs))
    keep(solved, solved_ref, solved_hbm)
    folded = mm3(split(key * tail), split(solved), TN)
    carry_ref[:, :n] = (jnp.where(eye, gamma_last, 0.0) - folded[:, :n]).astype(BF16)
    carry_ref[:, n:] = folded[:, n:].astype(BF16)
    for copy in kept:
        copy.wait()


def look_kernel(
    x_hbm, gain_ref, w_hbm, key_ref, solved_ref, decay_ref, gamma_ref,
    out_ref,
    x_buf, xn_buf, w_buf, sems,
):
    found = copies(x_hbm, w_hbm, (0,), x_buf, w_buf, sems)
    normalise(found, x_buf, xn_buf, gain_ref[...])
    n = x_buf.shape[0]
    query = unit_rows(project(found, xn_buf, w_buf, 0))
    scores = mm3(split(query), split(key_ref[...]), NT) * decay_ref[...]
    seen = mm3(split(scores), split(solved_ref[...]))
    out_ref[:, :n] = gamma_ref[...] * query - seen[:, :n]
    out_ref[:, n:] = seen[:, n:]


def after(later, earlier, n):
    both = mm(later[:, :n], earlier)
    return both[:, :n], both[:, n:] + later[:, n:].astype(F32)


def own_half(ref):
    half = ref.shape[0] // 2
    return ref[pl.ds(pl.multiple_of(lax.axis_index("core") * half, half), half)]


def hold(held, place, near_ref, swap_ref):
    half = near_ref.shape[0]
    core = lax.axis_index("core")
    held[place, pl.ds(pl.multiple_of(core * half, half), half)] = near_ref[...]
    held[place, pl.ds(pl.multiple_of((1 - core) * half, half), half)] = swap_ref[...]


def pair_kernel(own_ref, other_ref, out_ref, half_ref):
    n = own_ref.shape[0]
    first = lax.axis_index("core") == 0
    own, other = own_ref[...], other_ref[...]
    earlier = jnp.where(first, own, other)
    later = jnp.where(first, other, own)
    a, b = after(later, earlier, n)
    out_ref[:, :n] = a.astype(BF16)
    out_ref[:, n:] = b.astype(BF16)
    half_ref[...] = own_half(out_ref)


def row_kernel(own_ref, *refs):
    near, swapped, (half_ref, prefix_ref, held, total_ref) = refs[:3], refs[3:6], refs[6:]
    n = own_ref.shape[0]
    place = lax.axis_index("xh") * 2 + lax.axis_index("xl")
    held[place] = own_ref[...]
    for shift, ref, swap in zip((1, 2, 3), near, swapped):
        hold(held, (place + (4 - shift)) % 4, ref, swap)

    def joined(later, earlier):
        a, b = after(later, earlier, n)
        return jnp.concatenate([a, b], axis=1).astype(BF16)

    low = joined(held[1], held[0])
    high = joined(held[3], held[2])
    a, b = after(high, low, n)
    total_ref[:, :n] = a.astype(BF16)
    total_ref[:, n:] = b.astype(BF16)
    half_ref[...] = own_half(total_ref)

    @pl.when(place == 0)
    def _():
        prefix_ref[...] = jnp.zeros_like(prefix_ref)

    @pl.when(place == 1)
    def _():
        prefix_ref[...] = held[0]

    @pl.when(place == 2)
    def _():
        prefix_ref[...] = low

    @pl.when(place == 3)
    def _():
        prefix_ref[...] = joined(held[2], low)


def read_kernel(*refs):
    near, swapped = refs[:3], refs[3:6]
    prefix_ref, other_ref, look_ref, gain_ref, out_ref, held, state = refs[6:]
    n = look_ref.shape[0]
    place = lax.axis_index("yh") * 2 + lax.axis_index("yl")
    for shift, ref, swap in zip((1, 2, 3), near, swapped):
        hold(held, (place + (4 - shift)) % 4, ref, swap)

    def push(pair, value):
        hi, lo = split(value)
        return mm(pair[:, :n], hi) + mm(pair[:, :n], lo) + pair[:, n:].astype(F32)

    @pl.when(place == 0)
    def _():
        state[...] = jnp.zeros_like(state)

    @pl.when(place > 0)
    def _():
        state[...] = held[0, :, n:].astype(F32)

    for turn in (1, 2):
        @pl.when(place > turn)
        def _():
            state[...] = push(held[turn], state[...])

    @pl.when(lax.axis_index("xh") + lax.axis_index("xl") > 0)
    def _():
        state[...] = push(prefix_ref[...], state[...])

    @pl.when(lax.axis_index("core") > 0)
    def _():
        state[...] = push(other_ref[...], state[...])

    read = look_ref[:, n:] + mm3(split(look_ref[:, :n]), split(state[...]))
    read = read * lax.rsqrt(jnp.mean(read * read, axis=-1, keepdims=True) + 1e-06)
    flat = (read * gain_ref[...]).astype(BF16)
    for copy in range(out_ref.shape[0]):
        out_ref[copy] = flat


def column_block():
    return lax.axis_index("yl") * 2 + lax.axis_index("xl")


def take_kernel(whole_ref, out_ref, sem):
    width = out_ref.shape[1]
    columns = pl.ds(pl.multiple_of(column_block() * width, width), width)
    copy = pltpu.make_async_copy(whole_ref.at[:, columns], out_ref, sem)
    copy.start()
    copy.wait()


def mix_kernel(
    own_ref, other_ref, mine_ref, one_ref, two_ref, three_ref, four_ref, keep_ref, send_ref, total
):
    core, here, head = lax.axis_index("core"), column_block(), lax.axis_index("head")
    kept = keep_ref.shape[0]
    width = four_ref.shape[1]

    def rows(steps):
        source = (head + (2 * core - 1) * steps + 8) % 8
        block = [ref[here ^ k, source] for ref in (own_ref, other_ref) for k in range(4)]
        return jnp.concatenate(block, axis=0)

    total[...] = mm(rows(1), one_ref[...]) + mm(rows(2), two_ref[...]) + mm(rows(3), three_ref[...])

    @pl.when(core == 0)
    def _():
        total[...] = total[...] + mm(rows(0), mine_ref[...])

    part = pl.ds(pl.multiple_of(core * width, width), width)
    total[:, part] = total[:, part] + mm(rows(4), four_ref[...])
    keep_ref[...] = total[:kept]
    send_ref[...] = total[kept:].astype(BF16)


def add_kernel(keep_ref, come_ref, *outs):
    total = (keep_ref[...] + come_ref[...].astype(F32)).astype(BF16)
    rows = outs[0].shape[0]
    for k, ref in enumerate(outs):
        ref[...] = total[k * rows : (k + 1) * rows]


def lay_kernel(*refs):
    pieces, out_ref = refs[:-1], refs[-1]
    width = pieces[0].shape[1]
    here = column_block()
    for k, ref in enumerate(pieces):
        out_ref[:, pl.ds(pl.multiple_of((here ^ k) * width, width), width)] = ref[...]


def hbm():
    return pl.BlockSpec(memory_space=pltpu.HBM)


def vmem():
    return pl.BlockSpec(memory_space=pltpu.VMEM)


def per_device(
    frames, norm_gain, qkv_weight, gate_weight, beta_scale, decay_rate, resets, out_gain, out_weight
):
    rows, width = frames.shape
    n = qkv_weight.shape[2]
    weight = qkv_weight.transpose(1, 0, 2)
    gate = gate_weight.transpose(2, 1, 0).reshape(2, width)
    square = jax.ShapeDtypeStruct((rows, n), F32)
    gain = norm_gain.reshape(1, width)

    def buffers(matrices):
        return [
            pltpu.VMEM((rows, width), BF16),
            pltpu.VMEM((rows, width), BF16),
            pltpu.VMEM((matrices, width, n), BF16),
            pltpu.SemaphoreType.DMA((2 + 2 * matrices,)),
        ]

    carry, key, solved, decay, gamma = pl.pallas_call(
        fold_kernel,
        name="fold",
        in_specs=[hbm()] * 7,
        out_specs=[vmem()] + [hbm()] * 4,
        out_shape=[
            jax.ShapeDtypeStruct((n, 2 * n), BF16),
            square,
            jax.ShapeDtypeStruct((rows, 2 * n), F32),
            square,
            jax.ShapeDtypeStruct((rows, 1), F32),
        ],
        scratch_shapes=buffers(2)
        + [
            pltpu.SMEM((1,), F32),
            pltpu.SMEM((1,), F32),
            pltpu.VMEM((1, width), F32),
            pltpu.VMEM((2, width), BF16),
            pltpu.VMEM((1, rows), jnp.int32),
            pltpu.SemaphoreType.DMA((5,)),
            pltpu.VMEM((rows, n), F32),
            pltpu.VMEM((rows, 2 * n), F32),
            pltpu.VMEM((rows, n), F32),
            pltpu.VMEM((rows, 1), F32),
            pltpu.SemaphoreType.DMA((4,)),
        ],
        compiler_params=LARGE,
    )(beta_scale, decay_rate, frames, gain, weight, gate, resets.reshape(1, rows))

    def look():
        return pl.pallas_call(
            look_kernel,
            name="look",
            in_specs=[hbm(), vmem(), hbm()] + [vmem()] * 4,
            out_specs=vmem(),
            out_shape=jax.ShapeDtypeStruct((rows, 2 * n), F32),
            scratch_shapes=buffers(1),
            compiler_params=LARGE,
            cost_estimate=pl.CostEstimate(
                flops=4 * rows * width * n, bytes_accessed=16 << 20, transcendentals=0
            ),
        )(frames, gain, weight, key, solved, decay, gamma)

    count = 32

    def moved(value, place_of):
        return lax.ppermute(value, SEQ, [(i, place_of(i)) for i in range(count)])

    def along_x(shift):
        return lambda i: (i // 8) * 8 + (i + 2 * shift) % 8

    def along_y(shift):
        return lambda i: (i + 8 * shift) % 32

    def flip(bits):
        return lambda i: i ^ bits

    def around(value):
        up = [(z, (z + 1) % 8) for z in range(8)]
        down = [(8 + z, 8 + (z + 7) % 8) for z in range(8)]
        return lax.ppermute(value, ("core", "head"), up + down)

    def later(value, gate):
        return lax.optimization_barrier((value, gate))[0]

    wide = out_weight.shape[1] // 4
    mine = pl.pallas_call(
        take_kernel,
        name="take",
        in_specs=[hbm()],
        out_specs=vmem(),
        out_shape=jax.ShapeDtypeStruct((n, wide), BF16),
        scratch_shapes=[pltpu.SemaphoreType.DMA],
        compiler_params=LARGE,
    )(out_weight)
    one = around(mine)

    pair_shape = jax.ShapeDtypeStruct((n, 2 * n), BF16)
    half_shape = jax.ShapeDtypeStruct((n // 2, 2 * n), BF16)
    other = moved(carry, flip(1))
    two = around(later(one, other))
    pair, half = pl.pallas_call(
        pair_kernel,
        name="pair",
        in_specs=[vmem()] * 2,
        out_specs=[vmem()] * 2,
        out_shape=[pair_shape, half_shape],
        compiler_params=SMALL,
    )(carry, other)
    near = [moved(half, along_x(s)) for s in (1, 2, 3)]
    near, looked = lax.optimization_barrier((near, look()))
    three = around(later(two, near))
    swapped = [moved(value, flip(1)) for value in near]
    half, prefix = pl.pallas_call(
        row_kernel,
        name="row",
        in_specs=[vmem()] * 7,
        out_specs=[vmem()] * 2,
        out_shape=[half_shape, pair_shape],
        scratch_shapes=[pltpu.VMEM((4, n, 2 * n), BF16), pltpu.VMEM((n, 2 * n), BF16)],
        compiler_params=SMALL,
    )(pair, *near, *swapped)
    near = [moved(half, along_y(s)) for s in (1, 2, 3)]
    part_three = lax.dynamic_slice_in_dim(
        three, lax.axis_index("core") * (wide // 2), wide // 2, 1
    )
    four = around(later(part_three, near))
    swapped = [moved(value, flip(1)) for value in near]
    flat = pl.pallas_call(
        read_kernel,
        name="read",
        in_specs=[vmem()] * 10,
        out_specs=vmem(),
        out_shape=jax.ShapeDtypeStruct((4, rows, n), BF16),
        scratch_shapes=[pltpu.VMEM((4, n, 2 * n), BF16), pltpu.VMEM((n, n), F32)],
        compiler_params=SMALL,
    )(*near, *swapped, prefix, other, looked, out_gain.reshape(1, n))
    part = rows // 8
    flat, four = lax.optimization_barrier((flat, four))
    reads = lax.all_to_all(
        flat.reshape(32, part, n), ("yl", "xl", "head"), 0, 0, tiled=True
    ).reshape(4, 8, part, n)
    beside = moved(reads, flip(1))
    keep, send = pl.pallas_call(
        mix_kernel,
        name="mix",
        in_specs=[vmem()] * 7,
        out_specs=[vmem()] * 2,
        out_shape=[
            jax.ShapeDtypeStruct((4 * part, wide), F32),
            jax.ShapeDtypeStruct((4 * part, wide), BF16),
        ],
        scratch_shapes=[pltpu.VMEM((8 * part, wide), F32)],
        compiler_params=MIDDLE,
    )(reads, beside, mine, one, two, three, four)
    piece = jax.ShapeDtypeStruct((part, wide), BF16)
    kept, to_x, to_y, to_both = pl.pallas_call(
        add_kernel,
        name="add",
        in_specs=[vmem()] * 2,
        out_specs=[vmem()] * 4,
        out_shape=[piece] * 4,
        compiler_params=SMALL,
    )(keep, moved(send, flip(1)))
    return pl.pallas_call(
        lay_kernel,
        name="lay",
        in_specs=[vmem()] * 4,
        out_specs=vmem(),
        out_shape=jax.ShapeDtypeStruct((part, 4 * wide), BF16),
        compiler_params=SMALL,
    )(kept, moved(to_x, flip(2)), moved(to_y, flip(8)), moved(to_both, flip(10)))


def solution(mesh):
    fine = Mesh(mesh.devices.reshape(2, 2, 2, 2, 2, 8), SEQ + ("head",))
    in_specs = (
        P(SEQ, None),
        P(),
        P(None, None, "head"),
        P(None, None, "head"),
        P("head"),
        P("head"),
        P(SEQ),
        P("head"),
        P("head", None),
    )
    out_specs = P(SEQ + ("head",), None)
    return jax.shard_map(
        per_device, mesh=fine, in_specs=in_specs, out_specs=out_specs, check_vma=False
    )
```

```python
import jax
import jax.numpy as jnp
from jax import lax
from jax.experimental import pallas as pl
from jax.experimental.pallas import tpu as pltpu
from jax.sharding import Mesh
from jax.sharding import PartitionSpec as P

F32 = jnp.float32
BF16 = jnp.bfloat16
NN = (((1,), (0,)), ((), ()))
NT = (((1,), (1,)), ((), ()))
TN = (((0,), (0,)), ((), ()))
SEQ = ("yh", "yl", "xh", "xl", "core")
SMALL = pltpu.CompilerParams(vmem_limit_bytes=8 << 20)
MIDDLE = pltpu.CompilerParams(vmem_limit_bytes=16 << 20)
LARGE = pltpu.CompilerParams(vmem_limit_bytes=52 << 20)


def mm(a, b, dims=NN):
    return lax.dot_general(a, b, dims, preferred_element_type=F32)


def split(a):
    hi = a.astype(BF16)
    return hi, (a - hi.astype(F32)).astype(BF16)


def mm3(a, b, dims=NN):
    (ah, al), (bh, bl) = a, b
    return mm(ah, bh, dims) + (mm(ah, bl, dims) + mm(al, bh, dims))


def unit_rows(vectors):
    return vectors * lax.rsqrt(jnp.sum(vectors * vectors, axis=-1, keepdims=True) + 1e-06)


def norm_rows(x_ref, gain):
    x = x_ref[...].astype(F32)
    rs = lax.rsqrt(jnp.mean(x * x, axis=-1, keepdims=True) + 1e-06)
    return (x * rs * gain).astype(BF16)


def copies(x_hbm, w_hbm, slots, x_buf, w_buf, sems):
    halves = x_buf.shape[0] // 2
    depth = w_buf.shape[1] // 2
    rows = [pl.ds(i * halves, halves) for i in range(2)]
    parts = [pl.ds(i * depth, depth) for i in range(2)]
    found = [(x_hbm.at[part], x_buf.at[part]) for part in rows]
    for slot, j in enumerate(slots):
        found += [(w_hbm.at[j, part], w_buf.at[slot, part]) for part in parts]
    found = [pltpu.make_async_copy(a, b, sems.at[i]) for i, (a, b) in enumerate(found)]
    for copy in found:
        copy.start()
    return found


def normalise(found, x_buf, xn_buf, gain):
    half = x_buf.shape[0] // 2
    for i in range(2):
        found[i].wait()
        part = slice(i * half, (i + 1) * half)
        xn_buf[part] = norm_rows(x_buf.at[part], gain)


def project(found, xn_buf, w_buf, slot):
    depth = w_buf.shape[1] // 2
    total = None
    for i in range(2):
        found[2 + 2 * slot + i].wait()
        part = slice(i * depth, (i + 1) * depth)
        product = mm(xn_buf[:, part], w_buf[slot, part])
        total = product if total is None else total + product
    return total


def fold_kernel(
    scale_hbm, rate_hbm, x_hbm, gain_hbm, w_hbm, gate_hbm, resets_hbm,
    carry_ref, key_hbm, solved_hbm, decay_hbm, gamma_hbm,
    x_buf, xn_buf, w_buf, sems, scale_ref, rate_ref, gain_ref, gate_ref, resets_ref, small_sems,
    key_ref, solved_ref, decay_ref, gamma_ref, out_sems,
):
    small = [
        pltpu.make_async_copy(a, b, small_sems.at[i])
        for i, (a, b) in enumerate(
            (
                (gain_hbm, gain_ref),
                (gate_hbm, gate_ref),
                (resets_hbm, resets_ref),
                (scale_hbm, scale_ref),
                (rate_hbm, rate_ref),
            )
        )
    ]
    for copy in small:
        copy.start()
    found = copies(x_hbm, w_hbm, (1, 2), x_buf, w_buf, sems)
    small[0].wait()
    normalise(found, x_buf, xn_buf, gain_ref[...])
    n = x_buf.shape[0]
    for copy in small[1:] + found[2:]:
        copy.wait()
    kept = []

    def keep(value, ref, target):
        ref[...] = value
        kept.append(pltpu.make_async_copy(ref, target, out_sems.at[len(kept)]))
        kept[-1].start()

    gating = mm(xn_buf[...], gate_ref[...], NT)
    key = unit_rows(mm(xn_buf[...], w_buf[0]))
    beta = scale_ref[0] * jax.nn.sigmoid(gating[:, 0:1])
    logf = -rate_ref[0] * jax.nn.softplus(gating[:, 1:2])
    reset_row = resets_ref[...].astype(F32)
    t = lax.broadcasted_iota(jnp.int32, (n, n), 0)
    s = lax.broadcasted_iota(jnp.int32, (n, n), 1)
    causal = t >= s
    eye = t == s

    def to_row(col):
        return jnp.sum(jnp.where(eye, col, 0.0), axis=0, keepdims=True)

    cum = jnp.sum(jnp.where(causal, to_row(logf), 0.0), axis=1, keepdims=True)
    seg = jnp.sum(jnp.where(causal, reset_row, 0.0), axis=1, keepdims=True)
    cum_row = to_row(cum)
    seg_row = to_row(seg)
    same = (seg == seg_row) & causal
    decay = jnp.where(same, jnp.exp(jnp.where(same, cum - cum_row, 0.0)), 0.0)
    gamma = jnp.where(seg == 0.0, jnp.exp(cum), 0.0)
    cum_last, seg_last = cum[n - 1 : n], seg[n - 1 : n]
    tail = jnp.where(seg == seg_last, jnp.exp(cum_last - cum), 0.0)
    gamma_last = gamma[n - 1 : n]
    keep(key, key_ref, key_hbm)
    keep(decay, decay_ref, decay_hbm)
    keep(gamma, gamma_ref, gamma_hbm)

    ks = split(key)
    low = jnp.where(t > s, beta * decay * mm3(ks, ks, NT), 0.0)
    apart = t ^ s
    inv = jnp.where(eye, 1.0, jnp.where(apart == 1, -low, 0.0))
    levels = range(1, n.bit_length() - 1)
    depth = xn_buf.shape[1] // (len(levels) + 1)
    value = mm(xn_buf[:, :depth], w_buf[1, :depth])
    for level in levels:
        part = jnp.where((apart >> level) == 1, low, 0.0).astype(BF16)
        rough = inv.astype(BF16)
        inner = mm(part, rough).astype(BF16)
        chunk = slice(level * depth, (level + 1) * depth)
        value = value + mm(xn_buf[:, chunk], w_buf[1, chunk])
        inv = inv - mm(rough, inner)
    vs = split(inv)
    left = jnp.where(eye, 1.0, 0.0) - inv - mm3(split(low), vs)
    inv = inv + mm(vs[0], left.astype(BF16))

    rhs = jnp.concatenate([(beta * gamma) * key, beta * value], axis=1)
    solved = mm3(split(inv), split(rhs))
    keep(solved, solved_ref, solved_hbm)
    folded = mm3(split(key * tail), split(solved), TN)
    carry_ref[:, :n] = (jnp.where(eye, gamma_last, 0.0) - folded[:, :n]).astype(BF16)
    carry_ref[:, n:] = folded[:, n:].astype(BF16)
    for copy in kept:
        copy.wait()


def look_kernel(
    x_hbm, gain_ref, w_hbm, key_ref, solved_ref, decay_ref, gamma_ref,
    out_ref,
    x_buf, xn_buf, w_buf, sems,
):
    found = copies(x_hbm, w_hbm, (0,), x_buf, w_buf, sems)
    normalise(found, x_buf, xn_buf, gain_ref[...])
    n = x_buf.shape[0]
    query = unit_rows(project(found, xn_buf, w_buf, 0))
    scores = mm3(split(query), split(key_ref[...]), NT) * decay_ref[...]
    seen = mm3(split(scores), split(solved_ref[...]))
    out_ref[:, :n] = gamma_ref[...] * query - seen[:, :n]
    out_ref[:, n:] = seen[:, n:]


def after(later, earlier, n):
    both = mm(later[:, :n], earlier)
    return both[:, :n], both[:, n:] + later[:, n:].astype(F32)


def own_half(ref):
    half = ref.shape[0] // 2
    return ref[pl.ds(pl.multiple_of(lax.axis_index("core") * half, half), half)]


def hold(held, place, near_ref, swap_ref):
    half = near_ref.shape[0]
    core = lax.axis_index("core")
    held[place, pl.ds(pl.multiple_of(core * half, half), half)] = near_ref[...]
    held[place, pl.ds(pl.multiple_of((1 - core) * half, half), half)] = swap_ref[...]


def pair_kernel(own_ref, other_ref, out_ref, half_ref):
    n = own_ref.shape[0]
    first = lax.axis_index("core") == 0
    own, other = own_ref[...], other_ref[...]
    earlier = jnp.where(first, own, other)
    later = jnp.where(first, other, own)
    a, b = after(later, earlier, n)
    out_ref[:, :n] = a.astype(BF16)
    out_ref[:, n:] = b.astype(BF16)
    half_ref[...] = own_half(out_ref)


def row_kernel(own_ref, *refs):
    near, swapped, (half_ref, prefix_ref, held, total_ref) = refs[:3], refs[3:6], refs[6:]
    n = own_ref.shape[0]
    place = lax.axis_index("xh") * 2 + lax.axis_index("xl")
    held[place] = own_ref[...]
    for shift, ref, swap in zip((1, 2, 3), near, swapped):
        hold(held, (place + (4 - shift)) % 4, ref, swap)

    def joined(later, earlier):
        a, b = after(later, earlier, n)
        return jnp.concatenate([a, b], axis=1).astype(BF16)

    low = joined(held[1], held[0])
    high = joined(held[3], held[2])
    a, b = after(high, low, n)
    total_ref[:, :n] = a.astype(BF16)
    total_ref[:, n:] = b.astype(BF16)
    half_ref[...] = own_half(total_ref)

    @pl.when(place == 0)
    def _():
        prefix_ref[...] = jnp.zeros_like(prefix_ref)

    @pl.when(place == 1)
    def _():
        prefix_ref[...] = held[0]

    @pl.when(place == 2)
    def _():
        prefix_ref[...] = low

    @pl.when(place == 3)
    def _():
        prefix_ref[...] = joined(held[2], low)


def read_kernel(*refs):
    near, swapped = refs[:3], refs[3:6]
    prefix_ref, other_ref, look_ref, gain_ref, out_ref, held, state = refs[6:]
    n = look_ref.shape[0]
    place = lax.axis_index("yh") * 2 + lax.axis_index("yl")
    for shift, ref, swap in zip((1, 2, 3), near, swapped):
        hold(held, (place + (4 - shift)) % 4, ref, swap)

    def push(pair, value):
        hi, lo = split(value)
        return mm(pair[:, :n], hi) + mm(pair[:, :n], lo) + pair[:, n:].astype(F32)

    @pl.when(place == 0)
    def _():
        state[...] = jnp.zeros_like(state)

    @pl.when(place > 0)
    def _():
        state[...] = held[0, :, n:].astype(F32)

    for turn in (1, 2):
        @pl.when(place > turn)
        def _():
            state[...] = push(held[turn], state[...])

    @pl.when(lax.axis_index("xh") + lax.axis_index("xl") > 0)
    def _():
        state[...] = push(prefix_ref[...], state[...])

    @pl.when(lax.axis_index("core") > 0)
    def _():
        state[...] = push(other_ref[...], state[...])

    read = look_ref[:, n:] + mm3(split(look_ref[:, :n]), split(state[...]))
    read = read * lax.rsqrt(jnp.mean(read * read, axis=-1, keepdims=True) + 1e-06)
    flat = (read * gain_ref[...]).astype(BF16)
    for copy in range(out_ref.shape[0]):
        out_ref[copy] = flat


def column_block():
    return lax.axis_index("yl") * 2 + lax.axis_index("xl")


def take_kernel(whole_ref, out_ref, sem):
    width = out_ref.shape[1]
    columns = pl.ds(pl.multiple_of(column_block() * width, width), width)
    copy = pltpu.make_async_copy(whole_ref.at[:, columns], out_ref, sem)
    copy.start()
    copy.wait()


def mix_kernel(
    own_ref, other_ref, mine_ref, one_ref, two_ref, three_ref, four_ref, keep_ref, send_ref, total
):
    core, here, head = lax.axis_index("core"), column_block(), lax.axis_index("head")
    kept = keep_ref.shape[0]
    width = four_ref.shape[1]

    def rows(steps):
        source = (head + (2 * core - 1) * steps + 8) % 8
        block = [ref[here ^ k, source] for ref in (own_ref, other_ref) for k in range(4)]
        return jnp.concatenate(block, axis=0)

    total[...] = mm(rows(1), one_ref[...]) + mm(rows(2), two_ref[...]) + mm(rows(3), three_ref[...])

    @pl.when(core == 0)
    def _():
        total[...] = total[...] + mm(rows(0), mine_ref[...])

    part = pl.ds(pl.multiple_of(core * width, width), width)
    total[:, part] = total[:, part] + mm(rows(4), four_ref[...])
    keep_ref[...] = total[:kept]
    send_ref[...] = total[kept:].astype(BF16)


def add_kernel(keep_ref, come_ref, *outs):
    total = (keep_ref[...] + come_ref[...].astype(F32)).astype(BF16)
    rows = outs[0].shape[0]
    for k, ref in enumerate(outs):
        ref[...] = total[k * rows : (k + 1) * rows]


def lay_kernel(*refs):
    pieces, out_ref = refs[:-1], refs[-1]
    width = pieces[0].shape[1]
    here = column_block()
    for k, ref in enumerate(pieces):
        out_ref[:, pl.ds(pl.multiple_of((here ^ k) * width, width), width)] = ref[...]


def hbm():
    return pl.BlockSpec(memory_space=pltpu.HBM)


def vmem():
    return pl.BlockSpec(memory_space=pltpu.VMEM)


def per_device(
    frames, norm_gain, qkv_weight, gate_weight, beta_scale, decay_rate, resets, out_gain, out_weight
):
    rows, width = frames.shape
    n = qkv_weight.shape[2]
    weight = qkv_weight.transpose(1, 0, 2)
    gate = gate_weight.transpose(2, 1, 0).reshape(2, width)
    square = jax.ShapeDtypeStruct((rows, n), F32)
    gain = norm_gain.reshape(1, width)

    def buffers(matrices):
        return [
            pltpu.VMEM((rows, width), BF16),
            pltpu.VMEM((rows, width), BF16),
            pltpu.VMEM((matrices, width, n), BF16),
            pltpu.SemaphoreType.DMA((2 + 2 * matrices,)),
        ]

    carry, key, solved, decay, gamma = pl.pallas_call(
        fold_kernel,
        name="fold",
        in_specs=[hbm()] * 7,
        out_specs=[vmem()] + [hbm()] * 4,
        out_shape=[
            jax.ShapeDtypeStruct((n, 2 * n), BF16),
            square,
            jax.ShapeDtypeStruct((rows, 2 * n), F32),
            square,
            jax.ShapeDtypeStruct((rows, 1), F32),
        ],
        scratch_shapes=buffers(2)
        + [
            pltpu.SMEM((1,), F32),
            pltpu.SMEM((1,), F32),
            pltpu.VMEM((1, width), F32),
            pltpu.VMEM((2, width), BF16),
            pltpu.VMEM((1, rows), jnp.int32),
            pltpu.SemaphoreType.DMA((5,)),
            pltpu.VMEM((rows, n), F32),
            pltpu.VMEM((rows, 2 * n), F32),
            pltpu.VMEM((rows, n), F32),
            pltpu.VMEM((rows, 1), F32),
            pltpu.SemaphoreType.DMA((4,)),
        ],
        compiler_params=LARGE,
    )(beta_scale, decay_rate, frames, gain, weight, gate, resets.reshape(1, rows))

    def look():
        return pl.pallas_call(
            look_kernel,
            name="look",
            in_specs=[hbm(), vmem(), hbm()] + [vmem()] * 4,
            out_specs=vmem(),
            out_shape=jax.ShapeDtypeStruct((rows, 2 * n), F32),
            scratch_shapes=buffers(1),
            compiler_params=LARGE,
            cost_estimate=pl.CostEstimate(
                flops=4 * rows * width * n, bytes_accessed=16 << 20, transcendentals=0
            ),
        )(frames, gain, weight, key, solved, decay, gamma)

    count = 32

    def moved(value, place_of):
        return lax.ppermute(value, SEQ, [(i, place_of(i)) for i in range(count)])

    def along_x(shift):
        return lambda i: (i // 8) * 8 + (i + 2 * shift) % 8

    def along_y(shift):
        return lambda i: (i + 8 * shift) % 32

    def flip(bits):
        return lambda i: i ^ bits

    def around(value, steps):
        up = [(z, (z + steps) % 8) for z in range(8)]
        down = [(8 + z, 8 + (z + 8 - steps) % 8) for z in range(8)]
        return lax.ppermute(value, ("core", "head"), up + down)

    def later(value, gate):
        return lax.optimization_barrier((value, gate))[0]

    wide = out_weight.shape[1] // 4
    mine = pl.pallas_call(
        take_kernel,
        name="take",
        in_specs=[hbm()],
        out_specs=vmem(),
        out_shape=jax.ShapeDtypeStruct((n, wide), BF16),
        scratch_shapes=[pltpu.SemaphoreType.DMA],
        compiler_params=LARGE,
    )(out_weight)
    one = around(mine, 1)
    two = around(mine, 2)

    pair_shape = jax.ShapeDtypeStruct((n, 2 * n), BF16)
    half_shape = jax.ShapeDtypeStruct((n // 2, 2 * n), BF16)
    other = moved(carry, flip(1))
    pair, half = pl.pallas_call(
        pair_kernel,
        name="pair",
        in_specs=[vmem()] * 2,
        out_specs=[vmem()] * 2,
        out_shape=[pair_shape, half_shape],
        compiler_params=SMALL,
    )(carry, other)
    near = [moved(half, along_x(s)) for s in (1, 2, 3)]
    near, looked = lax.optimization_barrier((near, look()))
    one, ready = later((one, two), near)
    three = around(ready, 1)
    part_two = lax.dynamic_slice_in_dim(
        ready, lax.axis_index("core") * (wide // 2), wide // 2, 1
    )
    four = around(part_two, 2)
    swapped = [moved(value, flip(1)) for value in near]
    half, prefix = pl.pallas_call(
        row_kernel,
        name="row",
        in_specs=[vmem()] * 7,
        out_specs=[vmem()] * 2,
        out_shape=[half_shape, pair_shape],
        scratch_shapes=[pltpu.VMEM((4, n, 2 * n), BF16), pltpu.VMEM((n, 2 * n), BF16)],
        compiler_params=SMALL,
    )(pair, *near, *swapped)
    near = [moved(half, along_y(s)) for s in (1, 2, 3)]
    near, three, four = lax.optimization_barrier((near, three, four))
    swapped = [moved(value, flip(1)) for value in near]
    flat = pl.pallas_call(
        read_kernel,
        name="read",
        in_specs=[vmem()] * 10,
        out_specs=vmem(),
        out_shape=jax.ShapeDtypeStruct((4, rows, n), BF16),
        scratch_shapes=[pltpu.VMEM((4, n, 2 * n), BF16), pltpu.VMEM((n, n), F32)],
        compiler_params=SMALL,
    )(*near, *swapped, prefix, other, looked, out_gain.reshape(1, n))
    part = rows // 8
    reads = lax.all_to_all(
        flat.reshape(32, part, n), ("yl", "xl", "head"), 0, 0, tiled=True
    ).reshape(4, 8, part, n)
    beside = moved(reads, flip(1))
    keep, send = pl.pallas_call(
        mix_kernel,
        name="mix",
        in_specs=[vmem()] * 7,
        out_specs=[vmem()] * 2,
        out_shape=[
            jax.ShapeDtypeStruct((4 * part, wide), F32),
            jax.ShapeDtypeStruct((4 * part, wide), BF16),
        ],
        scratch_shapes=[pltpu.VMEM((8 * part, wide), F32)],
        compiler_params=MIDDLE,
    )(reads, beside, mine, one, two, three, four)
    piece = jax.ShapeDtypeStruct((part, wide), BF16)
    kept, to_x, to_y, to_both = pl.pallas_call(
        add_kernel,
        name="add",
        in_specs=[vmem()] * 2,
        out_specs=[vmem()] * 4,
        out_shape=[piece] * 4,
        compiler_params=SMALL,
    )(keep, moved(send, flip(1)))
    return pl.pallas_call(
        lay_kernel,
        name="lay",
        in_specs=[vmem()] * 4,
        out_specs=vmem(),
        out_shape=jax.ShapeDtypeStruct((part, 4 * wide), BF16),
        compiler_params=SMALL,
    )(kept, moved(to_x, flip(2)), moved(to_y, flip(8)), moved(to_both, flip(10)))


def solution(mesh):
    fine = Mesh(mesh.devices.reshape(2, 2, 2, 2, 2, 8), SEQ + ("head",))
    in_specs = (
        P(SEQ, None),
        P(),
        P(None, None, "head"),
        P(None, None, "head"),
        P("head"),
        P("head"),
        P(SEQ),
        P("head"),
        P("head", None),
    )
    out_specs = P(SEQ + ("head",), None)
    return jax.shard_map(
        per_device, mesh=fine, in_specs=in_specs, out_specs=out_specs, check_vma=False
    )
```

```python
import jax
import jax.numpy as jnp
from jax import lax
from jax.experimental import pallas as pl
from jax.experimental.pallas import tpu as pltpu
from jax.sharding import Mesh
from jax.sharding import PartitionSpec as P

F32 = jnp.float32
BF16 = jnp.bfloat16
NN = (((1,), (0,)), ((), ()))
NT = (((1,), (1,)), ((), ()))
TN = (((0,), (0,)), ((), ()))
SEQ = ("yh", "yl", "xh", "xl", "core")
SMALL = pltpu.CompilerParams(vmem_limit_bytes=8 << 20)
MIDDLE = pltpu.CompilerParams(vmem_limit_bytes=16 << 20)
LARGE = pltpu.CompilerParams(vmem_limit_bytes=52 << 20)


def mm(a, b, dims=NN):
    return lax.dot_general(a, b, dims, preferred_element_type=F32)


def split(a):
    hi = a.astype(BF16)
    return hi, (a - hi.astype(F32)).astype(BF16)


def mm3(a, b, dims=NN):
    (ah, al), (bh, bl) = a, b
    return mm(ah, bh, dims) + (mm(ah, bl, dims) + mm(al, bh, dims))


def unit_rows(vectors):
    return vectors * lax.rsqrt(jnp.sum(vectors * vectors, axis=-1, keepdims=True) + 1e-06)


def norm_rows(x_ref, gain):
    x = x_ref[...].astype(F32)
    rs = lax.rsqrt(jnp.mean(x * x, axis=-1, keepdims=True) + 1e-06)
    return (x * rs * gain).astype(BF16)


def copies(x_hbm, w_hbm, slots, x_buf, w_buf, sems):
    halves = x_buf.shape[0] // 2
    depth = w_buf.shape[1] // 2
    rows = [pl.ds(i * halves, halves) for i in range(2)]
    parts = [pl.ds(i * depth, depth) for i in range(2)]
    found = [(x_hbm.at[part], x_buf.at[part]) for part in rows]
    for slot, j in enumerate(slots):
        found += [(w_hbm.at[j, part], w_buf.at[slot, part]) for part in parts]
    found = [pltpu.make_async_copy(a, b, sems.at[i]) for i, (a, b) in enumerate(found)]
    for copy in found:
        copy.start()
    return found


def normalise(found, x_buf, xn_buf, gain):
    half = x_buf.shape[0] // 2
    for i in range(2):
        found[i].wait()
        part = slice(i * half, (i + 1) * half)
        xn_buf[part] = norm_rows(x_buf.at[part], gain)


def project(found, xn_buf, w_buf, slot):
    depth = w_buf.shape[1] // 2
    total = None
    for i in range(2):
        found[2 + 2 * slot + i].wait()
        part = slice(i * depth, (i + 1) * depth)
        product = mm(xn_buf[:, part], w_buf[slot, part])
        total = product if total is None else total + product
    return total


def fold_kernel(
    scale_hbm, rate_hbm, x_hbm, gain_hbm, w_hbm, gate_hbm, resets_hbm,
    carry_ref, key_hbm, solved_hbm, decay_hbm, gamma_hbm,
    x_buf, xn_buf, w_buf, sems, scale_ref, rate_ref, gain_ref, gate_ref, resets_ref, small_sems,
    key_ref, solved_ref, decay_ref, gamma_ref, out_sems,
):
    small = [
        pltpu.make_async_copy(a, b, small_sems.at[i])
        for i, (a, b) in enumerate(
            (
                (gain_hbm, gain_ref),
                (gate_hbm, gate_ref),
                (resets_hbm, resets_ref),
                (scale_hbm, scale_ref),
                (rate_hbm, rate_ref),
            )
        )
    ]
    for copy in small:
        copy.start()
    found = copies(x_hbm, w_hbm, (1, 2), x_buf, w_buf, sems)
    small[0].wait()
    normalise(found, x_buf, xn_buf, gain_ref[...])
    n = x_buf.shape[0]
    for copy in small[1:] + found[2:]:
        copy.wait()
    kept = []

    def keep(value, ref, target):
        ref[...] = value
        kept.append(pltpu.make_async_copy(ref, target, out_sems.at[len(kept)]))
        kept[-1].start()

    gating = mm(xn_buf[...], gate_ref[...], NT)
    key = unit_rows(mm(xn_buf[...], w_buf[0]))
    beta = scale_ref[0] * jax.nn.sigmoid(gating[:, 0:1])
    logf = -rate_ref[0] * jax.nn.softplus(gating[:, 1:2])
    reset_row = resets_ref[...].astype(F32)
    t = lax.broadcasted_iota(jnp.int32, (n, n), 0)
    s = lax.broadcasted_iota(jnp.int32, (n, n), 1)
    causal = t >= s
    eye = t == s

    def to_row(col):
        return jnp.sum(jnp.where(eye, col, 0.0), axis=0, keepdims=True)

    cum = jnp.sum(jnp.where(causal, to_row(logf), 0.0), axis=1, keepdims=True)
    seg = jnp.sum(jnp.where(causal, reset_row, 0.0), axis=1, keepdims=True)
    cum_row = to_row(cum)
    seg_row = to_row(seg)
    same = (seg == seg_row) & causal
    decay = jnp.where(same, jnp.exp(jnp.where(same, cum - cum_row, 0.0)), 0.0)
    gamma = jnp.where(seg == 0.0, jnp.exp(cum), 0.0)
    cum_last, seg_last = cum[n - 1 : n], seg[n - 1 : n]
    tail = jnp.where(seg == seg_last, jnp.exp(cum_last - cum), 0.0)
    gamma_last = gamma[n - 1 : n]
    keep(key, key_ref, key_hbm)
    keep(decay, decay_ref, decay_hbm)
    keep(gamma, gamma_ref, gamma_hbm)

    ks = split(key)
    low = jnp.where(t > s, beta * decay * mm3(ks, ks, NT), 0.0)
    apart = t ^ s
    inv = jnp.where(eye, 1.0, jnp.where(apart == 1, -low, 0.0))
    levels = range(1, n.bit_length() - 1)
    depth = xn_buf.shape[1] // (len(levels) + 1)
    value = mm(xn_buf[:, :depth], w_buf[1, :depth])
    for level in levels:
        part = jnp.where((apart >> level) == 1, low, 0.0).astype(BF16)
        rough = inv.astype(BF16)
        inner = mm(part, rough).astype(BF16)
        chunk = slice(level * depth, (level + 1) * depth)
        value = value + mm(xn_buf[:, chunk], w_buf[1, chunk])
        inv = inv - mm(rough, inner)
    vs = split(inv)
    left = jnp.where(eye, 1.0, 0.0) - inv - mm3(split(low), vs)
    inv = inv + mm(vs[0], left.astype(BF16))

    rhs = jnp.concatenate([(beta * gamma) * key, beta * value], axis=1)
    solved = mm3(split(inv), split(rhs))
    keep(solved, solved_ref, solved_hbm)
    folded = mm3(split(key * tail), split(solved), TN)
    carry_ref[:, :n] = (jnp.where(eye, gamma_last, 0.0) - folded[:, :n]).astype(BF16)
    carry_ref[:, n:] = folded[:, n:].astype(BF16)
    for copy in kept:
        copy.wait()


def look_kernel(
    x_hbm, gain_ref, w_hbm, key_ref, solved_ref, decay_ref, gamma_ref,
    out_ref,
    x_buf, xn_buf, w_buf, sems,
):
    found = copies(x_hbm, w_hbm, (0,), x_buf, w_buf, sems)
    normalise(found, x_buf, xn_buf, gain_ref[...])
    n = x_buf.shape[0]
    query = unit_rows(project(found, xn_buf, w_buf, 0))
    scores = mm3(split(query), split(key_ref[...]), NT) * decay_ref[...]
    seen = mm3(split(scores), split(solved_ref[...]))
    out_ref[:, :n] = gamma_ref[...] * query - seen[:, :n]
    out_ref[:, n:] = seen[:, n:]


def after(later, earlier, n):
    both = mm(later[:, :n], earlier)
    return both[:, :n], both[:, n:] + later[:, n:].astype(F32)


def own_half(ref):
    half = ref.shape[0] // 2
    return ref[pl.ds(pl.multiple_of(lax.axis_index("core") * half, half), half)]


def hold(held, place, near_ref, swap_ref):
    half = near_ref.shape[0]
    core = lax.axis_index("core")
    held[place, pl.ds(pl.multiple_of(core * half, half), half)] = near_ref[...]
    held[place, pl.ds(pl.multiple_of((1 - core) * half, half), half)] = swap_ref[...]


def pair_kernel(own_ref, other_ref, out_ref, half_ref):
    n = own_ref.shape[0]
    first = lax.axis_index("core") == 0
    own, other = own_ref[...], other_ref[...]
    earlier = jnp.where(first, own, other)
    later = jnp.where(first, other, own)
    a, b = after(later, earlier, n)
    out_ref[:, :n] = a.astype(BF16)
    out_ref[:, n:] = b.astype(BF16)
    half_ref[...] = own_half(out_ref)


def row_kernel(own_ref, *refs):
    near, swapped, (half_ref, prefix_ref, held, total_ref) = refs[:3], refs[3:6], refs[6:]
    n = own_ref.shape[0]
    place = lax.axis_index("xh") * 2 + lax.axis_index("xl")
    held[place] = own_ref[...]
    for shift, ref, swap in zip((1, 2, 3), near, swapped):
        hold(held, (place + (4 - shift)) % 4, ref, swap)

    def joined(later, earlier):
        a, b = after(later, earlier, n)
        return jnp.concatenate([a, b], axis=1).astype(BF16)

    low = joined(held[1], held[0])
    high = joined(held[3], held[2])
    a, b = after(high, low, n)
    total_ref[:, :n] = a.astype(BF16)
    total_ref[:, n:] = b.astype(BF16)
    half_ref[...] = own_half(total_ref)

    @pl.when(place == 0)
    def _():
        prefix_ref[...] = jnp.zeros_like(prefix_ref)

    @pl.when(place == 1)
    def _():
        prefix_ref[...] = held[0]

    @pl.when(place == 2)
    def _():
        prefix_ref[...] = low

    @pl.when(place == 3)
    def _():
        prefix_ref[...] = joined(held[2], low)


def read_kernel(*refs):
    near, swapped = refs[:3], refs[3:6]
    prefix_ref, other_ref, look_ref, gain_ref, out_ref, held, state = refs[6:]
    n = look_ref.shape[0]
    place = lax.axis_index("yh") * 2 + lax.axis_index("yl")
    for shift, ref, swap in zip((1, 2, 3), near, swapped):
        hold(held, (place + (4 - shift)) % 4, ref, swap)

    def push(pair, value):
        hi, lo = split(value)
        return mm(pair[:, :n], hi) + mm(pair[:, :n], lo) + pair[:, n:].astype(F32)

    @pl.when(place == 0)
    def _():
        state[...] = jnp.zeros_like(state)

    @pl.when(place > 0)
    def _():
        state[...] = held[0, :, n:].astype(F32)

    for turn in (1, 2):
        @pl.when(place > turn)
        def _():
            state[...] = push(held[turn], state[...])

    @pl.when(lax.axis_index("xh") + lax.axis_index("xl") > 0)
    def _():
        state[...] = push(prefix_ref[...], state[...])

    @pl.when(lax.axis_index("core") > 0)
    def _():
        state[...] = push(other_ref[...], state[...])

    read = look_ref[:, n:] + mm3(split(look_ref[:, :n]), split(state[...]))
    read = read * lax.rsqrt(jnp.mean(read * read, axis=-1, keepdims=True) + 1e-06)
    flat = (read * gain_ref[...]).astype(BF16)
    for copy in range(out_ref.shape[0]):
        out_ref[copy] = flat


def column_block():
    return lax.axis_index("yl") * 2 + lax.axis_index("xl")


def take_kernel(whole_ref, out_ref, sem):
    width = out_ref.shape[1]
    columns = pl.ds(pl.multiple_of(column_block() * width, width), width)
    copy = pltpu.make_async_copy(whole_ref.at[:, columns], out_ref, sem)
    copy.start()
    copy.wait()


def mix_kernel(
    own_ref, other_ref, mine_ref, one_ref, two_ref, three_ref, four_ref, keep_ref, send_ref, total
):
    core, here, head = lax.axis_index("core"), column_block(), lax.axis_index("head")
    kept = keep_ref.shape[0]
    width = four_ref.shape[1]

    def rows(steps):
        source = (head + (2 * core - 1) * steps + 8) % 8
        block = [ref[here ^ k, source] for ref in (own_ref, other_ref) for k in range(4)]
        return jnp.concatenate(block, axis=0)

    total[...] = mm(rows(1), one_ref[...]) + mm(rows(2), two_ref[...]) + mm(rows(3), three_ref[...])

    @pl.when(core == 0)
    def _():
        total[...] = total[...] + mm(rows(0), mine_ref[...])

    part = pl.ds(pl.multiple_of(core * width, width), width)
    total[:, part] = total[:, part] + mm(rows(4), four_ref[...])
    keep_ref[...] = total[:kept]
    send_ref[...] = total[kept:].astype(BF16)


def add_kernel(keep_ref, come_ref, *outs):
    total = (keep_ref[...] + come_ref[...].astype(F32)).astype(BF16)
    rows = outs[0].shape[0]
    for k, ref in enumerate(outs):
        ref[...] = total[k * rows : (k + 1) * rows]


def lay_kernel(*refs):
    pieces, out_ref = refs[:-1], refs[-1]
    width = pieces[0].shape[1]
    here = column_block()
    for k, ref in enumerate(pieces):
        out_ref[:, pl.ds(pl.multiple_of((here ^ k) * width, width), width)] = ref[...]


def hbm():
    return pl.BlockSpec(memory_space=pltpu.HBM)


def vmem():
    return pl.BlockSpec(memory_space=pltpu.VMEM)


def per_device(
    frames, norm_gain, qkv_weight, gate_weight, beta_scale, decay_rate, resets, out_gain, out_weight
):
    rows, width = frames.shape
    n = qkv_weight.shape[2]
    weight = qkv_weight.transpose(1, 0, 2)
    gate = gate_weight.transpose(2, 1, 0).reshape(2, width)
    square = jax.ShapeDtypeStruct((rows, n), F32)
    gain = norm_gain.reshape(1, width)

    def buffers(matrices):
        return [
            pltpu.VMEM((rows, width), BF16),
            pltpu.VMEM((rows, width), BF16),
            pltpu.VMEM((matrices, width, n), BF16),
            pltpu.SemaphoreType.DMA((2 + 2 * matrices,)),
        ]

    carry, key, solved, decay, gamma = pl.pallas_call(
        fold_kernel,
        name="fold",
        in_specs=[hbm()] * 7,
        out_specs=[vmem()] + [hbm()] * 4,
        out_shape=[
            jax.ShapeDtypeStruct((n, 2 * n), BF16),
            square,
            jax.ShapeDtypeStruct((rows, 2 * n), F32),
            square,
            jax.ShapeDtypeStruct((rows, 1), F32),
        ],
        scratch_shapes=buffers(2)
        + [
            pltpu.SMEM((1,), F32),
            pltpu.SMEM((1,), F32),
            pltpu.VMEM((1, width), F32),
            pltpu.VMEM((2, width), BF16),
            pltpu.VMEM((1, rows), jnp.int32),
            pltpu.SemaphoreType.DMA((5,)),
            pltpu.VMEM((rows, n), F32),
            pltpu.VMEM((rows, 2 * n), F32),
            pltpu.VMEM((rows, n), F32),
            pltpu.VMEM((rows, 1), F32),
            pltpu.SemaphoreType.DMA((4,)),
        ],
        compiler_params=LARGE,
    )(beta_scale, decay_rate, frames, gain, weight, gate, resets.reshape(1, rows))

    def look():
        return pl.pallas_call(
            look_kernel,
            name="look",
            in_specs=[hbm(), vmem(), hbm()] + [vmem()] * 4,
            out_specs=vmem(),
            out_shape=jax.ShapeDtypeStruct((rows, 2 * n), F32),
            scratch_shapes=buffers(1),
            compiler_params=LARGE,
            cost_estimate=pl.CostEstimate(
                flops=4 * rows * width * n, bytes_accessed=16 << 20, transcendentals=0
            ),
        )(frames, gain, weight, key, solved, decay, gamma)

    count = 32

    def moved(value, place_of):
        return lax.ppermute(value, SEQ, [(i, place_of(i)) for i in range(count)])

    def along_x(shift):
        return lambda i: (i // 8) * 8 + (i + 2 * shift) % 8

    def along_y(shift):
        return lambda i: (i + 8 * shift) % 32

    def flip(bits):
        return lambda i: i ^ bits

    def around(value, steps):
        up = [(z, (z + steps) % 8) for z in range(8)]
        down = [(8 + z, 8 + (z + 8 - steps) % 8) for z in range(8)]
        return lax.ppermute(value, ("core", "head"), up + down)

    def later(value, gate):
        return lax.optimization_barrier((value, gate))[0]

    wide = out_weight.shape[1] // 4
    mine = pl.pallas_call(
        take_kernel,
        name="take",
        in_specs=[hbm()],
        out_specs=vmem(),
        out_shape=jax.ShapeDtypeStruct((n, wide), BF16),
        scratch_shapes=[pltpu.SemaphoreType.DMA],
        compiler_params=LARGE,
    )(out_weight)
    one = around(mine, 1)
    two = around(mine, 2)

    pair_shape = jax.ShapeDtypeStruct((n, 2 * n), BF16)
    half_shape = jax.ShapeDtypeStruct((n // 2, 2 * n), BF16)
    other = moved(carry, flip(1))
    pair, half = pl.pallas_call(
        pair_kernel,
        name="pair",
        in_specs=[vmem()] * 2,
        out_specs=[vmem()] * 2,
        out_shape=[pair_shape, half_shape],
        compiler_params=SMALL,
    )(carry, other)
    near = [moved(half, along_x(s)) for s in (1, 2, 3)]
    near, looked = lax.optimization_barrier((near, look()))
    one, ready = later((one, two), near)
    three = around(ready, 1)
    part_two = lax.dynamic_slice_in_dim(
        ready, lax.axis_index("core") * (wide // 2), wide // 2, 1
    )
    four = around(part_two, 2)
    swapped = [moved(value, flip(1)) for value in near]
    half, prefix = pl.pallas_call(
        row_kernel,
        name="row",
        in_specs=[vmem()] * 7,
        out_specs=[vmem()] * 2,
        out_shape=[half_shape, pair_shape],
        scratch_shapes=[pltpu.VMEM((4, n, 2 * n), BF16), pltpu.VMEM((n, 2 * n), BF16)],
        compiler_params=SMALL,
    )(pair, *near, *swapped)
    near = [moved(half, along_y(s)) for s in (1, 2, 3)]
    swapped = [moved(value, flip(1)) for value in near]
    flat = pl.pallas_call(
        read_kernel,
        name="read",
        in_specs=[vmem()] * 10,
        out_specs=vmem(),
        out_shape=jax.ShapeDtypeStruct((4, rows, n), BF16),
        scratch_shapes=[pltpu.VMEM((4, n, 2 * n), BF16), pltpu.VMEM((n, n), F32)],
        compiler_params=SMALL,
    )(*near, *swapped, prefix, other, looked, out_gain.reshape(1, n))
    part = rows // 8
    flat, three, four = lax.optimization_barrier((flat, three, four))
    reads = lax.all_to_all(
        flat.reshape(32, part, n), ("yl", "xl", "head"), 0, 0, tiled=True
    ).reshape(4, 8, part, n)
    beside = moved(reads, flip(1))
    keep, send = pl.pallas_call(
        mix_kernel,
        name="mix",
        in_specs=[vmem()] * 7,
        out_specs=[vmem()] * 2,
        out_shape=[
            jax.ShapeDtypeStruct((4 * part, wide), F32),
            jax.ShapeDtypeStruct((4 * part, wide), BF16),
        ],
        scratch_shapes=[pltpu.VMEM((8 * part, wide), F32)],
        compiler_params=MIDDLE,
    )(reads, beside, mine, one, two, three, four)
    piece = jax.ShapeDtypeStruct((part, wide), BF16)
    kept, to_x, to_y, to_both = pl.pallas_call(
        add_kernel,
        name="add",
        in_specs=[vmem()] * 2,
        out_specs=[vmem()] * 4,
        out_shape=[piece] * 4,
        compiler_params=SMALL,
    )(keep, moved(send, flip(1)))
    return pl.pallas_call(
        lay_kernel,
        name="lay",
        in_specs=[vmem()] * 4,
        out_specs=vmem(),
        out_shape=jax.ShapeDtypeStruct((part, 4 * wide), BF16),
        compiler_params=SMALL,
    )(kept, moved(to_x, flip(2)), moved(to_y, flip(8)), moved(to_both, flip(10)))


def solution(mesh):
    fine = Mesh(mesh.devices.reshape(2, 2, 2, 2, 2, 8), SEQ + ("head",))
    in_specs = (
        P(SEQ, None),
        P(),
        P(None, None, "head"),
        P(None, None, "head"),
        P("head"),
        P("head"),
        P(SEQ),
        P("head"),
        P("head", None),
    )
    out_specs = P(SEQ + ("head",), None)
    return jax.shard_map(
        per_device, mesh=fine, in_specs=in_specs, out_specs=out_specs, check_vma=False
    )
```
